32 devices in a mesh: fsdp: 8 (over z, x), tensor: 4 (over y, core).
Axes of the slice: x: 2, y: 2, z: 4, core: 2. Of those that a mesh axis runs over, the one named last changes fastest.
Arguments:
- hidden_in: bfloat16 [4096, 2048], P(('fsdp', 'tensor')), may hold values from -6 to 6
- ln_gain: float32 [2048], replicated, may hold values from 0.5 to 1.5
- ln_bias: float32 [2048], replicated, may hold values from -1.75 to 1.75
- w_qkv: bfloat16 [2048, 3, 2048], P('fsdp', None, 'tensor'), may hold values from -0.125 to 0.125
- b_qkv: float32 [3, 2048], P(None, 'tensor'), may hold values from -1.75 to 1.75
- w_dense: bfloat16 [2048, 2048], P('tensor', 'fsdp'), may hold values from -0.5 to 0.5
- b_dense: float32 [2048], replicated, may hold values from -1.75 to 1.75
- w_fc1: bfloat16 [2048, 8192], P('fsdp', 'tensor'), may hold values from -0.125 to 0.125
- b_fc1: float32 [8192], P('tensor'), may hold values from -1.75 to 1.75
- w_fc2: bfloat16 [8192, 2048], P('tensor', 'fsdp'), may hold values from -0.0625 to 0.0625
- b_fc2: float32 [2048], replicated, may hold values from -1.75 to 1.75
- segment_ids: int32 [8, 512], P('fsdp'), may hold values from 0 to 7, never falling along the last dimension, each value on 1 to 256 neighbouring positions
- out_grad: bfloat16 [4096, 2048], P(('fsdp', 'tensor')), may hold values from -6 to 6
Outputs:
- hidden_out: bfloat16 [4096, 2048], P(('fsdp', 'tensor'))
- input_grad: float32 [4096, 2048], P(('fsdp', 'tensor'))
- ln_gain_grad: float32 [2048], replicated
- ln_bias_grad: float32 [2048], replicated
- w_qkv_grad: float32 [2048, 3, 2048], P('fsdp', None, 'tensor')
- b_qkv_grad: float32 [3, 2048], P(None, 'tensor')
- w_dense_grad: float32 [2048, 2048], P('tensor', 'fsdp')
- b_dense_grad: float32 [2048], replicated
- w_fc1_grad: float32 [2048, 8192], P('fsdp', 'tensor')
- b_fc1_grad: float32 [8192], P('tensor')
- w_fc2_grad: float32 [8192, 2048], P('tensor', 'fsdp')
- b_fc2_grad: float32 [2048], replicated
The draws below stay inside these ranges and needn't reach their ends.
Inputs may be any that keep to these rules, and one draw needn't show every extreme that they name: `segment_ids`: in each sequence the document numbers never fall; each document has 1 to 256 tokens and one has exactly 256.
All inputs are finite; a program needn't handle non-finite values.
Results may differ from the reference program's by a relative error of at most 0.0093.
Values may be sent and summed in bfloat16 or wider, within the bound.
No kernel may reach another device: no remote copies, remote signals or barrier semaphores. Data moves between devices by JAX's collectives and lax.ppermute only.
A program may use at most 192 MiB of HBM per device.

```python
import math
import jax
import jax.numpy as jnp
import numpy as np
from jax import lax

D = 2048
HEADS = 32
HEAD_DIM = 64
ROT = 32
FF = 8192
SEQ = 512
DOCS = 8
MOST = 256
TOKENS = 4096
N_FSDP = 8


def levels(rng, extent, split, low, largest):
    level, own = 1.0, jax.random.fold_in(rng, 6)
    for dim, parts in split:
        draws = jnp.exp(jax.random.uniform(jax.random.fold_in(own, dim), (parts,), jnp.float32, low / len(split), largest / len(split)))
        level = level * jnp.repeat(draws, extent[dim] // parts).reshape([-1 if axis == dim else 1 for axis in range(len(extent))])
    return level


def profile(amount, total, limit, lean):
    weights = [(1 << 20) // math.isqrt(standing ** lean) + 1 for standing in range(2, amount + 1)]
    surplus, holding = total - limit - (amount - 1), [1] * (amount - 1)
    while surplus > 0:
        movable = [i for i in range(amount - 1) if holding[i] < limit]
        whole, left = sum([weights[i] for i in movable]), surplus
        for i in movable:
            more = min(limit - holding[i], max(1, left * weights[i] // whole), surplus)
            holding[i] = holding[i] + more
            surplus = surplus - more
    return np.array([limit] + holding)


def ragged_sizes(rng, amount, total, reach, lean):
    if amount == 2:
        one = jax.random.randint(rng, (), max(1, total - reach), min(reach, total - 1) + 1)
        return jnp.stack([one, total - one])
    tallies = jnp.asarray(profile(amount, total, reach, lean), jnp.int32)
    twos = (amount - 1) // 2
    donor, taker = tallies[1:1 + 2 * twos:2], tallies[2:2 + 2 * twos:2]
    room = jnp.minimum(donor - 1, reach - taker)
    passed = jax.random.randint(jax.random.fold_in(rng, 1), (twos,), 0, 1 << 20) % (room + 1)
    tallies = tallies.at[1:1 + 2 * twos:2].set(donor - passed).at[2:2 + 2 * twos:2].set(taker + passed)
    return tallies[jax.random.permutation(jax.random.fold_in(rng, 2), amount)]


def noise(rng, dims, spread, limit, split=(), kind=jnp.bfloat16):
    entries = spread * jax.random.normal(rng, dims, jnp.float32)
    if split:
        entries = entries * levels(rng, dims, split, -0.22, 0.18)
    return jnp.clip(entries, -limit, limit).astype(kind)


def setup_inputs(seed: int = 0) -> dict:
    streams_of = jax.random.split(jax.random.key(seed), 14)
    hidden_in = noise(streams_of[0], (TOKENS, D), 1.0, 6.0, ((0, 32),))
    ln_gain = jnp.clip(1.0 + 0.1 * jax.random.normal(streams_of[1], (D,), jnp.float32), 0.5, 1.5)
    ln_bias = noise(streams_of[2], (D,), 0.3, 1.75, (), jnp.float32)
    w_qkv = noise(streams_of[3], (D, 3, D), D ** -0.5, 0.125, ((0, 8), (2, 4)))
    b_qkv = noise(streams_of[4], (3, D), 0.3, 1.75, ((1, 4),), jnp.float32)
    w_dense = noise(streams_of[5], (D, D), (D // 16) ** -0.5, 0.5, ((0, 4), (1, 8)))
    b_dense = noise(streams_of[6], (D,), 0.3, 1.75, (), jnp.float32)
    w_fc1 = noise(streams_of[7], (D, FF), D ** -0.5, 0.125, ((0, 8), (1, 4)))
    b_fc1 = noise(streams_of[8], (FF,), 0.3, 1.75, ((0, 4),), jnp.float32)
    w_fc2 = noise(streams_of[9], (FF, D), FF ** -0.5, 0.0625, ((0, 4), (1, 8)))
    b_fc2 = noise(streams_of[10], (D,), 0.3, 1.75, (), jnp.float32)
    segment_ids = jax.vmap(lambda own: jnp.searchsorted(jnp.cumsum(ragged_sizes(own, DOCS, SEQ, MOST, 2)), jnp.arange(SEQ), side="right"))(jax.random.split(streams_of[11], N_FSDP)).reshape((N_FSDP, SEQ)).astype(jnp.int32)
    out_grad = noise(streams_of[12], (TOKENS, D), 1.0, 6.0, ((0, 32),))
    return dict(hidden_in=hidden_in, ln_gain=ln_gain, ln_bias=ln_bias, w_qkv=w_qkv, b_qkv=b_qkv, w_dense=w_dense, b_dense=b_dense, w_fc1=w_fc1, b_fc1=b_fc1, w_fc2=w_fc2, b_fc2=b_fc2, segment_ids=segment_ids, out_grad=out_grad)


EPS = 1e-05
HIGH = lax.Precision.HIGHEST

@jax.custom_vjp
def low(v):
    return lax.optimization_barrier(v.astype(jnp.bfloat16)).astype(jnp.float32)

@jax.custom_vjp
def low_back(v):
    return v

def low_keep(v):
    return (low(v), None)

def low_pass(kept, grad):
    return (grad,)

def back_keep(v):
    return (v, None)

def back_low(kept, grad):
    return (low(grad),)
low.defvjp(low_keep, low_pass)
low_back.defvjp(back_keep, back_low)

def layer_norm(values, norm_gain, norm_shift):
    centred = values - lax.optimization_barrier(jnp.mean(values, axis=-1, keepdims=True))
    variance = lax.optimization_barrier(jnp.mean(centred * centred, axis=-1, keepdims=True))
    return centred * lax.rsqrt(variance + EPS) * norm_gain + norm_shift

def rotary_tables(length):
    positions = jnp.arange(length).astype(jnp.float32)
    inverse = 10000.0 ** (-jnp.arange(0, ROT, 2).astype(jnp.float32) / ROT)
    angles = positions[:, None] * inverse[None, :]
    return (jnp.cos(angles), jnp.sin(angles))

def rotate(values, cosine_rows, sine_rows):
    half_rot = ROT // 2
    first_half = values[..., :half_rot]
    second = values[..., half_rot:ROT]
    others = values[..., ROT:]
    cos_rows = cosine_rows[:, None, :]
    sin_rows = sine_rows[:, None, :]
    return jnp.concatenate([first_half * cos_rows - second * sin_rows, second * cos_rows + first_half * sin_rows, others], axis=-1)

def attention(queries, key_rows, value_rows, segments):
    block_rows = min(512, SEQ)
    block_count = SEQ // block_rows
    score_scale = 1.0 / math.sqrt(HEAD_DIM)
    col_pos = jnp.arange(SEQ, dtype=jnp.int32)

    def one_block(block_index):
        offset = (block_index * block_rows).astype(jnp.int32)
        query_rows = lax.dynamic_slice_in_dim(queries, offset, block_rows, 0)
        query_segs = lax.dynamic_slice_in_dim(segments, offset, block_rows, 0)
        scores = low_back(jnp.einsum('qhd,khd->hqk', query_rows, key_rows, precision=HIGH) * score_scale)
        row_pos = offset + jnp.arange(block_rows, dtype=jnp.int32)
        allowed = (col_pos[None, :] <= row_pos[:, None]) & (query_segs[:, None] == segments[None, :])
        scores = jnp.where(allowed[None], scores, -1e+30)
        attend = low(jax.nn.softmax(scores, axis=-1))
        return jnp.einsum('hqk,khd->qhd', attend, value_rows, precision=HIGH)
    blocks = lax.map(jax.checkpoint(one_block), jnp.arange(block_count, dtype=jnp.int32))
    return blocks.reshape(SEQ, HEADS, HEAD_DIM)

def layer_forward(params, hidden, segments, cosine_rows, sine_rows):
    norm_gain, norm_shift, qkv_weight, qkv_bias, dense_weight, dense_bias, up_weight, up_bias, down_weight, down_bias = params
    normed = low(layer_norm(hidden, norm_gain, norm_shift))
    mixed_proj = low_back(jnp.einsum('sd,djc->sjc', normed, qkv_weight, precision=HIGH) + qkv_bias)
    split_heads = mixed_proj.reshape(SEQ, 3, HEADS, HEAD_DIM)
    queries = low(rotate(split_heads[:, 0], cosine_rows, sine_rows))
    key_rows = low(rotate(split_heads[:, 1], cosine_rows, sine_rows))
    value_rows = low(split_heads[:, 2])
    context = attention(queries, key_rows, value_rows, segments)
    context = low(low_back(context)).reshape(SEQ, D)
    attn_out = jnp.dot(context, dense_weight, precision=HIGH)
    before = low_back(jnp.dot(normed, up_weight, precision=HIGH) + up_bias)
    activated = low(jax.nn.gelu(before, approximate=True))
    mlp_out = jnp.dot(activated, down_weight, precision=HIGH)
    return hidden + attn_out + mlp_out + dense_bias + down_bias

def reference(hidden_in, ln_gain, ln_bias, w_qkv, b_qkv, w_dense, b_dense, w_fc1, b_fc1, w_fc2, b_fc2, segment_ids, out_grad):
    params = (ln_gain.astype(jnp.float32), ln_bias.astype(jnp.float32), w_qkv.astype(jnp.float32), b_qkv.astype(jnp.float32), w_dense.astype(jnp.float32), b_dense.astype(jnp.float32), w_fc1.astype(jnp.float32), b_fc1.astype(jnp.float32), w_fc2.astype(jnp.float32), b_fc2.astype(jnp.float32))
    cosine_rows, sine_rows = rotary_tables(SEQ)
    hidden_seq = hidden_in.astype(jnp.float32).reshape(N_FSDP, SEQ, D)
    grad_seq = out_grad.astype(jnp.float32).reshape(N_FSDP, SEQ, D)

    def sequence_step(totals, seq_item):
        hidden, cotangent, segments = seq_item

        def forward(hidden_arg, param_arg):
            return layer_forward(param_arg, hidden_arg, segments, cosine_rows, sine_rows)
        result, pullback = jax.vjp(forward, hidden, params)
        hidden_grad, param_grads = pullback(cotangent)
        return (jax.tree.map(jnp.add, totals, param_grads), (result.astype(jnp.bfloat16), hidden_grad))
    zero_grads = jax.tree.map(jnp.zeros_like, params)
    sums, (results, hidden_grads) = lax.scan(sequence_step, zero_grads, (hidden_seq, grad_seq, segment_ids))
    return (results.reshape(TOKENS, D), hidden_grads.reshape(TOKENS, D), sums[0], sums[1], sums[2], sums[3], sums[4], sums[5], sums[6], sums[7], sums[8], sums[9])
```

```python
import math

import jax
import jax.numpy as jnp
from jax import lax
from jax.sharding import Mesh
from jax.sharding import PartitionSpec as P

HEAD_DIM = 64
ROT = 32
EPS = 1e-05

BF = jnp.bfloat16
F32 = jnp.float32


def layer_norm(values, norm_gain, norm_shift):
    centred = values - jnp.mean(values, axis=-1, keepdims=True)
    variance = jnp.mean(centred * centred, axis=-1, keepdims=True)
    return centred * lax.rsqrt(variance + EPS) * norm_gain + norm_shift


def gelu_tanh(values):
    return jax.nn.gelu(values, approximate=True)


def rotate(values, cosine, sine):
    half = ROT // 2
    first, second, others = values[..., :half], values[..., half:ROT], values[..., ROT:]
    return jnp.concatenate(
        [first * cosine - second * sine, second * cosine + first * sine, others], axis=-1
    )


def swap_with(values, axis, mask, size):
    return lax.ppermute(values, axis, [(i, i ^ mask) for i in range(size)])


def flip_pairs(values, axis, block):
    count = values.shape[axis] // block
    parts = [lax.slice_in_dim(values, i * block, (i + 1) * block, axis=axis) for i in range(count)]
    return jnp.concatenate([parts[i ^ 1] for i in range(count)], axis=axis)


def dot(left, right, dims):
    return lax.dot_general(left, right, (dims, ((), ())), preferred_element_type=F32)


def make_body(line):
    def body(
        hidden_in, ln_gain, ln_bias, w_qkv, b_qkv, w_dense, b_dense,
        w_fc1, b_fc1, w_fc2, b_fc2, segment_ids, out_grad,
    ):
        z, xb = lax.axis_index("z"), lax.axis_index("x")
        yb, cb = lax.axis_index("y"), lax.axis_index("core")
        tile, width = hidden_in.shape
        block = width // (2 * line)

        def half(values, which, axis):
            size = values.shape[axis] // 2
            return lax.dynamic_slice_in_dim(values, which * size, size, axis)

        def own_order(values, axis):
            return jnp.where(xb == 1, flip_pairs(values, axis, block), values)

        def swap_x(values):
            return swap_with(values, "x", 1, 2)

        def swap_y(values):
            return swap_with(values, "y", 1, 2)

        def swap_c(values):
            return swap_with(values, "core", 1, 2)

        def spread(keep, send, axis):
            both = jnp.concatenate([keep, swap_x(send)], axis=axis)
            return lax.all_gather(both, "z", axis=axis, tiled=True)

        def qkv_half(which):
            piece = half(w_qkv, which, 2)
            return jnp.concatenate([piece[:, j] for j in range(3)], axis=1)

        hidden = hidden_in.astype(F32)
        normed = layer_norm(hidden, ln_gain, ln_bias).astype(BF)

        up_w = spread(half(w_fc1, xb, 1), half(w_fc1, 1 - xb, 1), 0)
        qkv_w = spread(qkv_half(xb), qkv_half(1 - xb), 0)
        dense_w = spread(half(w_dense, xb, 0), half(w_dense, 1 - xb, 0), 1)
        down_w = spread(half(w_fc2, xb, 0), half(w_fc2, 1 - xb, 0), 1)

        def gather_tokens(values):
            mine = own_order(values, 1)
            other = swap_x(flip_pairs(mine, 1, block))
            rows = jnp.stack([mine, other])
            rows = jnp.concatenate([rows, swap_y(rows)], axis=1)
            rows = jnp.concatenate([rows, swap_c(rows)], axis=1)
            return rows.reshape(-1, width)

        def scatter_tokens(partial):
            rows = partial.reshape(2, 4 * tile, width)
            rows = rows[:, : 2 * tile].astype(F32) + swap_c(rows[:, 2 * tile :]).astype(F32)
            rows = rows.astype(BF)
            rows = rows[:, :tile].astype(F32) + swap_y(rows[:, tile:]).astype(F32)
            sent = flip_pairs(rows[1].astype(BF), 1, block)
            return own_order(rows[0] + swap_x(sent).astype(F32), 1)

        normed_all = gather_tokens(normed)
        grad_all = gather_tokens(out_grad)
        seq_len = 4 * tile

        def token_order(values):
            parts = [values[:, i * tile : (i + 1) * tile] for i in range(4)]
            order = [parts[0], parts[2], parts[1], parts[3]]
            order = [jnp.where(yb == 1, order[i ^ 1], order[i]) for i in range(4)]
            order = [jnp.where(cb == 1, order[i ^ 2], order[i]) for i in range(4)]
            return jnp.concatenate(order, axis=1)

        segments = jnp.concatenate([segment_ids, swap_x(segment_ids)], axis=0)
        segments = token_order(segments)
        positions = token_order(jnp.arange(seq_len, dtype=jnp.int32)[None, :])[0]
        inverse = 10000.0 ** (-jnp.arange(0, ROT, 2).astype(F32) / ROT)
        angles = jnp.arange(seq_len).astype(F32)[:, None] * inverse[None, :]
        cosine = token_order(jnp.cos(angles)[None])[0][None, :, None, :]
        sine = token_order(jnp.sin(angles)[None])[0][None, :, None, :]

        up_b = half(b_fc1, xb, 0)
        qkv_b = half(b_qkv, xb, 1).reshape(-1)
        before = dot(normed_all, up_w, ((1,), (0,))) + up_b
        activated = gelu_tanh(before).astype(BF)
        mixed = dot(normed_all, qkv_w, ((1,), (0,))) + qkv_b
        local = qkv_b.shape[0] // 3
        heads = local // HEAD_DIM

        def split(values):
            return values.reshape(2, seq_len, heads, HEAD_DIM)

        queries = rotate(split(mixed[:, :local]), cosine, sine).astype(BF)
        key_rows = rotate(split(mixed[:, local : 2 * local]), cosine, sine).astype(BF)
        value_rows = split(mixed[:, 2 * local :]).astype(BF)
        scale = 1.0 / math.sqrt(HEAD_DIM)
        allowed = (positions[None, None, :] <= positions[None, :, None]) & (
            segments[:, :, None] == segments[:, None, :]
        )

        def ein(spec, left, right):
            return jnp.einsum(spec, left, right, preferred_element_type=F32)

        scores = ein("sqhd,skhd->shqk", queries, key_rows) * scale
        scores = jnp.where(allowed[:, None], scores, -1e30)
        highest = jnp.max(scores, axis=-1, keepdims=True)
        shifted = jnp.exp(scores - highest)
        attend = shifted / jnp.sum(shifted, axis=-1, keepdims=True)
        attend_b = attend.astype(BF)
        context = ein("shqk,skhd->sqhd", attend_b, value_rows)
        context = context.reshape(2 * seq_len, local).astype(BF)

        branch = dot(context, dense_w, ((1,), (0,))) + dot(activated, down_w, ((1,), (0,)))
        branch = scatter_tokens(branch.astype(BF))
        hidden_out = (hidden + branch + b_dense + b_fc2).astype(BF)

        def collect(grad, axis):
            cur, count, bit = grad.astype(BF), line, 1
            while bit < line:
                own = (z // bit) % 2
                count //= 2

                def pick(which, cur=cur, count=count):
                    size = 2 * block
                    return jnp.concatenate(
                        [
                            lax.dynamic_slice_in_dim(cur, (2 * i + which) * size, size, axis)
                            for i in range(count)
                        ],
                        axis=axis,
                    )

                total = pick(own).astype(F32) + swap_with(pick(1 - own), "z", bit, line).astype(F32)
                bit *= 2
                cur = total.astype(BF) if bit < line else total
            keep = lax.slice_in_dim(cur, 0, block, axis=axis)
            back = swap_x(lax.slice_in_dim(cur, block, 2 * block, axis=axis).astype(BF))
            return keep.astype(F32), back.astype(F32)

        def join(keep, back, axis):
            return jnp.where(
                xb == 0,
                jnp.concatenate([keep, back], axis=axis),
                jnp.concatenate([back, keep], axis=axis),
            )

        down_grad = join(*collect(dot(activated, grad_all, ((0,), (0,))), 1), 0)
        dense_grad = join(*collect(dot(context, grad_all, ((0,), (0,))), 1), 0)

        context_grad = dot(grad_all, dense_w, ((1,), (1,))).astype(BF)
        activated_grad = dot(grad_all, down_w, ((1,), (1,)))
        before_grad = jax.vjp(gelu_tanh, before)[1](activated_grad)[0].astype(BF)
        up_grad = join(*collect(dot(normed_all, before_grad, ((0,), (0,))), 0), 1)

        context_heads = split(context_grad)
        attend_grad = ein("sqhd,skhd->shqk", context_heads, value_rows)
        inner = jnp.sum(attend * attend_grad, axis=-1, keepdims=True)
        score_grad = (attend * (attend_grad - inner)).astype(BF)
        query_grad = ein("shqk,skhd->sqhd", score_grad, key_rows) * scale
        key_grad = ein("shqk,sqhd->skhd", score_grad, queries) * scale
        value_grad = ein("shqk,sqhd->skhd", attend_b, context_heads)
        mixed_grad = jnp.concatenate(
            [
                part.reshape(2 * seq_len, local).astype(BF)
                for part in (
                    rotate(query_grad, cosine, -sine),
                    rotate(key_grad, cosine, -sine),
                    value_grad,
                )
            ],
            axis=1,
        )
        keep, back = collect(dot(normed_all, mixed_grad, ((0,), (0,))), 0)
        qkv_grad = join(
            jnp.stack([keep[:, j * local : (j + 1) * local] for j in range(3)], axis=1),
            jnp.stack([back[:, j * local : (j + 1) * local] for j in range(3)], axis=1),
            2,
        )
        normed_part = dot(mixed_grad, qkv_w, ((1,), (1,))) + dot(before_grad, up_w, ((1,), (1,)))
        normed_grad = scatter_tokens(normed_part.astype(BF))
        hidden_grad, gain_local, shift_local = jax.vjp(layer_norm, hidden, ln_gain, ln_bias)[1](
            normed_grad
        )
        cotangent = out_grad.astype(F32)
        input_grad = cotangent + hidden_grad

        def over_line(values):
            bit = 1
            while bit < line:
                values = values + swap_with(values, "z", bit, line)
                bit *= 2
            return values

        bias = over_line(
            jnp.concatenate(
                [
                    jnp.sum(mixed_grad, axis=0, dtype=F32),
                    jnp.sum(before_grad, axis=0, dtype=F32),
                ]
            )
        )
        bias_back = swap_x(bias)
        qkv_bias_grad = join(
            bias[: 3 * local].reshape(3, local), bias_back[: 3 * local].reshape(3, local), 1
        )
        up_bias_grad = join(bias[3 * local :], bias_back[3 * local :], 0)
        total = jnp.concatenate([gain_local, shift_local, jnp.sum(cotangent, axis=0)])
        total = over_line(total)
        for swap in (swap_x, swap_y, swap_c):
            total = total + swap(total)
        gain_grad, shift_grad, out_bias_grad = (
            total[:width], total[width : 2 * width], total[2 * width :]
        )
        return (
            hidden_out, input_grad, gain_grad, shift_grad, qkv_grad, qkv_bias_grad,
            dense_grad, out_bias_grad, up_grad, up_bias_grad, down_grad, out_bias_grad,
        )

    return body


def solution(mesh):
    line = mesh.shape["fsdp"] // 2
    grid = Mesh(mesh.devices.reshape(line, 2, 2, 2), ("z", "x", "y", "core"))
    rows, cols = ("z", "x"), ("y", "core")
    tokens = rows + cols
    in_specs = (
        P(tokens, None), P(), P(), P(rows, None, cols), P(None, cols), P(cols, rows), P(),
        P(rows, cols), P(cols), P(cols, rows), P(), P(rows, None), P(tokens, None),
    )
    out_specs = (
        P(tokens, None), P(tokens, None), P(), P(), P(rows, None, cols), P(None, cols),
        P(cols, rows), P(), P(rows, cols), P(cols), P(cols, rows), P(),
    )
    return jax.shard_map(
        make_body(line), mesh=grid, in_specs=in_specs, out_specs=out_specs, check_vma=False
    )
```

```python
import math

import jax
import jax.numpy as jnp
from jax import lax
from jax.experimental import pallas as pl
from jax.experimental.pallas import tpu as pltpu
from jax.sharding import Mesh
from jax.sharding import PartitionSpec as P

HEAD_DIM = 64
ROT = 32
EPS = 1e-05
BLOCK = 128
REACH = 256
SCALE = 1.0 / math.sqrt(HEAD_DIM)

BF = jnp.bfloat16
F32 = jnp.float32


def layer_norm(values, norm_gain, norm_shift):
    centred = values - jnp.mean(values, axis=-1, keepdims=True)
    variance = jnp.mean(centred * centred, axis=-1, keepdims=True)
    return centred * lax.rsqrt(variance + EPS) * norm_gain + norm_shift


def gelu_tanh(values):
    return jax.nn.gelu(values, approximate=True)


def rotary_tables(length, lanes):
    lane = jnp.arange(lanes) % HEAD_DIM
    pair = lane % (ROT // 2)
    angles = jnp.arange(length).astype(F32)[:, None] * (
        10000.0 ** (-(2.0 * pair.astype(F32)) / ROT)
    )
    cosine = jnp.where(lane < ROT, jnp.cos(angles), 1.0)
    sine = jnp.sin(angles)
    first = jnp.where(lane < ROT // 2, -sine, 0.0)
    second = jnp.where((lane >= ROT // 2) & (lane < ROT), sine, 0.0)
    return cosine, first, second


def turn(values, cosine, first, second):
    half, lanes = ROT // 2, values.shape[1]
    return (
        values * cosine
        + pltpu.roll(values, lanes - half, 1) * first
        + pltpu.roll(values, half, 1) * second
    )


def nt(left, right):
    return lax.dot_general(left, right, (((1,), (1,)), ((), ())), preferred_element_type=F32)


def tn(left, right):
    return lax.dot_general(left, right, (((0,), (0,)), ((), ())), preferred_element_type=F32)


def windows(length):
    for start in range(0, length, BLOCK):
        low = max(0, (start - REACH + 1) // BLOCK * BLOCK)
        yield start, low, start + BLOCK


def allowed_mask(row_ref, col_ref, start, low, high):
    size = high - low
    key = low + lax.broadcasted_iota(jnp.int32, (size, BLOCK), 0)
    query = start + lax.broadcasted_iota(jnp.int32, (size, BLOCK), 1)
    same = col_ref[low:high, :] == row_ref[0, :, start : start + BLOCK]
    return same & (key <= query)


def head_lanes(rows, head, lanes):
    lane = lax.broadcasted_iota(jnp.int32, (rows, lanes), 1)
    return lane // HEAD_DIM == head


def attend_kernel(mixed_ref, cos_ref, a_ref, b_ref, row_ref, col_ref, qkv_ref, out_ref, lse_ref):
    length, lanes = out_ref.shape
    tables = cos_ref[...], a_ref[...], b_ref[...]
    query = turn(mixed_ref[:, :lanes], *tables).astype(BF)
    query = (query.astype(F32) * SCALE).astype(BF)
    key = turn(mixed_ref[:, lanes : 2 * lanes], *tables).astype(BF)
    value = mixed_ref[:, 2 * lanes :].astype(BF)
    qkv_ref[:, :lanes] = query
    qkv_ref[:, lanes : 2 * lanes] = key
    qkv_ref[:, 2 * lanes :] = value
    for start, low, high in windows(length):
        mask = allowed_mask(row_ref, col_ref, start, low, high)
        mine = query[start:high]
        out = jnp.zeros((BLOCK, lanes), F32)
        for head in range(lanes // HEAD_DIM):
            own = head_lanes(BLOCK, head, lanes)
            scores = nt(key[low:high], jnp.where(own, mine, jnp.zeros_like(mine)))
            scores = jnp.where(mask, scores, -1e30)
            highest = jnp.max(scores, axis=0, keepdims=True)
            shifted = jnp.exp(scores - highest)
            total = jnp.sum(shifted, axis=0, keepdims=True)
            attend = (shifted / total).astype(BF)
            out = jnp.where(own, tn(attend, value[low:high]), out)
            lse_ref[0, head : head + 1, start:high] = highest + jnp.log(total)
        out_ref[start:high, :] = out.astype(BF)


def attend_grad_kernel(
    qkv_ref, grad_ref, lse_ref, cos_ref, a_ref, b_ref, row_ref, col_ref, out_ref, key_ref, value_ref
):
    length, lanes = grad_ref.shape
    key_ref[...] = jnp.zeros_like(key_ref)
    value_ref[...] = jnp.zeros_like(value_ref)
    for start, low, high in windows(length):
        mask = allowed_mask(row_ref, col_ref, start, low, high)
        query = qkv_ref[start:high, :lanes]
        key = qkv_ref[low:high, lanes : 2 * lanes]
        value = qkv_ref[low:high, 2 * lanes :]
        grad = grad_ref[start:high, :]
        query_grad = jnp.zeros((BLOCK, lanes), F32)
        key_grad = jnp.zeros((high - low, lanes), F32)
        value_grad = jnp.zeros((high - low, lanes), F32)
        for head in range(lanes // HEAD_DIM):
            own = head_lanes(BLOCK, head, lanes)
            own_keys = head_lanes(high - low, head, lanes)
            none = jnp.zeros_like(query)
            scores = nt(key, jnp.where(own, query, none))
            scores = jnp.where(mask, scores, -1e30)
            attend = jnp.exp(scores - lse_ref[0, head : head + 1, start:high])
            attend_grad = nt(value, jnp.where(own, grad, none))
            inner = jnp.sum(attend * attend_grad, axis=0, keepdims=True)
            score_grad = (attend * (attend_grad - inner)).astype(BF)
            query_grad = jnp.where(own, tn(score_grad, key), query_grad)
            key_grad = jnp.where(
                own_keys, jnp.dot(score_grad, query, preferred_element_type=F32), key_grad
            )
            value_grad = jnp.where(
                own_keys,
                jnp.dot(attend.astype(BF), grad, preferred_element_type=F32),
                value_grad,
            )
        back = [ref[start:high, :] for ref in (cos_ref, a_ref, b_ref)]
        query_grad = turn(query_grad * SCALE, back[0], -back[1], -back[2])
        out_ref[start:high, :lanes] = query_grad.astype(BF)
        key_ref[low:high, :] += key_grad
        value_ref[low:high, :] += value_grad
    key_grad = turn(key_ref[...], cos_ref[...], -a_ref[...], -b_ref[...])
    out_ref[:, lanes : 2 * lanes] = key_grad.astype(BF)
    out_ref[:, 2 * lanes :] = value_ref[...].astype(BF)


def attention_specs(length, lanes):
    table = pl.BlockSpec((length, lanes), lambda s: (0, 0))
    return dict(
        table=table,
        wide=pl.BlockSpec((length, 3 * lanes), lambda s: (s, 0)),
        slim=pl.BlockSpec((length, lanes), lambda s: (s, 0)),
        lse=pl.BlockSpec((1, lanes // HEAD_DIM, length), lambda s: (s, 0, 0)),
        row=pl.BlockSpec((1, 1, length), lambda s: (s, 0, 0)),
        col=pl.BlockSpec((length, 1), lambda s: (s, 0)),
    )


def attention(mixed, tables, segments):
    sequences, length = segments.shape
    lanes = mixed.shape[1] // 3
    spec = attention_specs(length, lanes)
    rows = sequences * length
    return pl.pallas_call(
        attend_kernel,
        grid=(sequences,),
        in_specs=[spec["wide"]] + [spec["table"]] * 3 + [spec["row"], spec["col"]],
        out_specs=[spec["wide"], spec["slim"], spec["lse"]],
        out_shape=[
            jax.ShapeDtypeStruct((rows, 3 * lanes), BF),
            jax.ShapeDtypeStruct((rows, lanes), BF),
            jax.ShapeDtypeStruct((sequences, lanes // HEAD_DIM, length), F32),
        ],
        compiler_params=pltpu.CompilerParams(vmem_limit_bytes=32 << 20),
        name="attend",
    )(mixed, *tables, segments[:, None, :], segments.reshape(-1, 1))


def attention_grad(qkv, grad, lse, tables, segments):
    sequences, length = segments.shape
    rows, lanes = grad.shape
    spec = attention_specs(length, lanes)
    return pl.pallas_call(
        attend_grad_kernel,
        grid=(sequences,),
        in_specs=[spec["wide"], spec["slim"], spec["lse"]]
        + [spec["table"]] * 3
        + [spec["row"], spec["col"]],
        out_specs=spec["wide"],
        out_shape=jax.ShapeDtypeStruct((rows, 3 * lanes), BF),
        scratch_shapes=[pltpu.VMEM((length, lanes), F32)] * 2,
        compiler_params=pltpu.CompilerParams(vmem_limit_bytes=32 << 20),
        name="attend_grad",
    )(qkv, grad, lse, *tables, segments[:, None, :], segments.reshape(-1, 1))


def place(order, sources, count, axis, shape):
    arrays = []
    for array, _, _, _ in sources:
        if not any(array is seen for seen in arrays):
            arrays.append(array)
    where = [[array is seen for seen in arrays].index(True) for array, _, _, _ in sources]
    size = shape[axis] // count

    def kernel(order_ref, *refs):
        ins, out = refs[: len(arrays)], refs[-1]
        for i, (_, (rows, cols), slot, entry) in enumerate(sources):
            to = pl.multiple_of((slot * 4 + order_ref[entry]) * size, size)
            if axis == 0:
                out[pl.ds(to, size), :] = ins[where[i]][rows : rows + size, cols : cols + shape[1]]
            else:
                out[:, pl.ds(to, size)] = ins[where[i]][rows : rows + shape[0], cols : cols + size]

    if axis == 1 and size % 128:
        result = jnp.zeros(shape, arrays[0].dtype)
        for array, (rows, cols), slot, entry in sources:
            piece = lax.slice(array, (rows, cols), (rows + shape[0], cols + size))
            to = (slot * 4 + order[entry]) * size
            result = lax.dynamic_update_slice_in_dim(result, piece, to, 1)
        return result

    whole = pl.BlockSpec(memory_space=pltpu.VMEM)
    return pl.pallas_call(
        kernel,
        in_specs=[pl.BlockSpec(memory_space=pltpu.SMEM)] + [whole] * len(arrays),
        out_specs=whole,
        out_shape=jax.ShapeDtypeStruct(shape, arrays[0].dtype),
        compiler_params=pltpu.CompilerParams(vmem_limit_bytes=24 << 20),
        name="place",
    )(order, *arrays)


def swap_with(values, axis, mask, size):
    return lax.ppermute(values, axis, [(i, i ^ mask) for i in range(size)])


def dot(left, right, dims):
    return lax.dot_general(left, right, (dims, ((), ())), preferred_element_type=F32)


def after(values, *earlier):
    return lax.optimization_barrier((values,) + earlier)[0]


def step(*values):
    return lax.optimization_barrier(values)


TEAM = ("l", "x", "y", "core")


def make_body(groups):
    def body(
        hidden_in, ln_gain, ln_bias, w_qkv, b_qkv, w_dense, b_dense,
        w_fc1, b_fc1, w_fc2, b_fc2, segment_ids, out_grad,
    ):
        group, lb, xb = lax.axis_index("h"), lax.axis_index("l"), lax.axis_index("x")
        quad = 2 * lb + xb
        tile, width = hidden_in.shape
        span = width // groups

        def part(values, which, count, axis):
            size = values.shape[axis] // count
            return lax.dynamic_slice_in_dim(values, which * size, size, axis)

        def fixed(values, which, count, axis):
            size = values.shape[axis] // count
            return lax.slice_in_dim(values, which * size, (which + 1) * size, axis=axis)

        def own_order(values, axis):
            bit = 1
            while bit < groups:
                blocks = [fixed(values, j ^ bit, groups, axis) for j in range(groups)]
                flipped = jnp.concatenate(blocks, axis=axis)
                values = jnp.where((group // bit) % 2 == 1, flipped, values)
                bit *= 2
            return values

        def trade(give, own):
            return [own] + [swap_with(give(quad ^ m), ("l", "x"), m, 4) for m in (1, 2, 3)]

        def in_order(parts, axis):
            blocks = [
                jnp.where(
                    lb == 1,
                    jnp.where(xb == 1, parts[j ^ 3], parts[j ^ 2]),
                    jnp.where(xb == 1, parts[j ^ 1], parts[j]),
                )
                for j in range(4)
            ]
            return jnp.concatenate(blocks, axis=axis)

        def swap_h(values):
            return [swap_with(values, "h", k, groups) for k in range(1, groups)]

        def fold_start(rows, axis, name):
            sent = lax.dynamic_index_in_dim(rows, 1 - lax.axis_index(name), axis, keepdims=False)
            return swap_with(sent, name, 1, 2)

        def fold_end(rows, got, axis, name):
            mine = lax.dynamic_index_in_dim(rows, lax.axis_index(name), axis, keepdims=False)
            return mine.astype(F32) + got.astype(F32)

        def halves(rows):
            return rows[..., : width // 2], rows[..., width // 2 :]

        def swap_c(values):
            return swap_with(values, "core", 1, 2)

        def quad_swap(values, m):
            return swap_with(values, ("l", "x"), m, 4)

        seg_len = segment_ids.shape[1]
        in_cols = 3 * w_qkv.shape[2] // 4 + w_fc1.shape[1] // 4
        labels = jnp.pad(segment_ids.astype(BF), ((0, 15), (0, in_cols - seg_len)))

        def take_in(which):
            piece = part(w_qkv, which, 4, 2)
            rows = jnp.concatenate(
                [piece[:, j] for j in range(3)] + [part(w_fc1, which, 4, 1)], axis=1
            )
            return jnp.concatenate([rows, labels], axis=0)

        def take_out(which):
            return jnp.concatenate([part(w_dense, which, 4, 0), part(w_fc2, which, 4, 0)], axis=0)

        def stacked(parts, axis):
            return jnp.concatenate(parts, axis=axis)

        def unstack(values, count, axis):
            return [fixed(values, m, count, axis) for m in range(count)]

        local = w_dense.shape[0] // 4
        qkv_cols = 3 * local

        order = jnp.stack([quad, quad ^ 1, quad ^ 2, quad ^ 3])
        rows_in, cols_out = w_fc1.shape[0], w_fc2.shape[1]

        hidden = hidden_in.astype(F32)
        mine_n = own_order(layer_norm(hidden, ln_gain, ln_bias).astype(BF), 1)
        mine_g = own_order(out_grad, 1)
        in_own = take_in(quad)
        in_first = swap_h(in_own[:rows_in])
        in_1 = quad_swap(take_in(quad ^ 1), 1)
        next_n = swap_with(mine_n, "l", 1, 2)
        in_first, in_1, next_n, in_own = step(in_first, in_1, next_n, in_own)

        def gather_tokens(mine, other):
            rows = lax.all_gather(
                jnp.stack([mine, other]), ("x", "y", "core"), axis=1, tiled=True
            )
            return rows.reshape(-1, width)

        normed_all = gather_tokens(mine_n, next_n)
        in_2, in_3 = (quad_swap(take_in(quad ^ m), m) for m in (2, 3))
        out_own = take_out(quad)
        out_first = swap_h(out_own)
        in_2, in_3, out_first, out_own = step(in_2, in_3, out_first, out_own)
        in_parts = [in_own, in_1, in_2, in_3]

        qkv_rest = swap_h(stacked([p[:rows_in, :qkv_cols] for p in in_parts[1:]], 0))
        out_parts = [out_own] + [quad_swap(take_out(quad ^ m), m) for m in (1, 2, 3)]
        next_g = swap_with(mine_g, "l", 1, 2)
        up_send = stacked([p[:rows_in, qkv_cols:] for p in in_parts[1:]], 0)
        qkv_rest, out_parts, next_g, up_send = step(qkv_rest, out_parts, next_g, up_send)

        def place_in(first_col, cols, rest):
            sources = [(p, (0, first_col), 0, m) for m, p in enumerate(in_parts)]
            for k in range(1, groups):
                sources.append((in_first[k - 1], (0, first_col), k, 0))
                sources += [(rest[k - 1], ((m - 1) * rows_in, 0), k, m) for m in (1, 2, 3)]
            return place(order, sources, 4 * groups, 0, (width, cols))

        def place_out(first_row, rows, rest):
            sources = [(p, (first_row, 0), 0, m) for m, p in enumerate(out_parts)]
            for k in range(1, groups):
                sources.append((out_first[k - 1], (first_row, 0), k, 0))
                sources += [(rest[k - 1], (0, (m - 1) * cols_out), k, m) for m in (1, 2, 3)]
            return place(order, sources, 4 * groups, 1, (rows, width))

        up_rest = swap_h(up_send)
        dense_rest = swap_h(stacked([p[:local] for p in out_parts[1:]], 1))
        qkv_w = place_in(0, qkv_cols, qkv_rest)
        labels_all = [p[rows_in, :seg_len].astype(jnp.int32)[None] for p in in_parts]
        ordered = in_order(labels_all, 0)
        segments = jnp.where(lb == 1, jnp.roll(ordered, 2, axis=0), ordered)
        grad_all = gather_tokens(after(mine_g, normed_all, qkv_w), next_g)
        up_b = part(b_fc1, quad, 4, 0)
        qkv_b = part(b_qkv, quad, 4, 1).reshape(-1)
        mixed = dot(normed_all, qkv_w, ((1,), (0,))) + qkv_b
        tables = rotary_tables(segments.shape[1], local)
        qkv, context, lse = attention(mixed, tables, segments)
        down_send = stacked([p[local:] for p in out_parts[1:]], 1)
        qkv, context, lse, up_rest, dense_rest, down_send = step(
            qkv, context, lse, up_rest, dense_rest, down_send
        )

        def slot(values, k, axis):
            return fixed(values, k, groups, axis)

        down_rest = swap_h(down_send)
        up_w = place_in(qkv_cols, in_cols - qkv_cols, up_rest)
        dense_w = place_out(0, local, dense_rest)
        before = dot(after(normed_all, context), up_w, ((1,), (0,))) + up_b
        activated = gelu_tanh(before).astype(BF)
        acts = stacked([context, activated], 1)
        out_part = dot(acts, grad_all, ((0,), (0,))).astype(BF)
        cuts = [0, out_part.shape[0] * 2 // 5, out_part.shape[0] * 7 // 10, out_part.shape[0]]

        def out_slot(k, i):
            return slot(out_part, k, 1)[cuts[i] : cuts[i + 1]]

        out_send = [[out_slot(k, i) for i in range(3)] for k in range(groups)]
        context_grad = dot(after(grad_all, out_part), dense_w, ((1,), (1,))).astype(BF)
        mixed_grad = attention_grad(qkv, context_grad, lse, tables, segments)
        mixed_grad, down_rest, out_send, before, acts = step(
            mixed_grad, down_rest, out_send, before, acts
        )

        def send_out(i):
            return [swap_with(out_send[k][i], "h", k, groups) for k in range(1, groups)]

        out_a = send_out(0)
        down_w = place_out(local, w_fc2.shape[0] // 4, down_rest)
        branch = dot(acts, stacked([dense_w, down_w], 0), ((1,), (0,)))
        branch = lax.psum_scatter(
            branch.astype(BF).reshape(2, -1, width),
            ("x", "y", "core"),
            scatter_dimension=1,
            tiled=True,
        )
        activated_grad = dot(after(grad_all, mixed_grad), down_w, ((1,), (1,)))
        before_grad = jax.vjp(gelu_tanh, before)[1](activated_grad)[0].astype(BF)
        into = stacked([mixed_grad, before_grad], 1)
        into, out_a = step(into, out_a)
        out_b = send_out(1)
        terms = dot(into, stacked([qkv_w, up_w], 1), ((1,), (1,)))
        unit = (normed_all.astype(F32) - own_order(ln_bias, 0)) / own_order(ln_gain, 0)
        small = [
            own_order(jnp.sum(terms * unit, axis=0), 0),
            own_order(jnp.sum(terms, axis=0), 0),
            jnp.sum(out_grad.astype(F32), axis=0),
        ]
        shape5 = (2, 2, 2, 2, tile, width)
        terms = terms.astype(BF).reshape(shape5)
        team = 4 * (2 * lax.axis_index("y") + lax.axis_index("core"))
        bias = jnp.sum(into, axis=0, dtype=F32)
        size = into.shape[1]
        bias = lax.dynamic_update_slice(jnp.zeros((16 * size,), F32), bias, ((team + quad) * size,))
        total = stacked(small + [bias], 0)
        sent_c = lax.dynamic_index_in_dim(terms, 1 - lax.axis_index("core"), 3, keepdims=False)
        terms, total, into, sent_c, out_b = step(terms, total, into, sent_c, out_b)
        out_c = send_out(2)
        in_part = dot(normed_all, into, ((0,), (0,))).astype(BF)

        def block(k, m):
            start = k * span + (quad ^ m) * (span // 4)
            return lax.dynamic_slice_in_dim(in_part, start, span // 4, 0)

        def add_up(mine, others):
            mine = mine.astype(F32)
            for piece in others:
                mine = mine + piece.astype(F32)
            return mine

        in_send = [[block(k, m) for m in range(4)] for k in range(groups)]
        in_send, out_c = step(in_send, out_c)

        def send_in(m):
            return [swap_with(in_send[k][m], "h", k, groups) for k in range(1, groups)]

        in_a = send_in(1)
        got_c = swap_c(sent_c)
        out_sum = [
            add_up(out_send[0][i], got) for i, got in enumerate((out_a, out_b, out_c))
        ]
        out_sum = stacked(out_sum, 0)
        sent = out_sum.astype(BF)
        out_back = [quad_swap(part(sent, quad ^ m, 4, 1), m) for m in (1, 2, 3)]
        in_a, got_c, out_back = step(in_a, got_c, out_back)

        in_b = send_in(2)
        rows = fold_end(terms, got_c, 3, "core").astype(BF)
        left, right = halves(rows)
        got_l, got_r = fold_start(left, 2, "y"), fold_start(right, 1, "x")
        total = total + swap_c(total)
        out_pieces = [part(out_sum, quad, 4, 1)] + [p.astype(F32) for p in out_back]
        dense_grad = in_order([p[:local] for p in out_pieces], 0)
        down_grad = in_order([p[local:] for p in out_pieces], 0)
        back_1 = add_up(in_send[0][1], in_a).astype(BF)
        in_b, left, right, got_l, got_r, total, back_1, dense_grad, down_grad = step(
            in_b, left, right, got_l, got_r, total, back_1, dense_grad, down_grad
        )

        in_c = send_in(3)
        back_1 = quad_swap(back_1, 1)
        left = fold_end(left, got_l, 2, "y").astype(BF)
        right = fold_end(right, got_r, 1, "x").astype(BF)
        got_l, got_r = fold_start(left, 1, "x"), fold_start(right, 1, "y")
        total = total + swap_with(total, "y", 1, 2)
        back_2 = add_up(in_send[0][2], in_b).astype(BF)
        in_c, left, right, got_l, got_r, total, back_1, back_2 = step(
            in_c, left, right, got_l, got_r, total, back_1, back_2
        )

        in_d = send_in(0)
        back_2 = quad_swap(back_2, 2)
        rows = stacked(
            [fold_end(left, got_l, 1, "x").astype(BF), fold_end(right, got_r, 1, "y").astype(BF)],
            -1,
        )
        got_n = swap_with(rows[1], "l", 1, 2)
        total = total + swap_with(total, "x", 1, 2)
        back_3 = add_up(in_send[0][3], in_c).astype(BF)
        in_d, back_2, back_3, got_n, total = step(in_d, back_2, back_3, got_n, total)

        back_3 = quad_swap(back_3, 3)
        total = total + swap_with(total, "l", 1, 2)
        got_m = swap_with(branch[1], "l", 1, 2)
        normed_grad = own_order(rows[0].astype(F32) + got_n.astype(F32), 1)
        hidden_grad = jax.vjp(lambda v: layer_norm(v, ln_gain, ln_bias), hidden)[1](normed_grad)[0]
        input_grad = out_grad.astype(F32) + hidden_grad
        bit = 1
        while bit < groups:
            total = total + swap_with(total, "h", bit, groups)
            bit *= 2
        branch = own_order(branch[0].astype(F32) + got_m.astype(F32), 1)
        hidden_out = (hidden + branch + b_dense + b_fc2).astype(BF)
        pieces = [add_up(in_send[0][0], in_d)] + [p.astype(F32) for p in (back_1, back_2, back_3)]
        up_grad = in_order([p[:, qkv_cols:] for p in pieces], 1)
        qkv_grad = jnp.stack(
            [in_order([p[:, j * local : (j + 1) * local] for p in pieces], 1) for j in range(3)],
            axis=1,
        )
        gain_grad, shift_grad, out_bias_grad = (
            total[:width], total[width : 2 * width], total[2 * width : 3 * width]
        )
        bias = lax.dynamic_slice(total, (3 * width + team * size,), (4 * size,)).reshape(4, size)
        up_bias_grad = bias[:, qkv_cols:].reshape(-1)
        qkv_bias_grad = jnp.stack(
            [bias[:, j * local : (j + 1) * local].reshape(-1) for j in range(3)]
        )
        return (
            hidden_out, input_grad, gain_grad, shift_grad, qkv_grad, qkv_bias_grad,
            dense_grad, out_bias_grad, up_grad, up_bias_grad, down_grad, out_bias_grad,
        )

    return body


def solution(mesh):
    groups = mesh.shape["fsdp"] // 4
    grid = Mesh(mesh.devices.reshape(groups, 2, 2, 2, 2), ("h", "l", "x", "y", "core"))
    rows, cols = ("h", "l", "x"), ("y", "core")
    tokens = rows + cols
    in_specs = (
        P(tokens, None), P(), P(), P(rows, None, cols), P(None, cols), P(cols, rows), P(),
        P(rows, cols), P(cols), P(cols, rows), P(), P(rows, None), P(tokens, None),
    )
    out_specs = (
        P(tokens, None), P(tokens, None), P(), P(), P(rows, None, cols), P(None, cols),
        P(cols, rows), P(), P(rows, cols), P(cols), P(cols, rows), P(),
    )
    return jax.shard_map(
        make_body(groups), mesh=grid, in_specs=in_specs, out_specs=out_specs, check_vma=False
    )
```

```python
import math

import jax
import jax.numpy as jnp
from jax import lax
from jax.experimental import pallas as pl
from jax.experimental.pallas import tpu as pltpu
from jax.sharding import Mesh
from jax.sharding import PartitionSpec as P

HEAD_DIM = 64
ROT = 32
EPS = 1e-05
BLOCK = 128
REACH = 256
SCALE = 1.0 / math.sqrt(HEAD_DIM)

BF = jnp.bfloat16
F32 = jnp.float32


def layer_norm(values, norm_gain, norm_shift):
    centred = values - jnp.mean(values, axis=-1, keepdims=True)
    variance = jnp.mean(centred * centred, axis=-1, keepdims=True)
    return centred * lax.rsqrt(variance + EPS) * norm_gain + norm_shift


def gelu_tanh(values):
    return jax.nn.gelu(values, approximate=True)


def rotary_tables(length, lanes):
    lane = jnp.arange(lanes) % HEAD_DIM
    pair = lane % (ROT // 2)
    angles = jnp.arange(length).astype(F32)[:, None] * (
        10000.0 ** (-(2.0 * pair.astype(F32)) / ROT)
    )
    cosine = jnp.where(lane < ROT, jnp.cos(angles), 1.0)
    sine = jnp.sin(angles)
    first = jnp.where(lane < ROT // 2, -sine, 0.0)
    second = jnp.where((lane >= ROT // 2) & (lane < ROT), sine, 0.0)
    return cosine, first, second


def turn(values, cosine, first, second):
    half, lanes = ROT // 2, values.shape[1]
    return (
        values * cosine
        + pltpu.roll(values, lanes - half, 1) * first
        + pltpu.roll(values, half, 1) * second
    )


def nt(left, right):
    return lax.dot_general(left, right, (((1,), (1,)), ((), ())), preferred_element_type=F32)


def tn(left, right):
    return lax.dot_general(left, right, (((0,), (0,)), ((), ())), preferred_element_type=F32)


def windows(length):
    for start in range(0, length, BLOCK):
        low = max(0, (start - REACH + 1) // BLOCK * BLOCK)
        yield start, low, start + BLOCK


def allowed_mask(row_ref, col_ref, start, low, high):
    size = high - low
    key = low + lax.broadcasted_iota(jnp.int32, (size, BLOCK), 0)
    query = start + lax.broadcasted_iota(jnp.int32, (size, BLOCK), 1)
    same = col_ref[low:high, :] == row_ref[0, :, start : start + BLOCK]
    return same & (key <= query)


def head_lanes(rows, head, lanes):
    lane = lax.broadcasted_iota(jnp.int32, (rows, lanes), 1)
    return lane // HEAD_DIM == head


def attend_kernel(mixed_ref, cos_ref, a_ref, b_ref, row_ref, col_ref, qkv_ref, out_ref, lse_ref):
    length, lanes = out_ref.shape
    tables = cos_ref[...], a_ref[...], b_ref[...]
    query = turn(mixed_ref[:, :lanes], *tables).astype(BF)
    query = (query.astype(F32) * SCALE).astype(BF)
    key = turn(mixed_ref[:, lanes : 2 * lanes], *tables).astype(BF)
    value = mixed_ref[:, 2 * lanes :].astype(BF)
    qkv_ref[:, :lanes] = query
    qkv_ref[:, lanes : 2 * lanes] = key
    qkv_ref[:, 2 * lanes :] = value
    for start, low, high in windows(length):
        mask = allowed_mask(row_ref, col_ref, start, low, high)
        mine = query[start:high]
        out = jnp.zeros((BLOCK, lanes), F32)
        for head in range(lanes // HEAD_DIM):
            own = head_lanes(BLOCK, head, lanes)
            scores = nt(key[low:high], jnp.where(own, mine, jnp.zeros_like(mine)))
            scores = jnp.where(mask, scores, -1e30)
            highest = jnp.max(scores, axis=0, keepdims=True)
            shifted = jnp.exp(scores - highest)
            total = jnp.sum(shifted, axis=0, keepdims=True)
            attend = (shifted / total).astype(BF)
            out = jnp.where(own, tn(attend, value[low:high]), out)
            lse_ref[0, head : head + 1, start:high] = highest + jnp.log(total)
        out_ref[start:high, :] = out.astype(BF)


def attend_grad_kernel(
    qkv_ref, grad_ref, lse_ref, cos_ref, a_ref, b_ref, row_ref, col_ref, out_ref, key_ref, value_ref
):
    length, lanes = grad_ref.shape
    key_ref[...] = jnp.zeros_like(key_ref)
    value_ref[...] = jnp.zeros_like(value_ref)
    for start, low, high in windows(length):
        mask = allowed_mask(row_ref, col_ref, start, low, high)
        query = qkv_ref[start:high, :lanes]
        key = qkv_ref[low:high, lanes : 2 * lanes]
        value = qkv_ref[low:high, 2 * lanes :]
        grad = grad_ref[start:high, :]
        query_grad = jnp.zeros((BLOCK, lanes), F32)
        key_grad = jnp.zeros((high - low, lanes), F32)
        value_grad = jnp.zeros((high - low, lanes), F32)
        for head in range(lanes // HEAD_DIM):
            own = head_lanes(BLOCK, head, lanes)
            own_keys = head_lanes(high - low, head, lanes)
            none = jnp.zeros_like(query)
            scores = nt(key, jnp.where(own, query, none))
            scores = jnp.where(mask, scores, -1e30)
            attend = jnp.exp(scores - lse_ref[0, head : head + 1, start:high])
            attend_grad = nt(value, jnp.where(own, grad, none))
            inner = jnp.sum(attend * attend_grad, axis=0, keepdims=True)
            score_grad = (attend * (attend_grad - inner)).astype(BF)
            query_grad = jnp.where(own, tn(score_grad, key), query_grad)
            key_grad = jnp.where(
                own_keys, jnp.dot(score_grad, query, preferred_element_type=F32), key_grad
            )
            value_grad = jnp.where(
                own_keys,
                jnp.dot(attend.astype(BF), grad, preferred_element_type=F32),
                value_grad,
            )
        back = [ref[start:high, :] for ref in (cos_ref, a_ref, b_ref)]
        query_grad = turn(query_grad * SCALE, back[0], -back[1], -back[2])
        out_ref[start:high, :lanes] = query_grad.astype(BF)
        key_ref[low:high, :] += key_grad
        value_ref[low:high, :] += value_grad
    key_grad = turn(key_ref[...], cos_ref[...], -a_ref[...], -b_ref[...])
    out_ref[:, lanes : 2 * lanes] = key_grad.astype(BF)
    out_ref[:, 2 * lanes :] = value_ref[...].astype(BF)


def attention_specs(length, lanes):
    table = pl.BlockSpec((length, lanes), lambda s: (0, 0))
    return dict(
        table=table,
        wide=pl.BlockSpec((length, 3 * lanes), lambda s: (s, 0)),
        slim=pl.BlockSpec((length, lanes), lambda s: (s, 0)),
        lse=pl.BlockSpec((1, lanes // HEAD_DIM, length), lambda s: (s, 0, 0)),
        row=pl.BlockSpec((1, 1, length), lambda s: (s, 0, 0)),
        col=pl.BlockSpec((length, 1), lambda s: (s, 0)),
    )


def attention(mixed, lanes, tables, segments):
    sequences, length = segments.shape
    spec = attention_specs(length, lanes)
    rows = sequences * length
    return pl.pallas_call(
        attend_kernel,
        grid=(sequences,),
        in_specs=[spec["wide"]] + [spec["table"]] * 3 + [spec["row"], spec["col"]],
        out_specs=[spec["wide"], spec["slim"], spec["lse"]],
        out_shape=[
            jax.ShapeDtypeStruct((rows, 3 * lanes), BF),
            jax.ShapeDtypeStruct((rows, lanes), BF),
            jax.ShapeDtypeStruct((sequences, lanes // HEAD_DIM, length), F32),
        ],
        compiler_params=pltpu.CompilerParams(vmem_limit_bytes=32 << 20),
        name="attend",
    )(mixed, *tables, segments[:, None, :], segments.reshape(-1, 1))


def attention_grad(qkv, grad, lse, tables, segments):
    sequences, length = segments.shape
    rows, lanes = grad.shape
    spec = attention_specs(length, lanes)
    return pl.pallas_call(
        attend_grad_kernel,
        grid=(sequences,),
        in_specs=[spec["wide"], spec["slim"], spec["lse"]]
        + [spec["table"]] * 3
        + [spec["row"], spec["col"]],
        out_specs=spec["wide"],
        out_shape=jax.ShapeDtypeStruct((rows, 3 * lanes), BF),
        scratch_shapes=[pltpu.VMEM((length, lanes), F32)] * 2,
        compiler_params=pltpu.CompilerParams(vmem_limit_bytes=32 << 20),
        name="attend_grad",
    )(qkv, grad, lse, *tables, segments[:, None, :], segments.reshape(-1, 1))


def place(order, sources, count, axis, shape):
    arrays = []
    for array, _, _, _ in sources:
        if not any(array is seen for seen in arrays):
            arrays.append(array)
    where = [[array is seen for seen in arrays].index(True) for array, _, _, _ in sources]
    size = shape[axis] // count

    def kernel(order_ref, *refs):
        ins, out = refs[: len(arrays)], refs[-1]
        for i, (_, (rows, cols), slot, entry) in enumerate(sources):
            to = pl.multiple_of((slot * 4 + order_ref[entry]) * size, size)
            if axis == 0:
                out[pl.ds(to, size), :] = ins[where[i]][rows : rows + size, cols : cols + shape[1]]
            else:
                out[:, pl.ds(to, size)] = ins[where[i]][rows : rows + shape[0], cols : cols + size]

    if axis == 1 and size % 128:
        result = jnp.zeros(shape, arrays[0].dtype)
        for array, (rows, cols), slot, entry in sources:
            piece = lax.slice(array, (rows, cols), (rows + shape[0], cols + size))
            to = (slot * 4 + order[entry]) * size
            result = lax.dynamic_update_slice_in_dim(result, piece, to, 1)
        return result

    whole = pl.BlockSpec(memory_space=pltpu.VMEM)
    return pl.pallas_call(
        kernel,
        in_specs=[pl.BlockSpec(memory_space=pltpu.SMEM)] + [whole] * len(arrays),
        out_specs=whole,
        out_shape=jax.ShapeDtypeStruct(shape, arrays[0].dtype),
        compiler_params=pltpu.CompilerParams(vmem_limit_bytes=24 << 20),
        name="place",
    )(order, *arrays)


def swap_with(values, axis, mask, size):
    return lax.ppermute(values, axis, [(i, i ^ mask) for i in range(size)])


def dot(left, right, dims):
    return lax.dot_general(left, right, (dims, ((), ())), preferred_element_type=F32)


def after(values, *earlier):
    return lax.optimization_barrier((values,) + earlier)[0]


def step(*values):
    return lax.optimization_barrier(values)


TEAM = ("l", "x", "y", "core")


def make_body(groups):
    def body(
        hidden_in, ln_gain, ln_bias, w_qkv, b_qkv, w_dense, b_dense,
        w_fc1, b_fc1, w_fc2, b_fc2, segment_ids, out_grad,
    ):
        group, lb, xb = lax.axis_index("h"), lax.axis_index("l"), lax.axis_index("x")
        quad = 2 * lb + xb
        tile, width = hidden_in.shape
        span = width // groups

        def part(values, which, count, axis):
            size = values.shape[axis] // count
            return lax.dynamic_slice_in_dim(values, which * size, size, axis)

        def fixed(values, which, count, axis):
            size = values.shape[axis] // count
            return lax.slice_in_dim(values, which * size, (which + 1) * size, axis=axis)

        def own_order(values, axis):
            bit = 1
            while bit < groups:
                blocks = [fixed(values, j ^ bit, groups, axis) for j in range(groups)]
                flipped = jnp.concatenate(blocks, axis=axis)
                values = jnp.where((group // bit) % 2 == 1, flipped, values)
                bit *= 2
            return values

        def trade(give, own):
            return [own] + [swap_with(give(quad ^ m), ("l", "x"), m, 4) for m in (1, 2, 3)]

        def in_order(parts, axis):
            blocks = [
                jnp.where(
                    lb == 1,
                    jnp.where(xb == 1, parts[j ^ 3], parts[j ^ 2]),
                    jnp.where(xb == 1, parts[j ^ 1], parts[j]),
                )
                for j in range(4)
            ]
            return jnp.concatenate(blocks, axis=axis)

        def swap_h(values):
            return [swap_with(values, "h", k, groups) for k in range(1, groups)]

        def fold_start(rows, axis, name):
            sent = lax.dynamic_index_in_dim(rows, 1 - lax.axis_index(name), axis, keepdims=False)
            return swap_with(sent, name, 1, 2)

        def fold_end(rows, got, axis, name):
            mine = lax.dynamic_index_in_dim(rows, lax.axis_index(name), axis, keepdims=False)
            return mine.astype(F32) + got.astype(F32)

        def halves(rows):
            return rows[..., : width // 2], rows[..., width // 2 :]

        def swap_c(values):
            return swap_with(values, "core", 1, 2)

        def quad_swap(values, m):
            return swap_with(values, ("l", "x"), m, 4)

        seg_len = segment_ids.shape[1]
        in_cols = 3 * w_qkv.shape[2] // 4 + w_fc1.shape[1] // 4
        labels = jnp.pad(segment_ids.astype(BF), ((0, 15), (0, in_cols - seg_len)))

        def take_in(which):
            piece = part(w_qkv, which, 4, 2)
            rows = jnp.concatenate(
                [piece[:, j] for j in range(3)] + [part(w_fc1, which, 4, 1)], axis=1
            )
            return jnp.concatenate([rows, labels], axis=0)

        def take_out(which):
            return jnp.concatenate([part(w_dense, which, 4, 0), part(w_fc2, which, 4, 0)], axis=0)

        def stacked(parts, axis):
            return jnp.concatenate(parts, axis=axis)

        def unstack(values, count, axis):
            return [fixed(values, m, count, axis) for m in range(count)]

        local = w_dense.shape[0] // 4
        qkv_cols = 3 * local

        order = jnp.stack([quad, quad ^ 1, quad ^ 2, quad ^ 3])
        rows_in, cols_out = w_fc1.shape[0], w_fc2.shape[1]

        hidden = hidden_in.astype(F32)
        mine_n = own_order(layer_norm(hidden, ln_gain, ln_bias).astype(BF), 1)
        mine_g = own_order(out_grad, 1)
        in_own = take_in(quad)
        in_first = swap_h(in_own[:rows_in])
        in_parts = trade(take_in, in_own)
        next_n = swap_with(mine_n, "l", 1, 2)
        in_first, in_parts, next_n = step(in_first, in_parts, next_n)

        def gather_tokens(mine, other):
            rows = lax.all_gather(
                jnp.stack([mine, other]), ("x", "y", "core"), axis=1, tiled=True
            )
            return rows.reshape(-1, width)

        normed_all = gather_tokens(mine_n, next_n)
        in_rest = swap_h(stacked([p[:rows_in] for p in in_parts[1:]], 0))
        out_parts = trade(take_out, take_out(quad))
        next_g = swap_with(mine_g, "l", 1, 2)
        out_stack = stacked(out_parts, 1)
        in_rest, out_parts, out_stack, next_g = step(in_rest, out_parts, out_stack, next_g)

        out_rest = swap_h(out_stack)
        in_first, in_parts, in_rest = step(in_first, in_parts, in_rest)
        sources = [(p, (0, 0), 0, m) for m, p in enumerate(in_parts)]
        for k in range(1, groups):
            sources.append((in_first[k - 1], (0, 0), k, 0))
            sources += [(in_rest[k - 1], ((m - 1) * rows_in, 0), k, m) for m in (1, 2, 3)]
        in_w = place(order, sources, 4 * groups, 0, (width, in_cols))
        labels_all = [p[rows_in, :seg_len].astype(jnp.int32)[None] for p in in_parts]
        ordered = in_order(labels_all, 0)
        segments = jnp.where(lb == 1, jnp.roll(ordered, 2, axis=0), ordered)
        grad_all = gather_tokens(after(mine_g, normed_all, out_stack), next_g)
        in_b = stacked([part(b_qkv, quad, 4, 1).reshape(-1), part(b_fc1, quad, 4, 0)], 0)
        mixed = dot(normed_all, in_w, ((1,), (0,))) + in_b
        tables = rotary_tables(segments.shape[1], local)
        qkv, context, lse = attention(mixed, local, tables, segments)
        before = mixed[:, qkv_cols:]
        acts = stacked([context, gelu_tanh(before).astype(BF)], 1)
        qkv, acts, lse, before, out_rest = step(qkv, acts, lse, before, out_rest)

        def slot(values, k, axis):
            return fixed(values, k, groups, axis)

        out_rows = acts.shape[1]
        out_part = dot(acts, grad_all, ((0,), (0,))).astype(BF)
        cuts = [out_rows * i // 40 for i in (0, 10, 17, 24, 33, 40)]
        out_send = [
            [slot(out_part, k, 1)[cuts[i] : cuts[i + 1]] for i in range(5)] for k in range(groups)
        ]
        out_ws = []
        for low, high in ((0, local), (local, out_rows)):
            sources = [(p, (low, 0), 0, m) for m, p in enumerate(out_parts)]
            for k in range(1, groups):
                sources += [(out_rest[k - 1], (low, m * cols_out), k, m) for m in range(4)]
            out_ws.append(place(order, sources, 4 * groups, 1, (high - low, width)))
        out_send, out_ws = step(out_send, out_ws)

        def send_out(i):
            return [swap_with(out_send[k][i], "h", k, groups) for k in range(1, groups)]

        out_0 = send_out(0)
        out_ws, qkv, lse = step(out_ws, qkv, lse)
        context_grad = dot(grad_all, out_ws[0], ((1,), (1,))).astype(BF)
        mixed_grad = attention_grad(qkv, context_grad, lse, tables, segments)
        mixed_grad, out_0, out_send = step(mixed_grad, out_0, out_send)

        out_1 = send_out(1)
        mixed_grad, before = step(mixed_grad, before)
        activated_grad = dot(after(grad_all, mixed_grad), out_ws[1], ((1,), (1,)))
        before_grad = jax.vjp(gelu_tanh, before)[1](activated_grad)[0].astype(BF)
        into = stacked([mixed_grad, before_grad], 1)
        out_w = stacked(out_ws, 0)
        into, out_1, out_w, out_send = step(into, out_1, out_w, out_send)
        out_2 = send_out(2)
        into, out_w = step(into, out_w)
        branch = dot(after(acts, into), out_w, ((1,), (0,))).astype(BF)
        team_sum = lax.psum_scatter(
            branch.reshape(2, -1, width), ("x", "y", "core"), scatter_dimension=1, tiled=True
        )
        into, branch, out_2, out_send = step(into, branch, out_2, out_send)
        out_3 = send_out(3)
        into, branch = step(into, branch)
        in_part = dot(normed_all, into, ((0,), (0,))).astype(BF)

        def block(k, m):
            start = k * span + (quad ^ m) * (span // 4)
            return lax.dynamic_slice_in_dim(in_part, start, span // 4, 0)

        def add_up(mine, others):
            mine = mine.astype(F32)
            for piece in others:
                mine = mine + piece.astype(F32)
            return mine

        in_part, out_3, into, out_send = step(in_part, out_3, into, out_send)

        out_4 = send_out(4)
        into, in_w = step(into, in_w)
        terms = dot(into, in_w, ((1,), (1,)))
        unit = (normed_all.astype(F32) - own_order(ln_bias, 0)) / own_order(ln_gain, 0)
        gain_sum, shift_sum = jnp.sum(terms * unit, axis=0), jnp.sum(terms, axis=0)
        shape5 = (2, 2, 2, 2, tile, width)
        terms = terms.astype(BF).reshape(shape5)
        in_part, terms, gain_sum, shift_sum, out_4 = step(
            in_part, terms, gain_sum, shift_sum, out_4
        )

        def send_in(m):
            return [swap_with(block(k, m), "h", k, groups) for k in range(1, groups)]

        in_1 = send_in(1)
        got_c = fold_start(terms, 3, "core")
        out_got = (out_0, out_1, out_2, out_3, out_4)
        out_sum = stacked([add_up(out_send[0][i], got) for i, got in enumerate(out_got)], 0)
        sent = out_sum.astype(BF)
        out_back = [quad_swap(part(sent, quad ^ m, 4, 1), m) for m in (1, 2, 3)]
        small = [
            own_order(gain_sum, 0),
            own_order(shift_sum, 0),
            jnp.sum(out_grad.astype(F32), axis=0),
        ]
        team = 4 * (2 * lax.axis_index("y") + lax.axis_index("core"))
        bias = jnp.sum(into, axis=0, dtype=F32)
        size = into.shape[1]
        bias = lax.dynamic_update_slice(jnp.zeros((16 * size,), F32), bias, ((team + quad) * size,))
        total = stacked(small + [bias], 0)
        rows = fold_end(terms, got_c, 3, "core").astype(BF)
        in_1, rows, out_back, out_sum, total, in_part = step(
            in_1, rows, out_back, out_sum, total, in_part
        )

        in_2 = send_in(2)
        left, right = halves(rows)
        got_l, got_r = fold_start(left, 2, "y"), fold_start(right, 1, "x")
        total = total + swap_c(total)
        back_1 = add_up(block(0, 1), in_1).astype(BF)
        left = fold_end(left, got_l, 2, "y").astype(BF)
        right = fold_end(right, got_r, 1, "x").astype(BF)
        out_pieces = [part(out_sum, quad, 4, 1)] + [p.astype(F32) for p in out_back]
        dense_grad = in_order([p[:local] for p in out_pieces], 0)
        down_grad = in_order([p[local:] for p in out_pieces], 0)
        in_2, left, right, total, dense_grad, down_grad, back_1, in_part = step(
            in_2, left, right, total, dense_grad, down_grad, back_1, in_part
        )

        in_3 = send_in(3)
        back_1 = quad_swap(back_1, 1)
        got_l, got_r = fold_start(left, 1, "x"), fold_start(right, 1, "y")
        total = total + swap_with(total, "y", 1, 2)
        back_2 = add_up(block(0, 2), in_2).astype(BF)
        rows = stacked(
            [fold_end(left, got_l, 1, "x").astype(BF), fold_end(right, got_r, 1, "y").astype(BF)],
            -1,
        )
        in_3, rows, total, back_1, back_2, in_part = step(
            in_3, rows, total, back_1, back_2, in_part
        )

        in_0 = send_in(0)
        got_n = swap_with(rows[1], "l", 1, 2)
        back_2 = quad_swap(back_2, 2)
        total = total + swap_with(total, "x", 1, 2)
        back_3 = add_up(block(0, 3), in_3).astype(BF)
        in_0, got_n, back_2, back_3, total, in_part = step(
            in_0, got_n, back_2, back_3, total, in_part
        )

        back_3 = quad_swap(back_3, 3)
        got_m = swap_with(team_sum[1], "l", 1, 2)
        total = total + swap_with(total, "l", 1, 2)
        normed_grad = own_order(rows[0].astype(F32) + got_n.astype(F32), 1)
        hidden_grad = jax.vjp(lambda v: layer_norm(v, ln_gain, ln_bias), hidden)[1](normed_grad)[0]
        input_grad = out_grad.astype(F32) + hidden_grad
        own_in = add_up(block(0, 0), in_0)
        back_3, got_m, total, input_grad, own_in = step(back_3, got_m, total, input_grad, own_in)

        bit = 1
        while bit < groups:
            total = total + swap_with(total, "h", bit, groups)
            bit *= 2
        branch = own_order(team_sum[0].astype(F32) + got_m.astype(F32), 1)
        hidden_out = (hidden + branch + b_dense + b_fc2).astype(BF)
        pieces = [own_in] + [p.astype(F32) for p in (back_1, back_2, back_3)]
        up_grad = in_order([p[:, qkv_cols:] for p in pieces], 1)
        qkv_grad = jnp.stack(
            [in_order([p[:, j * local : (j + 1) * local] for p in pieces], 1) for j in range(3)],
            axis=1,
        )
        gain_grad, shift_grad, out_bias_grad = (
            total[:width], total[width : 2 * width], total[2 * width : 3 * width]
        )
        bias = lax.dynamic_slice(total, (3 * width + team * size,), (4 * size,)).reshape(4, size)
        up_bias_grad = bias[:, qkv_cols:].reshape(-1)
        qkv_bias_grad = jnp.stack(
            [bias[:, j * local : (j + 1) * local].reshape(-1) for j in range(3)]
        )
        return (
            hidden_out, input_grad, gain_grad, shift_grad, qkv_grad, qkv_bias_grad,
            dense_grad, out_bias_grad, up_grad, up_bias_grad, down_grad, out_bias_grad,
        )

    return body


def solution(mesh):
    groups = mesh.shape["fsdp"] // 4
    grid = Mesh(mesh.devices.reshape(groups, 2, 2, 2, 2), ("h", "l", "x", "y", "core"))
    rows, cols = ("h", "l", "x"), ("y", "core")
    tokens = rows + cols
    in_specs = (
        P(tokens, None), P(), P(), P(rows, None, cols), P(None, cols), P(cols, rows), P(),
        P(rows, cols), P(cols), P(cols, rows), P(), P(rows, None), P(tokens, None),
    )
    out_specs = (
        P(tokens, None), P(tokens, None), P(), P(), P(rows, None, cols), P(None, cols),
        P(cols, rows), P(), P(rows, cols), P(cols), P(cols, rows), P(),
    )
    return jax.shard_map(
        make_body(groups), mesh=grid, in_specs=in_specs, out_specs=out_specs, check_vma=False
    )
```

```python
import math

import jax
import jax.numpy as jnp
from jax import lax
from jax.experimental import pallas as pl
from jax.experimental.pallas import tpu as pltpu
from jax.sharding import Mesh
from jax.sharding import PartitionSpec as P

HEAD_DIM = 64
ROT = 32
EPS = 1e-05
BLOCK = 128
REACH = 256
SCALE = 1.0 / math.sqrt(HEAD_DIM)

BF = jnp.bfloat16
F32 = jnp.float32


def layer_norm(values, norm_gain, norm_shift):
    centred = values - jnp.mean(values, axis=-1, keepdims=True)
    variance = jnp.mean(centred * centred, axis=-1, keepdims=True)
    return centred * lax.rsqrt(variance + EPS) * norm_gain + norm_shift


def gelu_tanh(values):
    return jax.nn.gelu(values, approximate=True)


def rotary_tables(length, lanes):
    lane = jnp.arange(lanes) % HEAD_DIM
    pair = lane % (ROT // 2)
    angles = jnp.arange(length).astype(F32)[:, None] * (
        10000.0 ** (-(2.0 * pair.astype(F32)) / ROT)
    )
    cosine = jnp.where(lane < ROT, jnp.cos(angles), 1.0)
    sine = jnp.sin(angles)
    first = jnp.where(lane < ROT // 2, -sine, 0.0)
    second = jnp.where((lane >= ROT // 2) & (lane < ROT), sine, 0.0)
    return cosine, first, second


def turn(values, cosine, first, second):
    half, lanes = ROT // 2, values.shape[1]
    return (
        values * cosine
        + pltpu.roll(values, lanes - half, 1) * first
        + pltpu.roll(values, half, 1) * second
    )


def nt(left, right):
    return lax.dot_general(left, right, (((1,), (1,)), ((), ())), preferred_element_type=F32)


def tn(left, right):
    return lax.dot_general(left, right, (((0,), (0,)), ((), ())), preferred_element_type=F32)


def windows(length):
    for start in range(0, length, BLOCK):
        low = max(0, (start - REACH + 1) // BLOCK * BLOCK)
        yield start, low, start + BLOCK


def allowed_mask(row_ref, col_ref, start, low, high):
    size = high - low
    key = low + lax.broadcasted_iota(jnp.int32, (size, BLOCK), 0)
    query = start + lax.broadcasted_iota(jnp.int32, (size, BLOCK), 1)
    same = col_ref[low:high, :] == row_ref[0, :, start : start + BLOCK]
    return same & (key <= query)


def head_lanes(rows, head, lanes):
    lane = lax.broadcasted_iota(jnp.int32, (rows, lanes), 1)
    return lane // HEAD_DIM == head


def attend_kernel(mixed_ref, cos_ref, a_ref, b_ref, row_ref, col_ref, qkv_ref, out_ref, lse_ref):
    length, lanes = out_ref.shape
    tables = cos_ref[...], a_ref[...], b_ref[...]
    query = turn(mixed_ref[:, :lanes], *tables).astype(BF)
    query = (query.astype(F32) * SCALE).astype(BF)
    key = turn(mixed_ref[:, lanes : 2 * lanes], *tables).astype(BF)
    value = mixed_ref[:, 2 * lanes :].astype(BF)
    qkv_ref[:, :lanes] = query
    qkv_ref[:, lanes : 2 * lanes] = key
    qkv_ref[:, 2 * lanes :] = value
    for start, low, high in windows(length):
        mask = allowed_mask(row_ref, col_ref, start, low, high)
        mine = query[start:high]
        out = jnp.zeros((BLOCK, lanes), F32)
        for head in range(lanes // HEAD_DIM):
            own = head_lanes(BLOCK, head, lanes)
            scores = nt(key[low:high], jnp.where(own, mine, jnp.zeros_like(mine)))
            scores = jnp.where(mask, scores, -1e30)
            highest = jnp.max(scores, axis=0, keepdims=True)
            shifted = jnp.exp(scores - highest)
            total = jnp.sum(shifted, axis=0, keepdims=True)
            attend = (shifted / total).astype(BF)
            out = jnp.where(own, tn(attend, value[low:high]), out)
            lse_ref[0, head : head + 1, start:high] = highest + jnp.log(total)
        out_ref[start:high, :] = out.astype(BF)


def attend_grad_kernel(
    qkv_ref, grad_ref, lse_ref, cos_ref, a_ref, b_ref, row_ref, col_ref, out_ref, key_ref, value_ref
):
    length, lanes = grad_ref.shape
    key_ref[...] = jnp.zeros_like(key_ref)
    value_ref[...] = jnp.zeros_like(value_ref)
    for start, low, high in windows(length):
        mask = allowed_mask(row_ref, col_ref, start, low, high)
        query = qkv_ref[start:high, :lanes]
        key = qkv_ref[low:high, lanes : 2 * lanes]
        value = qkv_ref[low:high, 2 * lanes :]
        grad = grad_ref[start:high, :]
        query_grad = jnp.zeros((BLOCK, lanes), F32)
        key_grad = jnp.zeros((high - low, lanes), F32)
        value_grad = jnp.zeros((high - low, lanes), F32)
        for head in range(lanes // HEAD_DIM):
            own = head_lanes(BLOCK, head, lanes)
            own_keys = head_lanes(high - low, head, lanes)
            none = jnp.zeros_like(query)
            scores = nt(key, jnp.where(own, query, none))
            scores = jnp.where(mask, scores, -1e30)
            attend = jnp.exp(scores - lse_ref[0, head : head + 1, start:high])
            attend_grad = nt(value, jnp.where(own, grad, none))
            inner = jnp.sum(attend * attend_grad, axis=0, keepdims=True)
            score_grad = (attend * (attend_grad - inner)).astype(BF)
            query_grad = jnp.where(own, tn(score_grad, key), query_grad)
            key_grad = jnp.where(
                own_keys, jnp.dot(score_grad, query, preferred_element_type=F32), key_grad
            )
            value_grad = jnp.where(
                own_keys,
                jnp.dot(attend.astype(BF), grad, preferred_element_type=F32),
                value_grad,
            )
        back = [ref[start:high, :] for ref in (cos_ref, a_ref, b_ref)]
        query_grad = turn(query_grad * SCALE, back[0], -back[1], -back[2])
        out_ref[start:high, :lanes] = query_grad.astype(BF)
        key_ref[low:high, :] += key_grad
        value_ref[low:high, :] += value_grad
    key_grad = turn(key_ref[...], cos_ref[...], -a_ref[...], -b_ref[...])
    out_ref[:, lanes : 2 * lanes] = key_grad.astype(BF)
    out_ref[:, 2 * lanes :] = value_ref[...].astype(BF)


def attention_specs(length, lanes):
    table = pl.BlockSpec((length, lanes), lambda s: (0, 0))
    return dict(
        table=table,
        wide=pl.BlockSpec((length, 3 * lanes), lambda s: (s, 0)),
        slim=pl.BlockSpec((length, lanes), lambda s: (s, 0)),
        lse=pl.BlockSpec((1, lanes // HEAD_DIM, length), lambda s: (s, 0, 0)),
        row=pl.BlockSpec((1, 1, length), lambda s: (s, 0, 0)),
        col=pl.BlockSpec((length, 1), lambda s: (s, 0)),
    )


def attention(mixed, lanes, tables, segments):
    sequences, length = segments.shape
    spec = attention_specs(length, lanes)
    rows = sequences * length
    return pl.pallas_call(
        attend_kernel,
        grid=(sequences,),
        in_specs=[spec["wide"]] + [spec["table"]] * 3 + [spec["row"], spec["col"]],
        out_specs=[spec["wide"], spec["slim"], spec["lse"]],
        out_shape=[
            jax.ShapeDtypeStruct((rows, 3 * lanes), BF),
            jax.ShapeDtypeStruct((rows, lanes), BF),
            jax.ShapeDtypeStruct((sequences, lanes // HEAD_DIM, length), F32),
        ],
        compiler_params=pltpu.CompilerParams(vmem_limit_bytes=32 << 20),
        name="attend",
    )(mixed, *tables, segments[:, None, :], segments.reshape(-1, 1))


def attention_grad(qkv, grad, lse, tables, segments):
    sequences, length = segments.shape
    rows, lanes = grad.shape
    spec = attention_specs(length, lanes)
    return pl.pallas_call(
        attend_grad_kernel,
        grid=(sequences,),
        in_specs=[spec["wide"], spec["slim"], spec["lse"]]
        + [spec["table"]] * 3
        + [spec["row"], spec["col"]],
        out_specs=spec["wide"],
        out_shape=jax.ShapeDtypeStruct((rows, 3 * lanes), BF),
        scratch_shapes=[pltpu.VMEM((length, lanes), F32)] * 2,
        compiler_params=pltpu.CompilerParams(vmem_limit_bytes=32 << 20),
        name="attend_grad",
    )(qkv, grad, lse, *tables, segments[:, None, :], segments.reshape(-1, 1))


def place(order, sources, count, axis, shape):
    arrays = []
    for array, _, _, _ in sources:
        if not any(array is seen for seen in arrays):
            arrays.append(array)
    where = [[array is seen for seen in arrays].index(True) for array, _, _, _ in sources]
    size = shape[axis] // count

    def kernel(order_ref, *refs):
        ins, out = refs[: len(arrays)], refs[-1]
        for i, (_, (rows, cols), slot, entry) in enumerate(sources):
            to = pl.multiple_of((slot * 4 + order_ref[entry]) * size, size)
            if axis == 0:
                out[pl.ds(to, size), :] = ins[where[i]][rows : rows + size, cols : cols + shape[1]]
            else:
                out[:, pl.ds(to, size)] = ins[where[i]][rows : rows + shape[0], cols : cols + size]

    if axis == 1 and size % 128:
        result = jnp.zeros(shape, arrays[0].dtype)
        for array, (rows, cols), slot, entry in sources:
            piece = lax.slice(array, (rows, cols), (rows + shape[0], cols + size))
            to = (slot * 4 + order[entry]) * size
            result = lax.dynamic_update_slice_in_dim(result, piece, to, 1)
        return result

    whole = pl.BlockSpec(memory_space=pltpu.VMEM)
    return pl.pallas_call(
        kernel,
        in_specs=[pl.BlockSpec(memory_space=pltpu.SMEM)] + [whole] * len(arrays),
        out_specs=whole,
        out_shape=jax.ShapeDtypeStruct(shape, arrays[0].dtype),
        compiler_params=pltpu.CompilerParams(vmem_limit_bytes=24 << 20),
        name="place",
    )(order, *arrays)


def swap_with(values, axis, mask, size):
    return lax.ppermute(values, axis, [(i, i ^ mask) for i in range(size)])


def dot(left, right, dims):
    return lax.dot_general(left, right, (dims, ((), ())), preferred_element_type=F32)


def after(values, *earlier):
    return lax.optimization_barrier((values,) + earlier)[0]


def step(*values):
    return lax.optimization_barrier(values)


TEAM = ("l", "x", "y", "core")


def make_body(groups):
    def body(
        hidden_in, ln_gain, ln_bias, w_qkv, b_qkv, w_dense, b_dense,
        w_fc1, b_fc1, w_fc2, b_fc2, segment_ids, out_grad,
    ):
        group, lb, xb = lax.axis_index("h"), lax.axis_index("l"), lax.axis_index("x")
        quad = 2 * lb + xb
        tile, width = hidden_in.shape
        span = width // groups

        def part(values, which, count, axis):
            size = values.shape[axis] // count
            return lax.dynamic_slice_in_dim(values, which * size, size, axis)

        def fixed(values, which, count, axis):
            size = values.shape[axis] // count
            return lax.slice_in_dim(values, which * size, (which + 1) * size, axis=axis)

        def own_order(values, axis):
            bit = 1
            while bit < groups:
                blocks = [fixed(values, j ^ bit, groups, axis) for j in range(groups)]
                flipped = jnp.concatenate(blocks, axis=axis)
                values = jnp.where((group // bit) % 2 == 1, flipped, values)
                bit *= 2
            return values

        def trade(give, own):
            return [own] + [swap_with(give(quad ^ m), ("l", "x"), m, 4) for m in (1, 2, 3)]

        def in_order(parts, axis):
            blocks = [
                jnp.where(
                    lb == 1,
                    jnp.where(xb == 1, parts[j ^ 3], parts[j ^ 2]),
                    jnp.where(xb == 1, parts[j ^ 1], parts[j]),
                )
                for j in range(4)
            ]
            return jnp.concatenate(blocks, axis=axis)

        def swap_h(values):
            return [swap_with(values, "h", k, groups) for k in range(1, groups)]

        def fold_start(rows, axis, name):
            sent = lax.dynamic_index_in_dim(rows, 1 - lax.axis_index(name), axis, keepdims=False)
            return swap_with(sent, name, 1, 2)

        def fold_end(rows, got, axis, name):
            mine = lax.dynamic_index_in_dim(rows, lax.axis_index(name), axis, keepdims=False)
            return mine.astype(F32) + got.astype(F32)

        def halves(rows):
            return rows[..., : width // 2], rows[..., width // 2 :]

        def swap_c(values):
            return swap_with(values, "core", 1, 2)

        def quad_swap(values, m):
            return swap_with(values, ("l", "x"), m, 4)

        seg_len = segment_ids.shape[1]
        in_cols = 3 * w_qkv.shape[2] // 4 + w_fc1.shape[1] // 4
        labels = jnp.pad(segment_ids.astype(BF), ((0, 15), (0, in_cols - seg_len)))

        def take_in(which):
            piece = part(w_qkv, which, 4, 2)
            rows = jnp.concatenate(
                [piece[:, j] for j in range(3)] + [part(w_fc1, which, 4, 1)], axis=1
            )
            return jnp.concatenate([rows, labels], axis=0)

        def take_out(which):
            return jnp.concatenate([part(w_dense, which, 4, 0), part(w_fc2, which, 4, 0)], axis=0)

        def stacked(parts, axis):
            return jnp.concatenate(parts, axis=axis)

        def unstack(values, count, axis):
            return [fixed(values, m, count, axis) for m in range(count)]

        local = w_dense.shape[0] // 4
        qkv_cols = 3 * local

        order = jnp.stack([quad, quad ^ 1, quad ^ 2, quad ^ 3])
        rows_in, cols_out = w_fc1.shape[0], w_fc2.shape[1]

        hidden = hidden_in.astype(F32)
        mine_n = own_order(layer_norm(hidden, ln_gain, ln_bias).astype(BF), 1)
        mine_g = own_order(out_grad, 1)
        in_own = take_in(quad)
        in_first = swap_h(in_own[:rows_in])
        in_parts = trade(take_in, in_own)
        next_n = swap_with(mine_n, "l", 1, 2)
        in_first, in_parts, next_n = step(in_first, in_parts, next_n)

        def gather_tokens(mine, other):
            rows = lax.all_gather(
                jnp.stack([mine, other]), ("x", "y", "core"), axis=1, tiled=True
            )
            return rows.reshape(-1, width)

        normed_all = gather_tokens(mine_n, next_n)
        in_rest = swap_h(stacked([p[:rows_in] for p in in_parts[1:]], 0))
        out_parts = trade(take_out, take_out(quad))
        next_g = swap_with(mine_g, "l", 1, 2)
        out_stack = stacked(out_parts, 1)
        in_rest, out_parts, out_stack, next_g = step(in_rest, out_parts, out_stack, next_g)

        out_rest = swap_h(out_stack)
        in_first, in_parts, in_rest = step(in_first, in_parts, in_rest)
        sources = [(p, (0, 0), 0, m) for m, p in enumerate(in_parts)]
        for k in range(1, groups):
            sources.append((in_first[k - 1], (0, 0), k, 0))
            sources += [(in_rest[k - 1], ((m - 1) * rows_in, 0), k, m) for m in (1, 2, 3)]
        in_w = place(order, sources, 4 * groups, 0, (width, in_cols))
        labels_all = [p[rows_in, :seg_len].astype(jnp.int32)[None] for p in in_parts]
        ordered = in_order(labels_all, 0)
        segments = jnp.where(lb == 1, jnp.roll(ordered, 2, axis=0), ordered)
        grad_all = gather_tokens(after(mine_g, normed_all, out_stack), next_g)
        in_b = stacked([part(b_qkv, quad, 4, 1).reshape(-1), part(b_fc1, quad, 4, 0)], 0)
        mixed = dot(normed_all, in_w, ((1,), (0,))) + in_b
        tables = rotary_tables(segments.shape[1], local)
        qkv, context, lse = attention(mixed, local, tables, segments)
        before = mixed[:, qkv_cols:]
        acts = stacked([context, gelu_tanh(before).astype(BF)], 1)
        qkv, acts, lse, before, out_rest = step(qkv, acts, lse, before, out_rest)

        def slot(values, k, axis):
            return fixed(values, k, groups, axis)

        out_rows = acts.shape[1]
        out_part = dot(acts, grad_all, ((0,), (0,))).astype(BF)
        cuts = [out_rows * i // 40 for i in (0, 7, 17, 24, 32, 40)]
        out_send = [
            [slot(out_part, k, 1)[cuts[i] : cuts[i + 1]] for i in range(5)] for k in range(groups)
        ]
        out_ws = []
        for low, high in ((0, local), (local, out_rows)):
            sources = [(p, (low, 0), 0, m) for m, p in enumerate(out_parts)]
            for k in range(1, groups):
                sources += [(out_rest[k - 1], (low, m * cols_out), k, m) for m in range(4)]
            out_ws.append(place(order, sources, 4 * groups, 1, (high - low, width)))
        out_send, out_ws = step(out_send, out_ws)

        def send_out(i):
            return [swap_with(out_send[k][i], "h", k, groups) for k in range(1, groups)]

        def team_sum(values):
            return lax.psum_scatter(
                values.reshape(2, -1, width), ("x", "y", "core"), scatter_dimension=1, tiled=True
            )

        out_0 = send_out(0)
        acts, out_ws = step(acts, out_ws)
        branch = dot(acts, stacked(out_ws, 0), ((1,), (0,))).astype(BF)
        branch, out_ws, out_0, out_send = step(branch, out_ws, out_0, out_send)
        branch_sum = team_sum(branch)
        out_1 = send_out(1)
        out_ws, qkv, lse = step(out_ws, qkv, lse)
        context_grad = dot(grad_all, out_ws[0], ((1,), (1,))).astype(BF)
        mixed_grad = attention_grad(qkv, context_grad, lse, tables, segments)
        mixed_grad, out_1, out_send = step(mixed_grad, out_1, out_send)

        out_2 = send_out(2)
        mixed_grad, before = step(mixed_grad, before)
        activated_grad = dot(after(grad_all, mixed_grad), out_ws[1], ((1,), (1,)))
        before_grad = jax.vjp(gelu_tanh, before)[1](activated_grad)[0].astype(BF)
        into = stacked([mixed_grad, before_grad], 1)
        into, out_2, out_send = step(into, out_2, out_send)
        out_3 = send_out(3)
        into, in_w = step(into, in_w)
        terms = dot(into, in_w, ((1,), (1,)))
        unit = (normed_all.astype(F32) - own_order(ln_bias, 0)) / own_order(ln_gain, 0)
        gain_sum, shift_sum = jnp.sum(terms * unit, axis=0), jnp.sum(terms, axis=0)
        terms = terms.astype(BF)
        terms, gain_sum, shift_sum, into, out_3, out_send = step(
            terms, gain_sum, shift_sum, into, out_3, out_send
        )
        terms_sum = team_sum(terms)

        out_4 = send_out(4)
        into, normed_all = step(into, normed_all)
        in_part = dot(normed_all, into, ((0,), (0,))).astype(BF)
        in_part, into, out_4 = step(in_part, into, out_4)

        def block(k, m):
            start = k * span + (quad ^ m) * (span // 4)
            return lax.dynamic_slice_in_dim(in_part, start, span // 4, 0)

        def blocks(k, *which):
            return stacked([block(k, m) for m in which], 0)

        def send_in(*which):
            return [swap_with(blocks(k, *which), "h", k, groups) for k in range(1, groups)]

        def add_up(mine, others):
            mine = mine.astype(F32)
            for piece in others:
                mine = mine + piece.astype(F32)
            return mine

        in_a = send_in(3, 2)
        out_got = (out_0, out_1, out_2, out_3, out_4)
        out_sum = stacked([add_up(out_send[0][i], got) for i, got in enumerate(out_got)], 0)
        sent = out_sum.astype(BF)
        out_back = [quad_swap(part(sent, quad ^ m, 4, 1), m) for m in (1, 2, 3)]
        got_m = swap_with(branch_sum[1], "l", 1, 2)
        small = [
            own_order(gain_sum, 0),
            own_order(shift_sum, 0),
            jnp.sum(out_grad.astype(F32), axis=0),
        ]
        team = 4 * (2 * lax.axis_index("y") + lax.axis_index("core"))
        bias = jnp.sum(into, axis=0, dtype=F32)
        size = into.shape[1]
        bias = lax.dynamic_update_slice(jnp.zeros((16 * size,), F32), bias, ((team + quad) * size,))
        total = stacked(small + [bias], 0)
        total = total + swap_c(total)
        total = total + swap_with(total, "y", 1, 2)
        send_b = [blocks(k, 1, 0) for k in range(groups)]
        keep_a = blocks(0, 3, 2)
        in_a, out_back, out_sum, total, send_b, keep_a, got_m = step(
            in_a, out_back, out_sum, total, send_b, keep_a, got_m
        )

        in_b = [swap_with(send_b[k], "h", k, groups) for k in range(1, groups)]
        keep_a, in_a = step(keep_a, in_a)
        sum_a = unstack(add_up(keep_a, in_a).astype(BF), 2, 0)
        back_3, back_2 = quad_swap(sum_a[0], 3), quad_swap(sum_a[1], 2)
        total = total + swap_with(total, "x", 1, 2)
        total = total + swap_with(total, "l", 1, 2)
        out_pieces = [part(out_sum, quad, 4, 1)] + [p.astype(F32) for p in out_back]
        dense_grad = in_order([p[:local] for p in out_pieces], 0)
        down_grad = in_order([p[local:] for p in out_pieces], 0)
        branch = own_order(branch_sum[0].astype(F32) + got_m.astype(F32), 1)
        hidden_out = (hidden + branch + b_dense + b_fc2).astype(BF)
        in_b, back_3, back_2, total, dense_grad, down_grad, terms_sum, send_b, hidden_out = step(
            in_b, back_3, back_2, total, dense_grad, down_grad, terms_sum, send_b, hidden_out
        )

        got_n = swap_with(terms_sum[1], "l", 1, 2)
        send_b, in_b = step(send_b, in_b)
        sum_b = unstack(add_up(send_b[0], in_b), 2, 0)
        back_1 = quad_swap(sum_b[0].astype(BF), 1)
        bit = 1
        while bit < groups:
            total = total + swap_with(total, "h", bit, groups)
            bit *= 2
        back_1, got_n, total, sum_b = step(back_1, got_n, total, sum_b)
        normed_grad = own_order(terms_sum[0].astype(F32) + got_n.astype(F32), 1)
        hidden_grad = jax.vjp(lambda v: layer_norm(v, ln_gain, ln_bias), hidden)[1](normed_grad)[0]
        input_grad = out_grad.astype(F32) + hidden_grad
        pieces = [sum_b[1]] + [p.astype(F32) for p in (back_1, back_2, back_3)]
        up_grad = in_order([p[:, qkv_cols:] for p in pieces], 1)
        qkv_grad = jnp.stack(
            [in_order([p[:, j * local : (j + 1) * local] for p in pieces], 1) for j in range(3)],
            axis=1,
        )
        gain_grad, shift_grad, out_bias_grad = (
            total[:width], total[width : 2 * width], total[2 * width : 3 * width]
        )
        bias = lax.dynamic_slice(total, (3 * width + team * size,), (4 * size,)).reshape(4, size)
        up_bias_grad = bias[:, qkv_cols:].reshape(-1)
        qkv_bias_grad = jnp.stack(
            [bias[:, j * local : (j + 1) * local].reshape(-1) for j in range(3)]
        )
        return (
            hidden_out, input_grad, gain_grad, shift_grad, qkv_grad, qkv_bias_grad,
            dense_grad, out_bias_grad, up_grad, up_bias_grad, down_grad, out_bias_grad,
        )

    return body


def solution(mesh):
    groups = mesh.shape["fsdp"] // 4
    grid = Mesh(mesh.devices.reshape(groups, 2, 2, 2, 2), ("h", "l", "x", "y", "core"))
    rows, cols = ("h", "l", "x"), ("y", "core")
    tokens = rows + cols
    in_specs = (
        P(tokens, None), P(), P(), P(rows, None, cols), P(None, cols), P(cols, rows), P(),
        P(rows, cols), P(cols), P(cols, rows), P(), P(rows, None), P(tokens, None),
    )
    out_specs = (
        P(tokens, None), P(tokens, None), P(), P(), P(rows, None, cols), P(None, cols),
        P(cols, rows), P(), P(rows, cols), P(cols), P(cols, rows), P(),
    )
    return jax.shard_map(
        make_body(groups), mesh=grid, in_specs=in_specs, out_specs=out_specs, check_vma=False
    )
```

```python
import math

import jax
import jax.numpy as jnp
from jax import lax
from jax.experimental import pallas as pl
from jax.experimental.pallas import tpu as pltpu
from jax.sharding import Mesh
from jax.sharding import PartitionSpec as P

HEAD_DIM = 64
ROT = 32
EPS = 1e-05
BLOCK = 128
ROWS = 512
CHUNK = 512
REACH = 256
SCALE = 1.0 / math.sqrt(HEAD_DIM)

BF = jnp.bfloat16
F32 = jnp.float32


def layer_norm(values, norm_gain, norm_shift):
    centred = values - jnp.mean(values, axis=-1, keepdims=True)
    variance = jnp.mean(centred * centred, axis=-1, keepdims=True)
    return centred * lax.rsqrt(variance + EPS) * norm_gain + norm_shift


def gelu_tanh(values):
    return jax.nn.gelu(values, approximate=True)


def rotary_tables(length, lanes):
    lane = jnp.arange(lanes) % HEAD_DIM
    pair = lane % (ROT // 2)
    angles = jnp.arange(length).astype(F32)[:, None] * (
        10000.0 ** (-(2.0 * pair.astype(F32)) / ROT)
    )
    cosine = jnp.where(lane < ROT, jnp.cos(angles), 1.0)
    sine = jnp.sin(angles)
    first = jnp.where(lane < ROT // 2, -sine, 0.0)
    second = jnp.where((lane >= ROT // 2) & (lane < ROT), sine, 0.0)
    return cosine, first, second


def turn(values, cosine, first, second):
    half, lanes = ROT // 2, values.shape[1]
    return (
        values * cosine
        + pltpu.roll(values, lanes - half, 1) * first
        + pltpu.roll(values, half, 1) * second
    )


def nt(left, right):
    return lax.dot_general(left, right, (((1,), (1,)), ((), ())), preferred_element_type=F32)


def tn(left, right):
    return lax.dot_general(left, right, (((0,), (0,)), ((), ())), preferred_element_type=F32)


def windows(length):
    for start in range(0, length, BLOCK):
        low = max(0, (start - REACH + 1) // BLOCK * BLOCK)
        yield start, low, start + BLOCK


def allowed_mask(row_ref, col_ref, start, low, high):
    size = high - low
    key = low + lax.broadcasted_iota(jnp.int32, (size, BLOCK), 0)
    query = start + lax.broadcasted_iota(jnp.int32, (size, BLOCK), 1)
    same = col_ref[low:high, :] == row_ref[0, :, start : start + BLOCK]
    return same & (key <= query)


def head_lanes(rows, head, lanes):
    lane = lax.broadcasted_iota(jnp.int32, (rows, lanes), 1)
    return lane // HEAD_DIM == head


def attend_kernel(mixed_ref, cos_ref, a_ref, b_ref, row_ref, col_ref, qkv_ref, out_ref, lse_ref):
    length, lanes = out_ref.shape
    tables = cos_ref[...], a_ref[...], b_ref[...]
    query = turn(mixed_ref[:, :lanes], *tables).astype(BF)
    query = (query.astype(F32) * SCALE).astype(BF)
    key = turn(mixed_ref[:, lanes : 2 * lanes], *tables).astype(BF)
    value = mixed_ref[:, 2 * lanes :].astype(BF)
    qkv_ref[:, :lanes] = query
    qkv_ref[:, lanes : 2 * lanes] = key
    qkv_ref[:, 2 * lanes :] = value
    for start, low, high in windows(length):
        mask = allowed_mask(row_ref, col_ref, start, low, high)
        mine = query[start:high]
        out = jnp.zeros((BLOCK, lanes), F32)
        for head in range(lanes // HEAD_DIM):
            own = head_lanes(BLOCK, head, lanes)
            scores = nt(key[low:high], jnp.where(own, mine, jnp.zeros_like(mine)))
            scores = jnp.where(mask, scores, -1e30)
            highest = jnp.max(scores, axis=0, keepdims=True)
            shifted = jnp.exp(scores - highest)
            total = jnp.sum(shifted, axis=0, keepdims=True)
            attend = (shifted / total).astype(BF)
            out = jnp.where(own, tn(attend, value[low:high]), out)
            lse_ref[0, head : head + 1, start:high] = highest + jnp.log(total)
        out_ref[start:high, :] = out.astype(BF)


def attend_grad_kernel(
    qkv_ref, grad_ref, lse_ref, cos_ref, a_ref, b_ref, row_ref, col_ref, into_ref,
    out_ref, key_ref, value_ref,
):
    length, lanes = grad_ref.shape
    key_ref[...] = jnp.zeros_like(key_ref)
    value_ref[...] = jnp.zeros_like(value_ref)
    for start, low, high in windows(length):
        mask = allowed_mask(row_ref, col_ref, start, low, high)
        query = qkv_ref[start:high, :lanes]
        key = qkv_ref[low:high, lanes : 2 * lanes]
        value = qkv_ref[low:high, 2 * lanes :]
        grad = grad_ref[start:high, :]
        query_grad = jnp.zeros((BLOCK, lanes), F32)
        key_grad = jnp.zeros((high - low, lanes), F32)
        value_grad = jnp.zeros((high - low, lanes), F32)
        for head in range(lanes // HEAD_DIM):
            own = head_lanes(BLOCK, head, lanes)
            own_keys = head_lanes(high - low, head, lanes)
            none = jnp.zeros_like(query)
            scores = nt(key, jnp.where(own, query, none))
            scores = jnp.where(mask, scores, -1e30)
            attend = jnp.exp(scores - lse_ref[0, head : head + 1, start:high])
            attend_grad = nt(value, jnp.where(own, grad, none))
            inner = jnp.sum(attend * attend_grad, axis=0, keepdims=True)
            score_grad = (attend * (attend_grad - inner)).astype(BF)
            query_grad = jnp.where(own, tn(score_grad, key), query_grad)
            key_grad = jnp.where(
                own_keys, jnp.dot(score_grad, query, preferred_element_type=F32), key_grad
            )
            value_grad = jnp.where(
                own_keys,
                jnp.dot(attend.astype(BF), grad, preferred_element_type=F32),
                value_grad,
            )
        back = [ref[start:high, :] for ref in (cos_ref, a_ref, b_ref)]
        query_grad = turn(query_grad * SCALE, back[0], -back[1], -back[2])
        out_ref[start:high, :lanes] = query_grad.astype(BF)
        key_ref[low:high, :] += key_grad
        value_ref[low:high, :] += value_grad
    key_grad = turn(key_ref[...], cos_ref[...], -a_ref[...], -b_ref[...])
    out_ref[:, lanes : 2 * lanes] = key_grad.astype(BF)
    out_ref[:, 2 * lanes :] = value_ref[...].astype(BF)


def attention_specs(length, lanes):
    table = pl.BlockSpec((length, lanes), lambda s: (0, 0))
    return dict(
        table=table,
        wide=pl.BlockSpec((length, 3 * lanes), lambda s: (s, 0)),
        slim=pl.BlockSpec((length, lanes), lambda s: (s, 0)),
        lse=pl.BlockSpec((1, lanes // HEAD_DIM, length), lambda s: (s, 0, 0)),
        row=pl.BlockSpec((1, 1, length), lambda s: (s, 0, 0)),
        col=pl.BlockSpec((length, 1), lambda s: (s, 0)),
    )


def attention(mixed, lanes, tables, segments):
    sequences, length = segments.shape
    spec = attention_specs(length, lanes)
    rows = sequences * length
    return pl.pallas_call(
        attend_kernel,
        grid=(sequences,),
        in_specs=[spec["wide"]] + [spec["table"]] * 3 + [spec["row"], spec["col"]],
        out_specs=[spec["wide"], spec["slim"], spec["lse"]],
        out_shape=[
            jax.ShapeDtypeStruct((rows, 3 * lanes), BF),
            jax.ShapeDtypeStruct((rows, lanes), BF),
            jax.ShapeDtypeStruct((sequences, lanes // HEAD_DIM, length), F32),
        ],
        compiler_params=pltpu.CompilerParams(vmem_limit_bytes=32 << 20),
        name="attend",
    )(mixed, *tables, segments[:, None, :], segments.reshape(-1, 1))


def attention_grad(qkv, grad, lse, tables, segments, into):
    sequences, length = segments.shape
    rows, lanes = grad.shape
    spec = attention_specs(length, lanes)
    return pl.pallas_call(
        attend_grad_kernel,
        grid=(sequences,),
        in_specs=[spec["wide"], spec["slim"], spec["lse"]]
        + [spec["table"]] * 3
        + [spec["row"], spec["col"], pl.BlockSpec(memory_space=pl.ANY)],
        out_specs=spec["wide"],
        out_shape=jax.ShapeDtypeStruct(into.shape, BF),
        input_output_aliases={8: 0},
        scratch_shapes=[pltpu.VMEM((length, lanes), F32)] * 2,
        compiler_params=pltpu.CompilerParams(vmem_limit_bytes=32 << 20),
        name="attend_grad",
    )(qkv, grad, lse, *tables, segments[:, None, :], segments.reshape(-1, 1), into)


def gelu_slope(values):
    scale = math.sqrt(2.0 / math.pi)
    square = values * values
    bent = jnp.tanh(scale * (values + 0.044715 * values * square))
    return 0.5 * (1.0 + bent) + 0.5 * values * (1.0 - bent * bent) * scale * (
        1.0 + 3.0 * 0.044715 * square
    )


def branch_kernel(acts_ref, dense_ref, down_ref, out_ref):
    local, width = dense_ref.shape
    for low in range(0, width, CHUNK):
        cols = slice(low, low + CHUNK)
        total = jnp.dot(
            acts_ref[:, :local], dense_ref[:, cols], preferred_element_type=F32
        ) + jnp.dot(acts_ref[:, local:], down_ref[:, cols], preferred_element_type=F32)
        out_ref[:, cols] = total.astype(BF)


def back_kernel(grad_ref, dense_ref, down_ref, mixed_ref, context_ref, into_ref):
    units = down_ref.shape[0]
    first = mixed_ref.shape[1] - units
    grad = grad_ref[...]
    context_ref[...] = nt(grad, dense_ref[...]).astype(BF)
    activated_grad = nt(grad, down_ref[...])
    slope = gelu_slope(mixed_ref[:, first:])
    into_ref[:, :first] = jnp.zeros((into_ref.shape[0], first), BF)
    into_ref[:, first:] = (activated_grad * slope).astype(BF)


def norm_grad(group, groups, mine, got, hidden_in, out_grad, ln_gain):
    rows, width = hidden_in.shape
    span = width // groups

    def kernel(group_ref, mine_ref, got_ref, hidden_ref, cot_ref, gain_ref, out_ref, sum_ref):
        for j in range(groups):
            cols = pl.ds(pl.multiple_of((group_ref[0] ^ j) * span, span), span)
            sum_ref[:, j * span : (j + 1) * span] = mine_ref[:, cols].astype(F32) + got_ref[
                :, cols
            ].astype(F32)
        hidden = hidden_ref[...].astype(F32)
        centred = hidden - jnp.mean(hidden, axis=-1, keepdims=True)
        variance = jnp.mean(centred * centred, axis=-1, keepdims=True)
        scale = lax.rsqrt(variance + EPS)
        unit = centred * scale
        slope = sum_ref[...] * gain_ref[...]
        first = jnp.mean(slope, axis=-1, keepdims=True)
        second = jnp.mean(slope * unit, axis=-1, keepdims=True)
        out_ref[...] = scale * (slope - first - unit * second) + cot_ref[...].astype(F32)

    whole = pl.BlockSpec(memory_space=pltpu.VMEM)
    return pl.pallas_call(
        kernel,
        in_specs=[pl.BlockSpec(memory_space=pltpu.SMEM)] + [whole] * 5,
        out_specs=whole,
        out_shape=jax.ShapeDtypeStruct((rows, width), F32),
        scratch_shapes=[pltpu.VMEM((rows, width), F32)],
        compiler_params=pltpu.CompilerParams(vmem_limit_bytes=24 << 20),
        name="norm_grad",
    )(group[None], mine, got, hidden_in, out_grad, ln_gain[None, :])


def settle(order, pieces, local):
    rows, cols = pieces[0].shape
    units = cols - 3 * local

    def kernel(order_ref, *refs):
        ins, qkv_ref, up_ref = refs[:4], refs[4], refs[5]
        for m, ref in enumerate(ins):
            to = pl.multiple_of(order_ref[m] * units, units)
            up_ref[:, pl.ds(to, units)] = ref[:, 3 * local :].astype(F32)
            to = pl.multiple_of(order_ref[m] * local, local)
            for j in range(3):
                qkv_ref[j, :, pl.ds(to, local)] = ref[:, j * local : (j + 1) * local].astype(F32)

    whole = pl.BlockSpec(memory_space=pltpu.VMEM)
    qkv, up = pl.pallas_call(
        kernel,
        in_specs=[pl.BlockSpec(memory_space=pltpu.SMEM)] + [whole] * 4,
        out_specs=[whole] * 2,
        out_shape=[
            jax.ShapeDtypeStruct((3, rows, 4 * local), F32),
            jax.ShapeDtypeStruct((rows, 4 * units), F32),
        ],
        compiler_params=pltpu.CompilerParams(vmem_limit_bytes=24 << 20),
        name="settle",
    )(order, *pieces)
    return jnp.transpose(qkv, (1, 0, 2)), up


def by_tokens(kernel, name, rows, flops, blocked, whole, outs):
    def cut(cols):
        return pl.BlockSpec((ROWS, cols), lambda i: (i, 0))

    def kept(array):
        return pl.BlockSpec(array.shape, lambda i: (0, 0))

    specs = [cut(a.shape[1]) if a.shape[0] == rows and cutting else kept(a)
             for a, cutting in [(a, True) for a in blocked] + [(a, False) for a in whole]]
    size = sum(a.size * a.dtype.itemsize for a in list(blocked) + list(whole))
    return pl.pallas_call(
        kernel,
        grid=(rows // ROWS,),
        in_specs=specs,
        out_specs=[cut(cols) for cols in outs],
        out_shape=[jax.ShapeDtypeStruct((rows, cols), BF) for cols in outs],
        compiler_params=pltpu.CompilerParams(vmem_limit_bytes=48 << 20),
        cost_estimate=pl.CostEstimate(
            flops=flops, bytes_accessed=size + 2 * rows * sum(outs), transcendentals=0
        ),
        name=name,
    )(*blocked, *whole)


def place(order, sources, count, axis, shape):
    arrays = []
    for array, _, _, _ in sources:
        if not any(array is seen for seen in arrays):
            arrays.append(array)
    where = [[array is seen for seen in arrays].index(True) for array, _, _, _ in sources]
    size = shape[axis] // count

    def kernel(order_ref, *refs):
        ins, out = refs[: len(arrays)], refs[-1]
        for i, (_, (rows, cols), slot, entry) in enumerate(sources):
            to = pl.multiple_of((slot * 4 + order_ref[entry]) * size, size)
            if axis == 0:
                out[pl.ds(to, size), :] = ins[where[i]][rows : rows + size, cols : cols + shape[1]]
            else:
                out[:, pl.ds(to, size)] = ins[where[i]][rows : rows + shape[0], cols : cols + size]

    if axis == 1 and size % 128:
        result = jnp.zeros(shape, arrays[0].dtype)
        for array, (rows, cols), slot, entry in sources:
            piece = lax.slice(array, (rows, cols), (rows + shape[0], cols + size))
            to = (slot * 4 + order[entry]) * size
            result = lax.dynamic_update_slice_in_dim(result, piece, to, 1)
        return result

    whole = pl.BlockSpec(memory_space=pltpu.VMEM)
    return pl.pallas_call(
        kernel,
        in_specs=[pl.BlockSpec(memory_space=pltpu.SMEM)] + [whole] * len(arrays),
        out_specs=whole,
        out_shape=jax.ShapeDtypeStruct(shape, arrays[0].dtype),
        compiler_params=pltpu.CompilerParams(vmem_limit_bytes=24 << 20),
        name="place",
    )(order, *arrays)


def swap_with(values, axis, mask, size):
    return lax.ppermute(values, axis, [(i, i ^ mask) for i in range(size)])


def dot(left, right, dims):
    return lax.dot_general(left, right, (dims, ((), ())), preferred_element_type=F32)


def after(values, *earlier):
    return lax.optimization_barrier((values,) + earlier)[0]


def step(*values):
    return lax.optimization_barrier(values)


TEAM = ("l", "x", "y", "core")


def make_body(groups):
    def body(
        hidden_in, ln_gain, ln_bias, w_qkv, b_qkv, w_dense, b_dense,
        w_fc1, b_fc1, w_fc2, b_fc2, segment_ids, out_grad,
    ):
        group, lb, xb = lax.axis_index("h"), lax.axis_index("l"), lax.axis_index("x")
        quad = 2 * lb + xb
        tile, width = hidden_in.shape
        span = width // groups

        def part(values, which, count, axis):
            size = values.shape[axis] // count
            return lax.dynamic_slice_in_dim(values, which * size, size, axis)

        def fixed(values, which, count, axis):
            size = values.shape[axis] // count
            return lax.slice_in_dim(values, which * size, (which + 1) * size, axis=axis)

        def own_order(values, axis):
            bit = 1
            while bit < groups:
                blocks = [fixed(values, j ^ bit, groups, axis) for j in range(groups)]
                flipped = jnp.concatenate(blocks, axis=axis)
                values = jnp.where((group // bit) % 2 == 1, flipped, values)
                bit *= 2
            return values

        def trade(give, own):
            return [own] + [swap_with(give(quad ^ m), ("l", "x"), m, 4) for m in (1, 2, 3)]

        def in_order(parts, axis):
            blocks = [
                jnp.where(
                    lb == 1,
                    jnp.where(xb == 1, parts[j ^ 3], parts[j ^ 2]),
                    jnp.where(xb == 1, parts[j ^ 1], parts[j]),
                )
                for j in range(4)
            ]
            return jnp.concatenate(blocks, axis=axis)

        def swap_h(values):
            return [swap_with(values, "h", k, groups) for k in range(1, groups)]

        def fold_start(rows, axis, name):
            sent = lax.dynamic_index_in_dim(rows, 1 - lax.axis_index(name), axis, keepdims=False)
            return swap_with(sent, name, 1, 2)

        def fold_end(rows, got, axis, name):
            mine = lax.dynamic_index_in_dim(rows, lax.axis_index(name), axis, keepdims=False)
            return mine.astype(F32) + got.astype(F32)

        def halves(rows):
            return rows[..., : width // 2], rows[..., width // 2 :]

        def swap_c(values):
            return swap_with(values, "core", 1, 2)

        def quad_swap(values, m):
            return swap_with(values, ("l", "x"), m, 4)

        seg_len = segment_ids.shape[1]
        in_cols = 3 * w_qkv.shape[2] // 4 + w_fc1.shape[1] // 4
        labels = jnp.pad(segment_ids.astype(BF), ((0, 15), (0, in_cols - seg_len)))

        def take_in(which):
            piece = part(w_qkv, which, 4, 2)
            rows = jnp.concatenate(
                [piece[:, j] for j in range(3)] + [part(w_fc1, which, 4, 1)], axis=1
            )
            return jnp.concatenate([rows, labels], axis=0)

        def take_out(which):
            return jnp.concatenate([part(w_dense, which, 4, 0), part(w_fc2, which, 4, 0)], axis=0)

        def stacked(parts, axis):
            return jnp.concatenate(parts, axis=axis)

        def unstack(values, count, axis):
            return [fixed(values, m, count, axis) for m in range(count)]

        local = w_dense.shape[0] // 4
        qkv_cols = 3 * local

        order = jnp.stack([quad, quad ^ 1, quad ^ 2, quad ^ 3])
        rows_in, cols_out = w_fc1.shape[0], w_fc2.shape[1]

        def gather_tokens(mine, other):
            rows = lax.all_gather(
                jnp.stack([mine, other]), ("x", "y", "core"), axis=1, tiled=True
            )
            return rows.reshape(-1, width)

        hidden = hidden_in.astype(F32)
        mine_n = own_order(layer_norm(hidden, ln_gain, ln_bias).astype(BF), 1)
        mine_g = own_order(out_grad, 1)
        in_own = take_in(quad)
        in_first = swap_h(in_own[:rows_in])
        next_n = swap_with(mine_n, "l", 1, 2)
        in_send = [take_in(quad ^ m) for m in (1, 2, 3)]
        mine_n, next_n, in_first, in_send, mine_g = step(
            mine_n, next_n, in_first, in_send, mine_g
        )
        normed_all = gather_tokens(mine_n, next_n)
        in_parts = [in_own] + [quad_swap(piece, m) for m, piece in zip((1, 2, 3), in_send)]
        out_own = take_out(quad)
        out_first = swap_h(out_own)
        out_send = [take_out(quad ^ m) for m in (1, 2, 3)]
        in_parts, mine_g, out_own, out_first, out_send = step(
            in_parts, mine_g, out_own, out_first, out_send
        )

        in_low = swap_h(in_parts[1][:rows_in])
        next_g = swap_with(mine_g, "l", 1, 2)
        out_1 = quad_swap(out_send[0], 1)
        in_high = stacked([p[:rows_in] for p in in_parts[2:]], 0)
        in_low, next_g, out_1, in_high, out_send, mine_g = step(
            in_low, next_g, out_1, in_high, out_send, mine_g
        )
        in_rest = swap_h(in_high)
        out_parts = [out_own, out_1] + [quad_swap(out_send[m - 1], m) for m in (2, 3)]
        grad_all = gather_tokens(mine_g, next_g)
        out_stack = stacked(out_parts[1:], 1)
        in_rest, out_parts, out_stack = step(in_rest, out_parts, out_stack)

        out_rest = swap_h(out_stack)
        in_first, in_parts, in_low, in_rest = step(in_first, in_parts, in_low, in_rest)
        sources = [(p, (0, 0), 0, m) for m, p in enumerate(in_parts)]
        for k in range(1, groups):
            sources.append((in_first[k - 1], (0, 0), k, 0))
            sources.append((in_low[k - 1], (0, 0), k, 1))
            sources += [(in_rest[k - 1], ((m - 2) * rows_in, 0), k, m) for m in (2, 3)]
        in_w = place(order, sources, 4 * groups, 0, (width, in_cols))
        labels_all = [p[rows_in, :seg_len].astype(jnp.int32)[None] for p in in_parts]
        ordered = in_order(labels_all, 0)
        segments = jnp.where(lb == 1, jnp.roll(ordered, 2, axis=0), ordered)
        in_b = stacked([part(b_qkv, quad, 4, 1).reshape(-1), part(b_fc1, quad, 4, 0)], 0)
        mixed = dot(normed_all, in_w, ((1,), (0,))) + in_b
        tables = rotary_tables(segments.shape[1], local)
        qkv, context, lse = attention(mixed, local, tables, segments)
        before = mixed[:, qkv_cols:]
        acts = stacked([context, gelu_tanh(before).astype(BF)], 1)
        qkv, acts, lse, mixed = step(qkv, acts, lse, mixed)

        def slot(values, k, axis):
            return fixed(values, k, groups, axis)

        out_rows = acts.shape[1]
        out_part = dot(acts, grad_all, ((0,), (0,))).astype(BF)
        cuts = [out_rows * i // 40 for i in (0, 6, 21, 30, 40)]
        out_send = [
            [slot(out_part, k, 1)[cuts[i] : cuts[i + 1]] for i in range(4)] for k in range(groups)
        ]
        out_send, out_rest = step(out_send, out_rest)
        out_ws = []
        for low, high in ((0, local), (local, out_rows)):
            sources = [(p, (low, 0), 0, m) for m, p in enumerate(out_parts)]
            for k in range(1, groups):
                sources.append((out_first[k - 1], (low, 0), k, 0))
                sources += [(out_rest[k - 1], (low, (m - 1) * cols_out), k, m) for m in (1, 2, 3)]
            out_ws.append(place(order, sources, 4 * groups, 1, (high - low, width)))

        def send_out(i):
            return [swap_with(out_send[k][i], "h", k, groups) for k in range(1, groups)]

        def team_sum(values):
            return lax.psum_scatter(
                values.reshape(2, -1, width), ("x", "y", "core"), scatter_dimension=1, tiled=True
            )

        out_0 = send_out(0)
        acts, out_ws = step(acts, out_ws)
        tokens = acts.shape[0]
        (branch,) = by_tokens(
            branch_kernel, "branch", tokens, 2 * tokens * out_rows * width, [acts], out_ws, [width]
        )
        branch, out_ws, out_0, out_send = step(branch, out_ws, out_0, out_send)
        branch_sum = team_sum(branch)
        out_1 = send_out(1)
        out_ws, qkv, lse, mixed = step(out_ws, qkv, lse, mixed)

        def back(grad_ref, mixed_ref, dense_ref, down_ref, context_ref, into_ref):
            back_kernel(grad_ref, dense_ref, down_ref, mixed_ref, context_ref, into_ref)

        context_grad, into = by_tokens(
            back, "back", tokens, 2 * tokens * out_rows * width, [grad_all, mixed], out_ws,
            [local, in_cols],
        )
        into = attention_grad(qkv, context_grad, lse, tables, segments, into)
        into, out_1, out_send = step(into, out_1, out_send)

        out_2 = send_out(2)
        into, in_w = step(into, in_w)
        terms = dot(into, in_w, ((1,), (1,)))
        unit = (normed_all.astype(F32) - own_order(ln_bias, 0)) / own_order(ln_gain, 0)
        gain_sum, shift_sum = jnp.sum(terms * unit, axis=0), jnp.sum(terms, axis=0)
        terms = terms.astype(BF)
        terms, gain_sum, shift_sum, into, out_2, out_send = step(
            terms, gain_sum, shift_sum, into, out_2, out_send
        )
        terms_sum = team_sum(terms)

        out_3 = send_out(3)
        small = [
            own_order(gain_sum, 0),
            own_order(shift_sum, 0),
            jnp.sum(out_grad.astype(F32), axis=0),
        ]
        bias = jnp.sum(into, axis=0, dtype=F32)
        size = in_cols
        team = 4 * (2 * lax.axis_index("y") + lax.axis_index("core"))
        bias = lax.dynamic_update_slice(jnp.zeros((16 * size,), F32), bias, ((team + quad) * size,))
        total = stacked(small + [bias], 0)
        got = swap_with(total, "l", 1, 2)
        into, normed_all = step(into, normed_all)
        in_part = dot(normed_all, into, ((0,), (0,))).astype(BF)
        in_part, into, out_3, total, got = step(in_part, into, out_3, total, got)

        def block(k, m):
            start = k * span + (quad ^ m) * (span // 4)
            return lax.dynamic_slice_in_dim(in_part, start, span // 4, 0)

        def blocks(k, *which):
            return stacked([block(k, m) for m in which], 0)

        def send_in(*which):
            return [swap_with(blocks(k, *which), "h", k, groups) for k in range(1, groups)]

        def add_up(mine, others):
            mine = mine.astype(F32)
            for piece in others:
                mine = mine + piece.astype(F32)
            return mine

        send_a = [blocks(k, 3, 2) for k in range(groups)]
        send_a, out_0, out_1, out_2, out_3 = step(send_a, out_0, out_1, out_2, out_3)
        in_a = [swap_with(send_a[k], "h", k, groups) for k in range(1, groups)]
        out_got = step(out_0, out_1, out_2, out_3)
        out_sum = stacked([add_up(out_send[0][i], got) for i, got in enumerate(out_got)], 0)
        sent = out_sum.astype(BF)
        out_back = [quad_swap(part(sent, quad ^ m, 4, 1), m) for m in (1, 2, 3)]
        got_m = swap_with(branch_sum[1], "l", 1, 2)
        total = total + got
        bit = 1
        while bit < groups:
            total = total + swap_with(total, "h", bit, groups)
            bit *= 2
        total = total + swap_c(total)
        send_b = [blocks(k, 1, 0) for k in range(groups)]
        keep_a = send_a[0]
        in_a, out_back, out_sum, total, send_b, keep_a, got_m = step(
            in_a, out_back, out_sum, total, send_b, keep_a, got_m
        )

        in_b = [swap_with(send_b[k], "h", k, groups) for k in range(1, groups)]
        keep_a, in_a = step(keep_a, in_a)
        sum_a = unstack(add_up(keep_a, in_a).astype(BF), 2, 0)
        back_3, back_2 = quad_swap(sum_a[0], 3), quad_swap(sum_a[1], 2)
        total = total + swap_with(total, "y", 1, 2)
        total = total + swap_with(total, "x", 1, 2)
        out_pieces = [part(out_sum, quad, 4, 1)] + [p.astype(F32) for p in out_back]
        dense_grad = in_order([p[:local] for p in out_pieces], 0)
        down_grad = in_order([p[local:] for p in out_pieces], 0)
        branch = own_order(branch_sum[0].astype(F32) + got_m.astype(F32), 1)
        hidden_out = (hidden + branch + b_dense + b_fc2).astype(BF)
        in_b, back_3, back_2, total, dense_grad, down_grad, terms_sum, send_b, hidden_out = step(
            in_b, back_3, back_2, total, dense_grad, down_grad, terms_sum, send_b, hidden_out
        )

        got_n = swap_with(terms_sum[1], "l", 1, 2)
        send_b, in_b = step(send_b, in_b)
        sum_b = unstack(add_up(send_b[0], in_b), 2, 0)
        back_1 = quad_swap(sum_b[0].astype(BF), 1)
        back_1, got_n, sum_b = step(back_1, got_n, sum_b)
        input_grad = norm_grad(group, groups, terms_sum[0], got_n, hidden_in, out_grad, ln_gain)
        qkv_grad, up_grad = settle(order, [sum_b[1], back_1, back_2, back_3], local)
        gain_grad, shift_grad, out_bias_grad = (
            total[:width], total[width : 2 * width], total[2 * width : 3 * width]
        )
        bias = lax.dynamic_slice(total, (3 * width + team * size,), (4 * size,)).reshape(4, size)
        up_bias_grad = bias[:, qkv_cols:].reshape(-1)
        qkv_bias_grad = jnp.stack(
            [bias[:, j * local : (j + 1) * local].reshape(-1) for j in range(3)]
        )
        return (
            hidden_out, input_grad, gain_grad, shift_grad, qkv_grad, qkv_bias_grad,
            dense_grad, out_bias_grad, up_grad, up_bias_grad, down_grad, out_bias_grad,
        )

    return body


def solution(mesh):
    groups = mesh.shape["fsdp"] // 4
    grid = Mesh(mesh.devices.reshape(groups, 2, 2, 2, 2), ("h", "l", "x", "y", "core"))
    rows, cols = ("h", "l", "x"), ("y", "core")
    tokens = rows + cols
    in_specs = (
        P(tokens, None), P(), P(), P(rows, None, cols), P(None, cols), P(cols, rows), P(),
        P(rows, cols), P(cols), P(cols, rows), P(), P(rows, None), P(tokens, None),
    )
    out_specs = (
        P(tokens, None), P(tokens, None), P(), P(), P(rows, None, cols), P(None, cols),
        P(cols, rows), P(), P(rows, cols), P(cols), P(cols, rows), P(),
    )
    return jax.shard_map(
        make_body(groups), mesh=grid, in_specs=in_specs, out_specs=out_specs, check_vma=False
    )
```

```python
import math

import jax
import jax.numpy as jnp
from jax import lax
from jax.experimental import pallas as pl
from jax.experimental.pallas import tpu as pltpu
from jax.sharding import Mesh
from jax.sharding import PartitionSpec as P

HEAD_DIM = 64
ROT = 32
EPS = 1e-05
BLOCK = 128
ROWS = 512
CHUNK = 512
REACH = 256
SCALE = 1.0 / math.sqrt(HEAD_DIM)

BF = jnp.bfloat16
F32 = jnp.float32


def layer_norm(values, norm_gain, norm_shift):
    centred = values - jnp.mean(values, axis=-1, keepdims=True)
    variance = jnp.mean(centred * centred, axis=-1, keepdims=True)
    return centred * lax.rsqrt(variance + EPS) * norm_gain + norm_shift


def gelu_tanh(values):
    return jax.nn.gelu(values, approximate=True)


def rotary_tables(length, lanes):
    lane = jnp.arange(lanes) % HEAD_DIM
    pair = lane % (ROT // 2)
    angles = jnp.arange(length).astype(F32)[:, None] * (
        10000.0 ** (-(2.0 * pair.astype(F32)) / ROT)
    )
    cosine = jnp.where(lane < ROT, jnp.cos(angles), 1.0)
    sine = jnp.sin(angles)
    first = jnp.where(lane < ROT // 2, -sine, 0.0)
    second = jnp.where((lane >= ROT // 2) & (lane < ROT), sine, 0.0)
    return cosine, first, second


def turn(values, cosine, first, second):
    half, lanes = ROT // 2, values.shape[1]
    return (
        values * cosine
        + pltpu.roll(values, lanes - half, 1) * first
        + pltpu.roll(values, half, 1) * second
    )


def nt(left, right):
    return lax.dot_general(left, right, (((1,), (1,)), ((), ())), preferred_element_type=F32)


def tn(left, right):
    return lax.dot_general(left, right, (((0,), (0,)), ((), ())), preferred_element_type=F32)


def windows(length):
    for start in range(0, length, BLOCK):
        low = max(0, (start - REACH + 1) // BLOCK * BLOCK)
        yield start, low, start + BLOCK


def allowed_mask(row_ref, col_ref, start, low, high):
    size = high - low
    key = low + lax.broadcasted_iota(jnp.int32, (size, BLOCK), 0)
    query = start + lax.broadcasted_iota(jnp.int32, (size, BLOCK), 1)
    same = col_ref[low:high, :] == row_ref[0, :, start : start + BLOCK]
    return same & (key <= query)


def head_lanes(rows, head, lanes):
    lane = lax.broadcasted_iota(jnp.int32, (rows, lanes), 1)
    return lane // HEAD_DIM == head


def attend_kernel(mixed_ref, cos_ref, a_ref, b_ref, row_ref, col_ref, qkv_ref, out_ref, lse_ref):
    length, lanes = out_ref.shape
    tables = cos_ref[...], a_ref[...], b_ref[...]
    query = turn(mixed_ref[:, :lanes], *tables).astype(BF)
    query = (query.astype(F32) * SCALE).astype(BF)
    key = turn(mixed_ref[:, lanes : 2 * lanes], *tables).astype(BF)
    value = mixed_ref[:, 2 * lanes :].astype(BF)
    qkv_ref[:, :lanes] = query
    qkv_ref[:, lanes : 2 * lanes] = key
    qkv_ref[:, 2 * lanes :] = value
    for start, low, high in windows(length):
        mask = allowed_mask(row_ref, col_ref, start, low, high)
        mine = query[start:high]
        out = jnp.zeros((BLOCK, lanes), F32)
        for head in range(lanes // HEAD_DIM):
            own = head_lanes(BLOCK, head, lanes)
            scores = nt(key[low:high], jnp.where(own, mine, jnp.zeros_like(mine)))
            scores = jnp.where(mask, scores, -1e30)
            highest = jnp.max(scores, axis=0, keepdims=True)
            shifted = jnp.exp(scores - highest)
            total = jnp.sum(shifted, axis=0, keepdims=True)
            attend = (shifted / total).astype(BF)
            out = jnp.where(own, tn(attend, value[low:high]), out)
            lse_ref[0, head : head + 1, start:high] = highest + jnp.log(total)
        out_ref[start:high, :] = out.astype(BF)


def attend_grad_kernel(
    qkv_ref, grad_ref, lse_ref, cos_ref, a_ref, b_ref, row_ref, col_ref, into_ref,
    out_ref, key_ref, value_ref,
):
    length, lanes = grad_ref.shape
    key_ref[...] = jnp.zeros_like(key_ref)
    value_ref[...] = jnp.zeros_like(value_ref)
    for start, low, high in windows(length):
        mask = allowed_mask(row_ref, col_ref, start, low, high)
        query = qkv_ref[start:high, :lanes]
        key = qkv_ref[low:high, lanes : 2 * lanes]
        value = qkv_ref[low:high, 2 * lanes :]
        grad = grad_ref[start:high, :]
        query_grad = jnp.zeros((BLOCK, lanes), F32)
        key_grad = jnp.zeros((high - low, lanes), F32)
        value_grad = jnp.zeros((high - low, lanes), F32)
        for head in range(lanes // HEAD_DIM):
            own = head_lanes(BLOCK, head, lanes)
            own_keys = head_lanes(high - low, head, lanes)
            none = jnp.zeros_like(query)
            scores = nt(key, jnp.where(own, query, none))
            scores = jnp.where(mask, scores, -1e30)
            attend = jnp.exp(scores - lse_ref[0, head : head + 1, start:high])
            attend_grad = nt(value, jnp.where(own, grad, none))
            inner = jnp.sum(attend * attend_grad, axis=0, keepdims=True)
            score_grad = (attend * (attend_grad - inner)).astype(BF)
            query_grad = jnp.where(own, tn(score_grad, key), query_grad)
            key_grad = jnp.where(
                own_keys, jnp.dot(score_grad, query, preferred_element_type=F32), key_grad
            )
            value_grad = jnp.where(
                own_keys,
                jnp.dot(attend.astype(BF), grad, preferred_element_type=F32),
                value_grad,
            )
        back = [ref[start:high, :] for ref in (cos_ref, a_ref, b_ref)]
        query_grad = turn(query_grad * SCALE, back[0], -back[1], -back[2])
        out_ref[start:high, :lanes] = query_grad.astype(BF)
        key_ref[low:high, :] += key_grad
        value_ref[low:high, :] += value_grad
    key_grad = turn(key_ref[...], cos_ref[...], -a_ref[...], -b_ref[...])
    out_ref[:, lanes : 2 * lanes] = key_grad.astype(BF)
    out_ref[:, 2 * lanes :] = value_ref[...].astype(BF)


def attention_specs(length, lanes):
    table = pl.BlockSpec((length, lanes), lambda s: (0, 0))
    return dict(
        table=table,
        wide=pl.BlockSpec((length, 3 * lanes), lambda s: (s, 0)),
        slim=pl.BlockSpec((length, lanes), lambda s: (s, 0)),
        lse=pl.BlockSpec((1, lanes // HEAD_DIM, length), lambda s: (s, 0, 0)),
        row=pl.BlockSpec((1, 1, length), lambda s: (s, 0, 0)),
        col=pl.BlockSpec((length, 1), lambda s: (s, 0)),
    )


def attention(mixed, lanes, tables, segments):
    sequences, length = segments.shape
    spec = attention_specs(length, lanes)
    rows = sequences * length
    return pl.pallas_call(
        attend_kernel,
        grid=(sequences,),
        in_specs=[spec["wide"]] + [spec["table"]] * 3 + [spec["row"], spec["col"]],
        out_specs=[spec["wide"], spec["slim"], spec["lse"]],
        out_shape=[
            jax.ShapeDtypeStruct((rows, 3 * lanes), BF),
            jax.ShapeDtypeStruct((rows, lanes), BF),
            jax.ShapeDtypeStruct((sequences, lanes // HEAD_DIM, length), F32),
        ],
        compiler_params=pltpu.CompilerParams(vmem_limit_bytes=32 << 20),
        name="attend",
    )(mixed, *tables, segments[:, None, :], segments.reshape(-1, 1))


def attention_grad(qkv, grad, lse, tables, segments, into):
    sequences, length = segments.shape
    rows, lanes = grad.shape
    spec = attention_specs(length, lanes)
    return pl.pallas_call(
        attend_grad_kernel,
        grid=(sequences,),
        in_specs=[spec["wide"], spec["slim"], spec["lse"]]
        + [spec["table"]] * 3
        + [spec["row"], spec["col"], pl.BlockSpec(memory_space=pl.ANY)],
        out_specs=spec["wide"],
        out_shape=jax.ShapeDtypeStruct(into.shape, BF),
        input_output_aliases={8: 0},
        scratch_shapes=[pltpu.VMEM((length, lanes), F32)] * 2,
        compiler_params=pltpu.CompilerParams(vmem_limit_bytes=32 << 20),
        name="attend_grad",
    )(qkv, grad, lse, *tables, segments[:, None, :], segments.reshape(-1, 1), into)


def gelu_slope(values):
    scale = math.sqrt(2.0 / math.pi)
    square = values * values
    bent = jnp.tanh(scale * (values + 0.044715 * values * square))
    return 0.5 * (1.0 + bent) + 0.5 * values * (1.0 - bent * bent) * scale * (
        1.0 + 3.0 * 0.044715 * square
    )


def branch_kernel(acts_ref, dense_ref, down_ref, out_ref):
    local, width = dense_ref.shape
    for low in range(0, width, CHUNK):
        cols = slice(low, low + CHUNK)
        total = jnp.dot(
            acts_ref[:, :local], dense_ref[:, cols], preferred_element_type=F32
        ) + jnp.dot(acts_ref[:, local:], down_ref[:, cols], preferred_element_type=F32)
        out_ref[:, cols] = total.astype(BF)


def back_kernel(grad_ref, dense_ref, down_ref, mixed_ref, context_ref, into_ref):
    units = down_ref.shape[0]
    first = mixed_ref.shape[1] - units
    grad = grad_ref[...]
    context_ref[...] = nt(grad, dense_ref[...]).astype(BF)
    activated_grad = nt(grad, down_ref[...])
    slope = gelu_slope(mixed_ref[:, first:])
    into_ref[:, :first] = jnp.zeros((into_ref.shape[0], first), BF)
    into_ref[:, first:] = (activated_grad * slope).astype(BF)


def norm_grad(group, groups, mine, got, hidden_in, out_grad, ln_gain):
    rows, width = hidden_in.shape
    span = width // groups

    def kernel(group_ref, mine_ref, got_ref, hidden_ref, cot_ref, gain_ref, out_ref, sum_ref):
        for j in range(groups):
            cols = pl.ds(pl.multiple_of((group_ref[0] ^ j) * span, span), span)
            sum_ref[:, j * span : (j + 1) * span] = mine_ref[:, cols].astype(F32) + got_ref[
                :, cols
            ].astype(F32)
        hidden = hidden_ref[...].astype(F32)
        centred = hidden - jnp.mean(hidden, axis=-1, keepdims=True)
        variance = jnp.mean(centred * centred, axis=-1, keepdims=True)
        scale = lax.rsqrt(variance + EPS)
        unit = centred * scale
        slope = sum_ref[...] * gain_ref[...]
        first = jnp.mean(slope, axis=-1, keepdims=True)
        second = jnp.mean(slope * unit, axis=-1, keepdims=True)
        out_ref[...] = scale * (slope - first - unit * second) + cot_ref[...].astype(F32)

    whole = pl.BlockSpec(memory_space=pltpu.VMEM)
    return pl.pallas_call(
        kernel,
        in_specs=[pl.BlockSpec(memory_space=pltpu.SMEM)] + [whole] * 5,
        out_specs=whole,
        out_shape=jax.ShapeDtypeStruct((rows, width), F32),
        scratch_shapes=[pltpu.VMEM((rows, width), F32)],
        compiler_params=pltpu.CompilerParams(vmem_limit_bytes=24 << 20),
        name="norm_grad",
    )(group[None], mine, got, hidden_in, out_grad, ln_gain[None, :])


def settle(order, pieces, local):
    rows, cols = pieces[0].shape
    units = cols - 3 * local

    def kernel(order_ref, *refs):
        ins, qkv_ref, up_ref = refs[:4], refs[4], refs[5]
        for m, ref in enumerate(ins):
            to = pl.multiple_of(order_ref[m] * units, units)
            up_ref[:, pl.ds(to, units)] = ref[:, 3 * local :].astype(F32)
            to = pl.multiple_of(order_ref[m] * local, local)
            for j in range(3):
                qkv_ref[j, :, pl.ds(to, local)] = ref[:, j * local : (j + 1) * local].astype(F32)

    whole = pl.BlockSpec(memory_space=pltpu.VMEM)
    qkv, up = pl.pallas_call(
        kernel,
        in_specs=[pl.BlockSpec(memory_space=pltpu.SMEM)] + [whole] * 4,
        out_specs=[whole] * 2,
        out_shape=[
            jax.ShapeDtypeStruct((3, rows, 4 * local), F32),
            jax.ShapeDtypeStruct((rows, 4 * units), F32),
        ],
        compiler_params=pltpu.CompilerParams(vmem_limit_bytes=24 << 20),
        name="settle",
    )(order, *pieces)
    return jnp.transpose(qkv, (1, 0, 2)), up


def by_tokens(kernel, name, rows, flops, blocked, whole, outs):
    def cut(cols):
        return pl.BlockSpec((ROWS, cols), lambda i: (i, 0))

    def kept(array):
        return pl.BlockSpec(array.shape, lambda i: (0, 0))

    specs = [cut(a.shape[1]) if a.shape[0] == rows and cutting else kept(a)
             for a, cutting in [(a, True) for a in blocked] + [(a, False) for a in whole]]
    size = sum(a.size * a.dtype.itemsize for a in list(blocked) + list(whole))
    return pl.pallas_call(
        kernel,
        grid=(rows // ROWS,),
        in_specs=specs,
        out_specs=[cut(cols) for cols in outs],
        out_shape=[jax.ShapeDtypeStruct((rows, cols), BF) for cols in outs],
        compiler_params=pltpu.CompilerParams(vmem_limit_bytes=48 << 20),
        cost_estimate=pl.CostEstimate(
            flops=flops, bytes_accessed=size + 2 * rows * sum(outs), transcendentals=0
        ),
        name=name,
    )(*blocked, *whole)


def place(order, sources, count, axis, shape):
    arrays = []
    for array, _, _, _ in sources:
        if not any(array is seen for seen in arrays):
            arrays.append(array)
    where = [[array is seen for seen in arrays].index(True) for array, _, _, _ in sources]
    size = shape[axis] // count

    def kernel(order_ref, *refs):
        ins, out = refs[: len(arrays)], refs[-1]
        for i, (_, (rows, cols), slot, entry) in enumerate(sources):
            to = pl.multiple_of((slot * 4 + order_ref[entry]) * size, size)
            if axis == 0:
                out[pl.ds(to, size), :] = ins[where[i]][rows : rows + size, cols : cols + shape[1]]
            else:
                out[:, pl.ds(to, size)] = ins[where[i]][rows : rows + shape[0], cols : cols + size]

    if axis == 1 and size % 128:
        result = jnp.zeros(shape, arrays[0].dtype)
        for array, (rows, cols), slot, entry in sources:
            piece = lax.slice(array, (rows, cols), (rows + shape[0], cols + size))
            to = (slot * 4 + order[entry]) * size
            result = lax.dynamic_update_slice_in_dim(result, piece, to, 1)
        return result

    whole = pl.BlockSpec(memory_space=pltpu.VMEM)
    return pl.pallas_call(
        kernel,
        in_specs=[pl.BlockSpec(memory_space=pltpu.SMEM)] + [whole] * len(arrays),
        out_specs=whole,
        out_shape=jax.ShapeDtypeStruct(shape, arrays[0].dtype),
        compiler_params=pltpu.CompilerParams(vmem_limit_bytes=24 << 20),
        name="place",
    )(order, *arrays)


def swap_with(values, axis, mask, size):
    return lax.ppermute(values, axis, [(i, i ^ mask) for i in range(size)])


def dot(left, right, dims):
    return lax.dot_general(left, right, (dims, ((), ())), preferred_element_type=F32)


def after(values, *earlier):
    return lax.optimization_barrier((values,) + earlier)[0]


def step(*values):
    return lax.optimization_barrier(values)


TEAM = ("l", "x", "y", "core")


def make_body(groups):
    def body(
        hidden_in, ln_gain, ln_bias, w_qkv, b_qkv, w_dense, b_dense,
        w_fc1, b_fc1, w_fc2, b_fc2, segment_ids, out_grad,
    ):
        group, lb, xb = lax.axis_index("h"), lax.axis_index("l"), lax.axis_index("x")
        quad = 2 * lb + xb
        tile, width = hidden_in.shape
        span = width // groups

        def part(values, which, count, axis):
            size = values.shape[axis] // count
            return lax.dynamic_slice_in_dim(values, which * size, size, axis)

        def fixed(values, which, count, axis):
            size = values.shape[axis] // count
            return lax.slice_in_dim(values, which * size, (which + 1) * size, axis=axis)

        def own_order(values, axis):
            bit = 1
            while bit < groups:
                blocks = [fixed(values, j ^ bit, groups, axis) for j in range(groups)]
                flipped = jnp.concatenate(blocks, axis=axis)
                values = jnp.where((group // bit) % 2 == 1, flipped, values)
                bit *= 2
            return values

        def trade(give, own):
            return [own] + [swap_with(give(quad ^ m), ("l", "x"), m, 4) for m in (1, 2, 3)]

        def in_order(parts, axis):
            blocks = [
                jnp.where(
                    lb == 1,
                    jnp.where(xb == 1, parts[j ^ 3], parts[j ^ 2]),
                    jnp.where(xb == 1, parts[j ^ 1], parts[j]),
                )
                for j in range(4)
            ]
            return jnp.concatenate(blocks, axis=axis)

        def swap_h(values):
            return [swap_with(values, "h", k, groups) for k in range(1, groups)]

        def fold_start(rows, axis, name):
            sent = lax.dynamic_index_in_dim(rows, 1 - lax.axis_index(name), axis, keepdims=False)
            return swap_with(sent, name, 1, 2)

        def fold_end(rows, got, axis, name):
            mine = lax.dynamic_index_in_dim(rows, lax.axis_index(name), axis, keepdims=False)
            return mine.astype(F32) + got.astype(F32)

        def halves(rows):
            return rows[..., : width // 2], rows[..., width // 2 :]

        def swap_c(values):
            return swap_with(values, "core", 1, 2)

        def quad_swap(values, m):
            return swap_with(values, ("l", "x"), m, 4)

        seg_len = segment_ids.shape[1]
        in_cols = 3 * w_qkv.shape[2] // 4 + w_fc1.shape[1] // 4
        labels = jnp.pad(segment_ids.astype(BF), ((0, 15), (0, in_cols - seg_len)))

        def take_in(which):
            piece = part(w_qkv, which, 4, 2)
            rows = jnp.concatenate(
                [piece[:, j] for j in range(3)] + [part(w_fc1, which, 4, 1)], axis=1
            )
            return jnp.concatenate([rows, labels], axis=0)

        def take_out(which):
            return jnp.concatenate([part(w_dense, which, 4, 0), part(w_fc2, which, 4, 0)], axis=0)

        def stacked(parts, axis):
            return jnp.concatenate(parts, axis=axis)

        def unstack(values, count, axis):
            return [fixed(values, m, count, axis) for m in range(count)]

        local = w_dense.shape[0] // 4
        qkv_cols = 3 * local

        order = jnp.stack([quad, quad ^ 1, quad ^ 2, quad ^ 3])
        rows_in, cols_out = w_fc1.shape[0], w_fc2.shape[1]

        def gather_tokens(mine, other):
            rows = lax.all_gather(
                jnp.stack([mine, other]), ("x", "y", "core"), axis=1, tiled=True
            )
            return rows.reshape(-1, width)

        hidden = hidden_in.astype(F32)
        mine_n = own_order(layer_norm(hidden, ln_gain, ln_bias).astype(BF), 1)
        mine_g = own_order(out_grad, 1)
        in_own = take_in(quad)
        in_first = swap_h(in_own[:rows_in])
        next_n = swap_with(mine_n, "l", 1, 2)
        in_send = [take_in(quad ^ m) for m in (1, 2, 3)]
        mine_n, next_n, in_first, in_send, mine_g = step(
            mine_n, next_n, in_first, in_send, mine_g
        )
        normed_all = gather_tokens(mine_n, next_n)
        in_parts = [in_own] + [quad_swap(piece, m) for m, piece in zip((1, 2, 3), in_send)]
        out_own = take_out(quad)
        out_first = swap_h(out_own)
        out_send = [take_out(quad ^ m) for m in (1, 2, 3)]
        in_parts, mine_g, out_own, out_first, out_send = step(
            in_parts, mine_g, out_own, out_first, out_send
        )

        in_low = swap_h(in_parts[1][:rows_in])
        next_g = swap_with(mine_g, "l", 1, 2)
        out_1 = quad_swap(out_send[0], 1)
        in_high = stacked([p[:rows_in] for p in in_parts[2:]], 0)
        in_low, next_g, out_1, in_high, out_send, mine_g = step(
            in_low, next_g, out_1, in_high, out_send, mine_g
        )
        in_rest = swap_h(in_high)
        out_parts = [out_own, out_1] + [quad_swap(out_send[m - 1], m) for m in (2, 3)]
        grad_all = gather_tokens(mine_g, next_g)
        out_stack = stacked(out_parts[1:], 1)
        in_rest, out_parts, out_stack = step(in_rest, out_parts, out_stack)

        out_rest = swap_h(out_stack)
        in_first, in_parts, in_low, in_rest = step(in_first, in_parts, in_low, in_rest)
        sources = [(p, (0, 0), 0, m) for m, p in enumerate(in_parts)]
        for k in range(1, groups):
            sources.append((in_first[k - 1], (0, 0), k, 0))
            sources.append((in_low[k - 1], (0, 0), k, 1))
            sources += [(in_rest[k - 1], ((m - 2) * rows_in, 0), k, m) for m in (2, 3)]
        in_w = place(order, sources, 4 * groups, 0, (width, in_cols))
        labels_all = [p[rows_in, :seg_len].astype(jnp.int32)[None] for p in in_parts]
        ordered = in_order(labels_all, 0)
        segments = jnp.where(lb == 1, jnp.roll(ordered, 2, axis=0), ordered)
        in_b = stacked([part(b_qkv, quad, 4, 1).reshape(-1), part(b_fc1, quad, 4, 0)], 0)
        mixed = dot(normed_all, in_w, ((1,), (0,))) + in_b
        tables = rotary_tables(segments.shape[1], local)
        qkv, context, lse = attention(mixed, local, tables, segments)
        before = mixed[:, qkv_cols:]
        acts = stacked([context, gelu_tanh(before).astype(BF)], 1)
        qkv, acts, lse, mixed = step(qkv, acts, lse, mixed)

        def slot(values, k, axis):
            return fixed(values, k, groups, axis)

        out_rows = acts.shape[1]
        out_part = dot(acts, grad_all, ((0,), (0,))).astype(BF)
        cuts = [out_rows * i // 40 for i in (0, 6, 27, 40)]
        out_send = [
            [slot(out_part, k, 1)[cuts[i] : cuts[i + 1]] for i in range(3)] for k in range(groups)
        ]
        out_send, out_rest = step(out_send, out_rest)
        out_ws = []
        for low, high in ((0, local), (local, out_rows)):
            sources = [(p, (low, 0), 0, m) for m, p in enumerate(out_parts)]
            for k in range(1, groups):
                sources.append((out_first[k - 1], (low, 0), k, 0))
                sources += [(out_rest[k - 1], (low, (m - 1) * cols_out), k, m) for m in (1, 2, 3)]
            out_ws.append(place(order, sources, 4 * groups, 1, (high - low, width)))

        def send_out(i):
            return [swap_with(out_send[k][i], "h", k, groups) for k in range(1, groups)]

        def team_sum(values):
            return lax.psum_scatter(
                values.reshape(2, -1, width), ("x", "y", "core"), scatter_dimension=1, tiled=True
            )

        out_0 = send_out(0)
        acts, out_ws = step(acts, out_ws)
        tokens = acts.shape[0]
        (branch,) = by_tokens(
            branch_kernel, "branch", tokens, 2 * tokens * out_rows * width, [acts], out_ws, [width]
        )
        branch, out_ws, out_0, out_send = step(branch, out_ws, out_0, out_send)
        branch_sum = team_sum(branch)
        out_1 = send_out(1)
        out_ws, qkv, lse, mixed = step(out_ws, qkv, lse, mixed)

        def back(grad_ref, mixed_ref, dense_ref, down_ref, context_ref, into_ref):
            back_kernel(grad_ref, dense_ref, down_ref, mixed_ref, context_ref, into_ref)

        context_grad, into = by_tokens(
            back, "back", tokens, 2 * tokens * out_rows * width, [grad_all, mixed], out_ws,
            [local, in_cols],
        )
        into = attention_grad(qkv, context_grad, lse, tables, segments, into)
        into, out_1, out_send = step(into, out_1, out_send)

        def add_up(mine, others):
            mine = mine.astype(F32)
            for piece in others:
                mine = mine + piece.astype(F32)
            return mine

        def out_total(pieces, got):
            total = stacked([add_up(out_send[0][i], g) for i, g in zip(pieces, got)], 0)
            sent = total.astype(BF)
            return part(total, quad, 4, 1), [part(sent, quad ^ m, 4, 1) for m in (1, 2, 3)]

        out_2 = send_out(2)
        low_kept, low_send = out_total((0, 1), (out_0, out_1))
        low_kept, low_send = step(low_kept, low_send)
        low_back = [quad_swap(piece, m) for m, piece in zip((1, 2, 3), low_send)]
        into, normed_all = step(into, normed_all)
        in_part = dot(normed_all, into, ((0,), (0,))).astype(BF)
        in_part, into, out_2, low_back, low_kept = step(in_part, into, out_2, low_back, low_kept)

        def block(k, m):
            start = k * span + (quad ^ m) * (span // 4)
            return lax.dynamic_slice_in_dim(in_part, start, span // 4, 0)

        def swap_block(m):
            return [swap_with(in_send[m][k], "h", k, groups) for k in range(1, groups)]

        high_kept, high_send = out_total((2,), (out_2,))
        in_send = [[block(k, m) for k in range(groups)] for m in range(4)]
        in_send, high_send, high_kept = step(in_send, high_send, high_kept)

        in_3 = swap_block(3)
        high_back = [quad_swap(piece, m) for m, piece in zip((1, 2, 3), high_send)]
        into, in_w, normed_all = step(into, in_w, normed_all)
        terms = dot(into, in_w, ((1,), (1,)))
        unit = (normed_all.astype(F32) - own_order(ln_bias, 0)) / own_order(ln_gain, 0)
        gain_sum, shift_sum = jnp.sum(terms * unit, axis=0), jnp.sum(terms, axis=0)
        terms = terms.astype(BF)
        terms, gain_sum, shift_sum, in_3, in_send, high_back = step(
            terms, gain_sum, shift_sum, in_3, in_send, high_back
        )
        terms_sum = team_sum(terms)
        branch_own, branch_next = branch_sum[0], branch_sum[1]

        in_2, in_1 = swap_block(2), swap_block(1)
        in_send[3], in_3 = step(in_send[3], in_3)
        back_3 = quad_swap(add_up(in_send[3][0], in_3).astype(BF), 3)
        got_m = swap_with(branch_next, "l", 1, 2)
        small = [
            own_order(gain_sum, 0),
            own_order(shift_sum, 0),
            jnp.sum(out_grad.astype(F32), axis=0),
        ]
        bias = jnp.sum(into, axis=0, dtype=F32)
        size = in_cols
        team = 4 * (2 * lax.axis_index("y") + lax.axis_index("core"))
        bias = lax.dynamic_update_slice(jnp.zeros((16 * size,), F32), bias, ((team + quad) * size,))
        total = stacked(small + [bias], 0)
        total = total + swap_c(total)
        total = total + swap_with(total, "y", 1, 2)
        in_2, in_1, back_3, got_m, total, in_send = step(
            in_2, in_1, back_3, got_m, total, in_send
        )

        in_0 = swap_block(0)
        in_1, in_2 = step(in_1, in_2)
        back_1 = quad_swap(add_up(in_send[1][0], in_1).astype(BF), 1)
        back_2 = quad_swap(add_up(in_send[2][0], in_2).astype(BF), 2)
        total = total + swap_with(total, "x", 1, 2)
        total = total + swap_with(total, "l", 1, 2)
        out_pieces = [stacked([low_kept, high_kept], 0)] + [
            stacked([low, high], 0).astype(F32) for low, high in zip(low_back, high_back)
        ]
        dense_grad = in_order([p[:local] for p in out_pieces], 0)
        down_grad = in_order([p[local:] for p in out_pieces], 0)
        branch = own_order(branch_own.astype(F32) + got_m.astype(F32), 1)
        hidden_out = (hidden + branch + b_dense + b_fc2).astype(BF)
        own_in = add_up(in_send[0][0], in_0)
        own_in, back_1, back_2, total, dense_grad, down_grad, hidden_out = step(
            own_in, back_1, back_2, total, dense_grad, down_grad, hidden_out
        )

        bit = 1
        while bit < groups:
            total = total + swap_with(total, "h", bit, groups)
            bit *= 2
        got_n = swap_with(terms_sum[1], "l", 1, 2)
        input_grad = norm_grad(group, groups, terms_sum[0], got_n, hidden_in, out_grad, ln_gain)
        qkv_grad, up_grad = settle(order, [own_in, back_1, back_2, back_3], local)
        gain_grad, shift_grad, out_bias_grad = (
            total[:width], total[width : 2 * width], total[2 * width : 3 * width]
        )
        bias = lax.dynamic_slice(total, (3 * width + team * size,), (4 * size,)).reshape(4, size)
        up_bias_grad = bias[:, qkv_cols:].reshape(-1)
        qkv_bias_grad = jnp.stack(
            [bias[:, j * local : (j + 1) * local].reshape(-1) for j in range(3)]
        )
        return (
            hidden_out, input_grad, gain_grad, shift_grad, qkv_grad, qkv_bias_grad,
            dense_grad, out_bias_grad, up_grad, up_bias_grad, down_grad, out_bias_grad,
        )

    return body


def solution(mesh):
    groups = mesh.shape["fsdp"] // 4
    grid = Mesh(mesh.devices.reshape(groups, 2, 2, 2, 2), ("h", "l", "x", "y", "core"))
    rows, cols = ("h", "l", "x"), ("y", "core")
    tokens = rows + cols
    in_specs = (
        P(tokens, None), P(), P(), P(rows, None, cols), P(None, cols), P(cols, rows), P(),
        P(rows, cols), P(cols), P(cols, rows), P(), P(rows, None), P(tokens, None),
    )
    out_specs = (
        P(tokens, None), P(tokens, None), P(), P(), P(rows, None, cols), P(None, cols),
        P(cols, rows), P(), P(rows, cols), P(cols), P(cols, rows), P(),
    )
    return jax.shard_map(
        make_body(groups), mesh=grid, in_specs=in_specs, out_specs=out_specs, check_vma=False
    )
```

```python
import math

import jax
import jax.numpy as jnp
from jax import lax
from jax.experimental import pallas as pl
from jax.experimental.pallas import tpu as pltpu
from jax.sharding import Mesh
from jax.sharding import PartitionSpec as P

HEAD_DIM = 64
ROT = 32
EPS = 1e-05
BLOCK = 128
ROWS = 512
CHUNK = 512
REACH = 256
SCALE = 1.0 / math.sqrt(HEAD_DIM)

BF = jnp.bfloat16
F32 = jnp.float32


def layer_norm(values, norm_gain, norm_shift):
    centred = values - jnp.mean(values, axis=-1, keepdims=True)
    variance = jnp.mean(centred * centred, axis=-1, keepdims=True)
    return centred * lax.rsqrt(variance + EPS) * norm_gain + norm_shift


def gelu_tanh(values):
    return jax.nn.gelu(values, approximate=True)


def rotary_tables(length, lanes):
    lane = jnp.arange(lanes) % HEAD_DIM
    pair = lane % (ROT // 2)
    angles = jnp.arange(length).astype(F32)[:, None] * (
        10000.0 ** (-(2.0 * pair.astype(F32)) / ROT)
    )
    cosine = jnp.where(lane < ROT, jnp.cos(angles), 1.0)
    sine = jnp.sin(angles)
    first = jnp.where(lane < ROT // 2, -sine, 0.0)
    second = jnp.where((lane >= ROT // 2) & (lane < ROT), sine, 0.0)
    return cosine, first, second


def turn(values, cosine, first, second):
    half, lanes = ROT // 2, values.shape[1]
    return (
        values * cosine
        + pltpu.roll(values, lanes - half, 1) * first
        + pltpu.roll(values, half, 1) * second
    )


def nt(left, right):
    return lax.dot_general(left, right, (((1,), (1,)), ((), ())), preferred_element_type=F32)


def tn(left, right):
    return lax.dot_general(left, right, (((0,), (0,)), ((), ())), preferred_element_type=F32)


def windows(length):
    for start in range(0, length, BLOCK):
        low = max(0, (start - REACH + 1) // BLOCK * BLOCK)
        yield start, low, start + BLOCK


def allowed_mask(row_ref, col_ref, start, low, high):
    size = high - low
    key = low + lax.broadcasted_iota(jnp.int32, (size, BLOCK), 0)
    query = start + lax.broadcasted_iota(jnp.int32, (size, BLOCK), 1)
    same = col_ref[low:high, :] == row_ref[0, :, start : start + BLOCK]
    return same & (key <= query)


def head_lanes(rows, head, lanes):
    lane = lax.broadcasted_iota(jnp.int32, (rows, lanes), 1)
    return lane // HEAD_DIM == head


def attend_kernel(mixed_ref, cos_ref, a_ref, b_ref, row_ref, col_ref, qkv_ref, out_ref, lse_ref):
    length, lanes = out_ref.shape
    tables = cos_ref[...], a_ref[...], b_ref[...]
    query = turn(mixed_ref[:, :lanes], *tables).astype(BF)
    query = (query.astype(F32) * SCALE).astype(BF)
    key = turn(mixed_ref[:, lanes : 2 * lanes], *tables).astype(BF)
    value = mixed_ref[:, 2 * lanes :].astype(BF)
    qkv_ref[:, :lanes] = query
    qkv_ref[:, lanes : 2 * lanes] = key
    qkv_ref[:, 2 * lanes :] = value
    for start, low, high in windows(length):
        mask = allowed_mask(row_ref, col_ref, start, low, high)
        mine = query[start:high]
        out = jnp.zeros((BLOCK, lanes), F32)
        for head in range(lanes // HEAD_DIM):
            own = head_lanes(BLOCK, head, lanes)
            scores = nt(key[low:high], jnp.where(own, mine, jnp.zeros_like(mine)))
            scores = jnp.where(mask, scores, -1e30)
            highest = jnp.max(scores, axis=0, keepdims=True)
            shifted = jnp.exp(scores - highest)
            total = jnp.sum(shifted, axis=0, keepdims=True)
            attend = (shifted / total).astype(BF)
            out = jnp.where(own, tn(attend, value[low:high]), out)
            lse_ref[0, head : head + 1, start:high] = highest + jnp.log(total)
        out_ref[start:high, :] = out.astype(BF)


def attend_grad_kernel(
    qkv_ref, grad_ref, lse_ref, cos_ref, a_ref, b_ref, row_ref, col_ref, into_ref,
    out_ref, key_ref, value_ref,
):
    length, lanes = grad_ref.shape
    key_ref[...] = jnp.zeros_like(key_ref)
    value_ref[...] = jnp.zeros_like(value_ref)
    for start, low, high in windows(length):
        mask = allowed_mask(row_ref, col_ref, start, low, high)
        query = qkv_ref[start:high, :lanes]
        key = qkv_ref[low:high, lanes : 2 * lanes]
        value = qkv_ref[low:high, 2 * lanes :]
        grad = grad_ref[start:high, :]
        query_grad = jnp.zeros((BLOCK, lanes), F32)
        key_grad = jnp.zeros((high - low, lanes), F32)
        value_grad = jnp.zeros((high - low, lanes), F32)
        for head in range(lanes // HEAD_DIM):
            own = head_lanes(BLOCK, head, lanes)
            own_keys = head_lanes(high - low, head, lanes)
            none = jnp.zeros_like(query)
            scores = nt(key, jnp.where(own, query, none))
            scores = jnp.where(mask, scores, -1e30)
            attend = jnp.exp(scores - lse_ref[0, head : head + 1, start:high])
            attend_grad = nt(value, jnp.where(own, grad, none))
            inner = jnp.sum(attend * attend_grad, axis=0, keepdims=True)
            score_grad = (attend * (attend_grad - inner)).astype(BF)
            query_grad = jnp.where(own, tn(score_grad, key), query_grad)
            key_grad = jnp.where(
                own_keys, jnp.dot(score_grad, query, preferred_element_type=F32), key_grad
            )
            value_grad = jnp.where(
                own_keys,
                jnp.dot(attend.astype(BF), grad, preferred_element_type=F32),
                value_grad,
            )
        back = [ref[start:high, :] for ref in (cos_ref, a_ref, b_ref)]
        query_grad = turn(query_grad * SCALE, back[0], -back[1], -back[2])
        out_ref[start:high, :lanes] = query_grad.astype(BF)
        key_ref[low:high, :] += key_grad
        value_ref[low:high, :] += value_grad
    key_grad = turn(key_ref[...], cos_ref[...], -a_ref[...], -b_ref[...])
    out_ref[:, lanes : 2 * lanes] = key_grad.astype(BF)
    out_ref[:, 2 * lanes :] = value_ref[...].astype(BF)


def attention_specs(length, lanes):
    table = pl.BlockSpec((length, lanes), lambda s: (0, 0))
    return dict(
        table=table,
        wide=pl.BlockSpec((length, 3 * lanes), lambda s: (s, 0)),
        slim=pl.BlockSpec((length, lanes), lambda s: (s, 0)),
        lse=pl.BlockSpec((1, lanes // HEAD_DIM, length), lambda s: (s, 0, 0)),
        row=pl.BlockSpec((1, 1, length), lambda s: (s, 0, 0)),
        col=pl.BlockSpec((length, 1), lambda s: (s, 0)),
    )


def attention(mixed, lanes, tables, segments):
    sequences, length = segments.shape
    spec = attention_specs(length, lanes)
    rows = sequences * length
    return pl.pallas_call(
        attend_kernel,
        grid=(sequences,),
        in_specs=[spec["wide"]] + [spec["table"]] * 3 + [spec["row"], spec["col"]],
        out_specs=[spec["wide"], spec["slim"], spec["lse"]],
        out_shape=[
            jax.ShapeDtypeStruct((rows, 3 * lanes), BF),
            jax.ShapeDtypeStruct((rows, lanes), BF),
            jax.ShapeDtypeStruct((sequences, lanes // HEAD_DIM, length), F32),
        ],
        compiler_params=pltpu.CompilerParams(vmem_limit_bytes=32 << 20),
        name="attend",
    )(mixed, *tables, segments[:, None, :], segments.reshape(-1, 1))


def attention_grad(qkv, grad, lse, tables, segments, into):
    sequences, length = segments.shape
    rows, lanes = grad.shape
    spec = attention_specs(length, lanes)
    return pl.pallas_call(
        attend_grad_kernel,
        grid=(sequences,),
        in_specs=[spec["wide"], spec["slim"], spec["lse"]]
        + [spec["table"]] * 3
        + [spec["row"], spec["col"], pl.BlockSpec(memory_space=pl.ANY)],
        out_specs=spec["wide"],
        out_shape=jax.ShapeDtypeStruct(into.shape, BF),
        input_output_aliases={8: 0},
        scratch_shapes=[pltpu.VMEM((length, lanes), F32)] * 2,
        compiler_params=pltpu.CompilerParams(vmem_limit_bytes=32 << 20),
        name="attend_grad",
    )(qkv, grad, lse, *tables, segments[:, None, :], segments.reshape(-1, 1), into)


def gelu_slope(values):
    scale = math.sqrt(2.0 / math.pi)
    square = values * values
    bent = jnp.tanh(scale * (values + 0.044715 * values * square))
    return 0.5 * (1.0 + bent) + 0.5 * values * (1.0 - bent * bent) * scale * (
        1.0 + 3.0 * 0.044715 * square
    )


def branch_kernel(acts_ref, dense_ref, down_ref, out_ref):
    local, width = dense_ref.shape
    for low in range(0, width, CHUNK):
        cols = slice(low, low + CHUNK)
        total = jnp.dot(
            acts_ref[:, :local], dense_ref[:, cols], preferred_element_type=F32
        ) + jnp.dot(acts_ref[:, local:], down_ref[:, cols], preferred_element_type=F32)
        out_ref[:, cols] = total.astype(BF)


def back_kernel(grad_ref, dense_ref, down_ref, mixed_ref, context_ref, into_ref):
    units = down_ref.shape[0]
    first = mixed_ref.shape[1] - units
    grad = grad_ref[...]
    context_ref[...] = nt(grad, dense_ref[...]).astype(BF)
    activated_grad = nt(grad, down_ref[...])
    slope = gelu_slope(mixed_ref[:, first:])
    into_ref[:, :first] = jnp.zeros((into_ref.shape[0], first), BF)
    into_ref[:, first:] = (activated_grad * slope).astype(BF)


def norm_grad(group, groups, mine, got, hidden_in, out_grad, ln_gain):
    rows, width = hidden_in.shape
    span = width // groups

    def kernel(group_ref, mine_ref, got_ref, hidden_ref, cot_ref, gain_ref, out_ref, sum_ref):
        for j in range(groups):
            cols = pl.ds(pl.multiple_of((group_ref[0] ^ j) * span, span), span)
            sum_ref[:, j * span : (j + 1) * span] = mine_ref[:, cols].astype(F32) + got_ref[
                :, cols
            ].astype(F32)
        hidden = hidden_ref[...].astype(F32)
        centred = hidden - jnp.mean(hidden, axis=-1, keepdims=True)
        variance = jnp.mean(centred * centred, axis=-1, keepdims=True)
        scale = lax.rsqrt(variance + EPS)
        unit = centred * scale
        slope = sum_ref[...] * gain_ref[...]
        first = jnp.mean(slope, axis=-1, keepdims=True)
        second = jnp.mean(slope * unit, axis=-1, keepdims=True)
        out_ref[...] = scale * (slope - first - unit * second) + cot_ref[...].astype(F32)

    whole = pl.BlockSpec(memory_space=pltpu.VMEM)
    return pl.pallas_call(
        kernel,
        in_specs=[pl.BlockSpec(memory_space=pltpu.SMEM)] + [whole] * 5,
        out_specs=whole,
        out_shape=jax.ShapeDtypeStruct((rows, width), F32),
        scratch_shapes=[pltpu.VMEM((rows, width), F32)],
        compiler_params=pltpu.CompilerParams(vmem_limit_bytes=24 << 20),
        name="norm_grad",
    )(group[None], mine, got, hidden_in, out_grad, ln_gain[None, :])


def settle(order, pieces, local):
    rows, cols = pieces[0].shape
    units = cols - 3 * local

    def kernel(order_ref, *refs):
        ins, qkv_ref, up_ref = refs[:4], refs[4], refs[5]
        for m, ref in enumerate(ins):
            to = pl.multiple_of(order_ref[m] * units, units)
            up_ref[:, pl.ds(to, units)] = ref[:, 3 * local :].astype(F32)
            to = pl.multiple_of(order_ref[m] * local, local)
            for j in range(3):
                qkv_ref[j, :, pl.ds(to, local)] = ref[:, j * local : (j + 1) * local].astype(F32)

    whole = pl.BlockSpec(memory_space=pltpu.VMEM)
    qkv, up = pl.pallas_call(
        kernel,
        in_specs=[pl.BlockSpec(memory_space=pltpu.SMEM)] + [whole] * 4,
        out_specs=[whole] * 2,
        out_shape=[
            jax.ShapeDtypeStruct((3, rows, 4 * local), F32),
            jax.ShapeDtypeStruct((rows, 4 * units), F32),
        ],
        compiler_params=pltpu.CompilerParams(vmem_limit_bytes=24 << 20),
        name="settle",
    )(order, *pieces)
    return jnp.transpose(qkv, (1, 0, 2)), up


def by_tokens(kernel, name, rows, flops, blocked, whole, outs):
    def cut(cols):
        return pl.BlockSpec((ROWS, cols), lambda i: (i, 0))

    def kept(array):
        return pl.BlockSpec(array.shape, lambda i: (0, 0))

    specs = [cut(a.shape[1]) if a.shape[0] == rows and cutting else kept(a)
             for a, cutting in [(a, True) for a in blocked] + [(a, False) for a in whole]]
    size = sum(a.size * a.dtype.itemsize for a in list(blocked) + list(whole))
    return pl.pallas_call(
        kernel,
        grid=(rows // ROWS,),
        in_specs=specs,
        out_specs=[cut(cols) for cols in outs],
        out_shape=[jax.ShapeDtypeStruct((rows, cols), BF) for cols in outs],
        compiler_params=pltpu.CompilerParams(vmem_limit_bytes=48 << 20),
        cost_estimate=pl.CostEstimate(
            flops=flops, bytes_accessed=size + 2 * rows * sum(outs), transcendentals=0
        ),
        name=name,
    )(*blocked, *whole)


def place(order, sources, count, axis, shape):
    arrays = []
    for array, _, _, _ in sources:
        if not any(array is seen for seen in arrays):
            arrays.append(array)
    where = [[array is seen for seen in arrays].index(True) for array, _, _, _ in sources]
    size = shape[axis] // count

    def kernel(order_ref, *refs):
        ins, out = refs[: len(arrays)], refs[-1]
        for i, (_, (rows, cols), slot, entry) in enumerate(sources):
            to = pl.multiple_of((slot * 4 + order_ref[entry]) * size, size)
            if axis == 0:
                out[pl.ds(to, size), :] = ins[where[i]][rows : rows + size, cols : cols + shape[1]]
            else:
                out[:, pl.ds(to, size)] = ins[where[i]][rows : rows + shape[0], cols : cols + size]

    if axis == 1 and size % 128:
        result = jnp.zeros(shape, arrays[0].dtype)
        for array, (rows, cols), slot, entry in sources:
            piece = lax.slice(array, (rows, cols), (rows + shape[0], cols + size))
            to = (slot * 4 + order[entry]) * size
            result = lax.dynamic_update_slice_in_dim(result, piece, to, 1)
        return result

    whole = pl.BlockSpec(memory_space=pltpu.VMEM)
    return pl.pallas_call(
        kernel,
        in_specs=[pl.BlockSpec(memory_space=pltpu.SMEM)] + [whole] * len(arrays),
        out_specs=whole,
        out_shape=jax.ShapeDtypeStruct(shape, arrays[0].dtype),
        compiler_params=pltpu.CompilerParams(vmem_limit_bytes=24 << 20),
        name="place",
    )(order, *arrays)


def swap_with(values, axis, mask, size):
    return lax.ppermute(values, axis, [(i, i ^ mask) for i in range(size)])


def dot(left, right, dims):
    return lax.dot_general(left, right, (dims, ((), ())), preferred_element_type=F32)


def after(values, *earlier):
    return lax.optimization_barrier((values,) + earlier)[0]


def step(*values):
    return lax.optimization_barrier(values)


TEAM = ("l", "x", "y", "core")


def make_body(groups):
    def body(
        hidden_in, ln_gain, ln_bias, w_qkv, b_qkv, w_dense, b_dense,
        w_fc1, b_fc1, w_fc2, b_fc2, segment_ids, out_grad,
    ):
        group, lb, xb = lax.axis_index("h"), lax.axis_index("l"), lax.axis_index("x")
        quad = 2 * lb + xb
        tile, width = hidden_in.shape
        span = width // groups

        def part(values, which, count, axis):
            size = values.shape[axis] // count
            return lax.dynamic_slice_in_dim(values, which * size, size, axis)

        def fixed(values, which, count, axis):
            size = values.shape[axis] // count
            return lax.slice_in_dim(values, which * size, (which + 1) * size, axis=axis)

        def own_order(values, axis):
            bit = 1
            while bit < groups:
                blocks = [fixed(values, j ^ bit, groups, axis) for j in range(groups)]
                flipped = jnp.concatenate(blocks, axis=axis)
                values = jnp.where((group // bit) % 2 == 1, flipped, values)
                bit *= 2
            return values

        def trade(give, own):
            return [own] + [swap_with(give(quad ^ m), ("l", "x"), m, 4) for m in (1, 2, 3)]

        def in_order(parts, axis):
            blocks = [
                jnp.where(
                    lb == 1,
                    jnp.where(xb == 1, parts[j ^ 3], parts[j ^ 2]),
                    jnp.where(xb == 1, parts[j ^ 1], parts[j]),
                )
                for j in range(4)
            ]
            return jnp.concatenate(blocks, axis=axis)

        def swap_h(values):
            return [swap_with(values, "h", k, groups) for k in range(1, groups)]

        def fold_start(rows, axis, name):
            sent = lax.dynamic_index_in_dim(rows, 1 - lax.axis_index(name), axis, keepdims=False)
            return swap_with(sent, name, 1, 2)

        def fold_end(rows, got, axis, name):
            mine = lax.dynamic_index_in_dim(rows, lax.axis_index(name), axis, keepdims=False)
            return mine.astype(F32) + got.astype(F32)

        def halves(rows):
            return rows[..., : width // 2], rows[..., width // 2 :]

        def swap_c(values):
            return swap_with(values, "core", 1, 2)

        def quad_swap(values, m):
            return swap_with(values, ("l", "x"), m, 4)

        seg_len = segment_ids.shape[1]
        in_cols = 3 * w_qkv.shape[2] // 4 + w_fc1.shape[1] // 4
        labels = jnp.pad(segment_ids.astype(BF), ((0, 15), (0, in_cols - seg_len)))

        def take_in(which):
            piece = part(w_qkv, which, 4, 2)
            rows = jnp.concatenate(
                [piece[:, j] for j in range(3)] + [part(w_fc1, which, 4, 1)], axis=1
            )
            return jnp.concatenate([rows, labels], axis=0)

        def take_out(which):
            return jnp.concatenate([part(w_dense, which, 4, 0), part(w_fc2, which, 4, 0)], axis=0)

        def stacked(parts, axis):
            return jnp.concatenate(parts, axis=axis)

        def unstack(values, count, axis):
            return [fixed(values, m, count, axis) for m in range(count)]

        local = w_dense.shape[0] // 4
        qkv_cols = 3 * local

        order = jnp.stack([quad, quad ^ 1, quad ^ 2, quad ^ 3])
        rows_in, cols_out = w_fc1.shape[0], w_fc2.shape[1]

        def gather_tokens(mine, other):
            rows = lax.all_gather(
                jnp.stack([mine, other]), ("x", "y", "core"), axis=1, tiled=True
            )
            return rows.reshape(-1, width)

        hidden = hidden_in.astype(F32)
        mine_n = own_order(layer_norm(hidden, ln_gain, ln_bias).astype(BF), 1)
        mine_g = own_order(out_grad, 1)
        next_n = swap_with(mine_n, "l", 1, 2)
        in_own = take_in(quad)
        in_send = [take_in(quad ^ m) for m in (1, 2, 3)]
        mine_n, next_n, in_own, in_send, mine_g = step(mine_n, next_n, in_own, in_send, mine_g)
        normed_all = gather_tokens(mine_n, next_n)
        in_first = swap_h(in_own[:rows_in])
        in_parts = [in_own] + [quad_swap(piece, m) for m, piece in zip((1, 2, 3), in_send)]
        out_own = take_out(quad)
        out_first = swap_h(out_own)
        out_send = [take_out(quad ^ m) for m in (1, 2, 3)]
        in_parts, in_first, mine_g, out_own, out_first, out_send = step(
            in_parts, in_first, mine_g, out_own, out_first, out_send
        )

        in_low = swap_h(in_parts[1][:rows_in])
        next_g = swap_with(mine_g, "l", 1, 2)
        out_1 = quad_swap(out_send[0], 1)
        in_high = stacked([p[:rows_in] for p in in_parts[2:]], 0)
        in_low, next_g, out_1, in_high, out_send, mine_g = step(
            in_low, next_g, out_1, in_high, out_send, mine_g
        )
        in_rest = swap_h(in_high)
        out_parts = [out_own, out_1] + [quad_swap(out_send[m - 1], m) for m in (2, 3)]
        grad_all = gather_tokens(mine_g, next_g)
        out_stack = stacked(out_parts[1:], 1)
        in_rest, out_parts, out_stack = step(in_rest, out_parts, out_stack)

        out_rest = swap_h(out_stack)
        in_first, in_parts, in_low, in_rest = step(in_first, in_parts, in_low, in_rest)
        sources = [(p, (0, 0), 0, m) for m, p in enumerate(in_parts)]
        for k in range(1, groups):
            sources.append((in_first[k - 1], (0, 0), k, 0))
            sources.append((in_low[k - 1], (0, 0), k, 1))
            sources += [(in_rest[k - 1], ((m - 2) * rows_in, 0), k, m) for m in (2, 3)]
        in_w = place(order, sources, 4 * groups, 0, (width, in_cols))
        labels_all = [p[rows_in, :seg_len].astype(jnp.int32)[None] for p in in_parts]
        ordered = in_order(labels_all, 0)
        segments = jnp.where(lb == 1, jnp.roll(ordered, 2, axis=0), ordered)
        in_b = stacked([part(b_qkv, quad, 4, 1).reshape(-1), part(b_fc1, quad, 4, 0)], 0)
        mixed = dot(normed_all, in_w, ((1,), (0,))) + in_b
        tables = rotary_tables(segments.shape[1], local)
        qkv, context, lse = attention(mixed, local, tables, segments)
        before = mixed[:, qkv_cols:]
        acts = stacked([context, gelu_tanh(before).astype(BF)], 1)
        qkv, acts, lse, mixed = step(qkv, acts, lse, mixed)

        def slot(values, k, axis):
            return fixed(values, k, groups, axis)

        out_rows = acts.shape[1]
        out_part = dot(acts, grad_all, ((0,), (0,))).astype(BF)
        cuts = [out_rows * i // 40 for i in (0, 6, 27, 40)]
        out_send = [
            [slot(out_part, k, 1)[cuts[i] : cuts[i + 1]] for i in range(3)] for k in range(groups)
        ]
        out_send, out_rest = step(out_send, out_rest)
        out_ws = []
        for low, high in ((0, local), (local, out_rows)):
            sources = [(p, (low, 0), 0, m) for m, p in enumerate(out_parts)]
            for k in range(1, groups):
                sources.append((out_first[k - 1], (low, 0), k, 0))
                sources += [(out_rest[k - 1], (low, (m - 1) * cols_out), k, m) for m in (1, 2, 3)]
            out_ws.append(place(order, sources, 4 * groups, 1, (high - low, width)))

        def send_out(i):
            return [swap_with(out_send[k][i], "h", k, groups) for k in range(1, groups)]

        def team_sum(values):
            return lax.psum_scatter(
                values.reshape(2, -1, width), ("x", "y", "core"), scatter_dimension=1, tiled=True
            )

        out_0 = send_out(0)
        acts, out_ws = step(acts, out_ws)
        tokens = acts.shape[0]
        (branch,) = by_tokens(
            branch_kernel, "branch", tokens, 2 * tokens * out_rows * width, [acts], out_ws, [width]
        )
        branch, out_ws, out_0, out_send = step(branch, out_ws, out_0, out_send)
        branch_sum = team_sum(branch)
        out_1 = send_out(1)
        out_ws, qkv, lse, mixed = step(out_ws, qkv, lse, mixed)

        def back(grad_ref, mixed_ref, dense_ref, down_ref, context_ref, into_ref):
            back_kernel(grad_ref, dense_ref, down_ref, mixed_ref, context_ref, into_ref)

        context_grad, into = by_tokens(
            back, "back", tokens, 2 * tokens * out_rows * width, [grad_all, mixed], out_ws,
            [local, in_cols],
        )
        into = attention_grad(qkv, context_grad, lse, tables, segments, into)
        into, out_1, out_send = step(into, out_1, out_send)

        def add_up(mine, others):
            mine = mine.astype(F32)
            for piece in others:
                mine = mine + piece.astype(F32)
            return mine

        def out_total(pieces, got):
            total = stacked([add_up(out_send[0][i], g) for i, g in zip(pieces, got)], 0)
            sent = total.astype(BF)
            return part(total, quad, 4, 1), [part(sent, quad ^ m, 4, 1) for m in (1, 2, 3)]

        out_2 = send_out(2)
        low_kept, low_send = out_total((0, 1), (out_0, out_1))
        low_kept, low_send = step(low_kept, low_send)
        low_back = [quad_swap(piece, m) for m, piece in zip((1, 2, 3), low_send)]
        into, normed_all = step(into, normed_all)
        in_part = dot(normed_all, into, ((0,), (0,))).astype(BF)
        in_part, into, out_2, low_back, low_kept = step(in_part, into, out_2, low_back, low_kept)

        def block(k, m):
            start = k * span + (quad ^ m) * (span // 4)
            return lax.dynamic_slice_in_dim(in_part, start, span // 4, 0)

        def swap_block(m):
            return [swap_with(in_send[m][k], "h", k, groups) for k in range(1, groups)]

        high_kept, high_send = out_total((2,), (out_2,))
        in_send = [[block(k, m) for k in range(groups)] for m in range(4)]
        in_send, high_send, high_kept = step(in_send, high_send, high_kept)

        in_3 = swap_block(3)
        high_back = [quad_swap(piece, m) for m, piece in zip((1, 2, 3), high_send)]
        into, in_w, normed_all = step(into, in_w, normed_all)
        terms = dot(into, in_w, ((1,), (1,)))
        unit = (normed_all.astype(F32) - own_order(ln_bias, 0)) / own_order(ln_gain, 0)
        gain_sum, shift_sum = jnp.sum(terms * unit, axis=0), jnp.sum(terms, axis=0)
        terms = terms.astype(BF)
        terms, gain_sum, shift_sum, in_3, in_send, high_back = step(
            terms, gain_sum, shift_sum, in_3, in_send, high_back
        )
        terms_sum = team_sum(terms)
        branch_own, branch_next = branch_sum[0], branch_sum[1]

        in_2, in_1 = swap_block(2), swap_block(1)
        in_send[3], in_3 = step(in_send[3], in_3)
        back_3 = quad_swap(add_up(in_send[3][0], in_3).astype(BF), 3)
        got_m = swap_with(branch_next, "l", 1, 2)
        small = [
            own_order(gain_sum, 0),
            own_order(shift_sum, 0),
            jnp.sum(out_grad.astype(F32), axis=0),
        ]
        bias = jnp.sum(into, axis=0, dtype=F32)
        size = in_cols
        team = 4 * (2 * lax.axis_index("y") + lax.axis_index("core"))
        bias = lax.dynamic_update_slice(jnp.zeros((16 * size,), F32), bias, ((team + quad) * size,))
        total = stacked(small + [bias], 0)
        total = total + swap_c(total)
        total = total + swap_with(total, "y", 1, 2)
        in_2, in_1, back_3, got_m, total, in_send = step(
            in_2, in_1, back_3, got_m, total, in_send
        )

        in_0 = swap_block(0)
        in_1, in_2 = step(in_1, in_2)
        back_1 = quad_swap(add_up(in_send[1][0], in_1).astype(BF), 1)
        back_2 = quad_swap(add_up(in_send[2][0], in_2).astype(BF), 2)
        total = total + swap_with(total, "x", 1, 2)
        total = total + swap_with(total, "l", 1, 2)
        out_pieces = [stacked([low_kept, high_kept], 0)] + [
            stacked([low, high], 0).astype(F32) for low, high in zip(low_back, high_back)
        ]
        dense_grad = in_order([p[:local] for p in out_pieces], 0)
        down_grad = in_order([p[local:] for p in out_pieces], 0)
        branch = own_order(branch_own.astype(F32) + got_m.astype(F32), 1)
        hidden_out = (hidden + branch + b_dense + b_fc2).astype(BF)
        own_in = add_up(in_send[0][0], in_0)
        own_in, back_1, back_2, total, dense_grad, down_grad, hidden_out = step(
            own_in, back_1, back_2, total, dense_grad, down_grad, hidden_out
        )

        bit = 1
        while bit < groups:
            total = total + swap_with(total, "h", bit, groups)
            bit *= 2
        got_n = swap_with(terms_sum[1], "l", 1, 2)
        input_grad = norm_grad(group, groups, terms_sum[0], got_n, hidden_in, out_grad, ln_gain)
        qkv_grad, up_grad = settle(order, [own_in, back_1, back_2, back_3], local)
        gain_grad, shift_grad, out_bias_grad = (
            total[:width], total[width : 2 * width], total[2 * width : 3 * width]
        )
        bias = lax.dynamic_slice(total, (3 * width + team * size,), (4 * size,)).reshape(4, size)
        up_bias_grad = bias[:, qkv_cols:].reshape(-1)
        qkv_bias_grad = jnp.stack(
            [bias[:, j * local : (j + 1) * local].reshape(-1) for j in range(3)]
        )
        return (
            hidden_out, input_grad, gain_grad, shift_grad, qkv_grad, qkv_bias_grad,
            dense_grad, out_bias_grad, up_grad, up_bias_grad, down_grad, out_bias_grad,
        )

    return body


def solution(mesh):
    groups = mesh.shape["fsdp"] // 4
    grid = Mesh(mesh.devices.reshape(groups, 2, 2, 2, 2), ("h", "l", "x", "y", "core"))
    rows, cols = ("h", "l", "x"), ("y", "core")
    tokens = rows + cols
    in_specs = (
        P(tokens, None), P(), P(), P(rows, None, cols), P(None, cols), P(cols, rows), P(),
        P(rows, cols), P(cols), P(cols, rows), P(), P(rows, None), P(tokens, None),
    )
    out_specs = (
        P(tokens, None), P(tokens, None), P(), P(), P(rows, None, cols), P(None, cols),
        P(cols, rows), P(), P(rows, cols), P(cols), P(cols, rows), P(),
    )
    return jax.shard_map(
        make_body(groups), mesh=grid, in_specs=in_specs, out_specs=out_specs, check_vma=False
    )
```

```python
import math

import jax
import jax.numpy as jnp
from jax import lax
from jax.experimental import pallas as pl
from jax.experimental.pallas import tpu as pltpu
from jax.sharding import Mesh
from jax.sharding import PartitionSpec as P

HEAD_DIM = 64
ROT = 32
EPS = 1e-05
BLOCK = 128
ROWS = 512
CHUNK = 512
REACH = 256
SCALE = 1.0 / math.sqrt(HEAD_DIM)

BF = jnp.bfloat16
F32 = jnp.float32


def layer_norm(values, norm_gain, norm_shift):
    centred = values - jnp.mean(values, axis=-1, keepdims=True)
    variance = jnp.mean(centred * centred, axis=-1, keepdims=True)
    return centred * lax.rsqrt(variance + EPS) * norm_gain + norm_shift


def gelu_tanh(values):
    return jax.nn.gelu(values, approximate=True)


def rotary_tables(length, lanes):
    lane = jnp.arange(lanes) % HEAD_DIM
    pair = lane % (ROT // 2)
    angles = jnp.arange(length).astype(F32)[:, None] * (
        10000.0 ** (-(2.0 * pair.astype(F32)) / ROT)
    )
    cosine = jnp.where(lane < ROT, jnp.cos(angles), 1.0)
    sine = jnp.sin(angles)
    first = jnp.where(lane < ROT // 2, -sine, 0.0)
    second = jnp.where((lane >= ROT // 2) & (lane < ROT), sine, 0.0)
    return cosine, first, second


def turn(values, cosine, first, second):
    half, lanes = ROT // 2, values.shape[1]
    return (
        values * cosine
        + pltpu.roll(values, lanes - half, 1) * first
        + pltpu.roll(values, half, 1) * second
    )


def nt(left, right):
    return lax.dot_general(left, right, (((1,), (1,)), ((), ())), preferred_element_type=F32)


def tn(left, right):
    return lax.dot_general(left, right, (((0,), (0,)), ((), ())), preferred_element_type=F32)


def windows(length):
    for start in range(0, length, BLOCK):
        low = max(0, (start - REACH + 1) // BLOCK * BLOCK)
        yield start, low, start + BLOCK


def allowed_mask(row_ref, col_ref, start, low, high):
    size = high - low
    key = low + lax.broadcasted_iota(jnp.int32, (size, BLOCK), 0)
    query = start + lax.broadcasted_iota(jnp.int32, (size, BLOCK), 1)
    same = col_ref[low:high, :] == row_ref[0, :, start : start + BLOCK]
    return same & (key <= query)


def head_lanes(rows, head, lanes):
    lane = lax.broadcasted_iota(jnp.int32, (rows, lanes), 1)
    return lane // HEAD_DIM == head


def attend_kernel(mixed_ref, cos_ref, a_ref, b_ref, row_ref, col_ref, qkv_ref, out_ref, lse_ref):
    length, lanes = out_ref.shape
    tables = cos_ref[...], a_ref[...], b_ref[...]
    query = turn(mixed_ref[:, :lanes], *tables).astype(BF)
    query = (query.astype(F32) * SCALE).astype(BF)
    key = turn(mixed_ref[:, lanes : 2 * lanes], *tables).astype(BF)
    value = mixed_ref[:, 2 * lanes :].astype(BF)
    qkv_ref[:, :lanes] = query
    qkv_ref[:, lanes : 2 * lanes] = key
    qkv_ref[:, 2 * lanes :] = value
    for start, low, high in windows(length):
        mask = allowed_mask(row_ref, col_ref, start, low, high)
        mine = query[start:high]
        out = jnp.zeros((BLOCK, lanes), F32)
        for head in range(lanes // HEAD_DIM):
            own = head_lanes(BLOCK, head, lanes)
            scores = nt(key[low:high], jnp.where(own, mine, jnp.zeros_like(mine)))
            scores = jnp.where(mask, scores, -1e30)
            highest = jnp.max(scores, axis=0, keepdims=True)
            shifted = jnp.exp(scores - highest)
            total = jnp.sum(shifted, axis=0, keepdims=True)
            attend = (shifted / total).astype(BF)
            out = jnp.where(own, tn(attend, value[low:high]), out)
            lse_ref[0, head : head + 1, start:high] = highest + jnp.log(total)
        out_ref[start:high, :] = out.astype(BF)


def attend_grad_kernel(
    qkv_ref, grad_ref, lse_ref, cos_ref, a_ref, b_ref, row_ref, col_ref, into_ref,
    out_ref, key_ref, value_ref,
):
    length, lanes = grad_ref.shape
    key_ref[...] = jnp.zeros_like(key_ref)
    value_ref[...] = jnp.zeros_like(value_ref)
    for start, low, high in windows(length):
        mask = allowed_mask(row_ref, col_ref, start, low, high)
        query = qkv_ref[start:high, :lanes]
        key = qkv_ref[low:high, lanes : 2 * lanes]
        value = qkv_ref[low:high, 2 * lanes :]
        grad = grad_ref[start:high, :]
        query_grad = jnp.zeros((BLOCK, lanes), F32)
        key_grad = jnp.zeros((high - low, lanes), F32)
        value_grad = jnp.zeros((high - low, lanes), F32)
        for head in range(lanes // HEAD_DIM):
            own = head_lanes(BLOCK, head, lanes)
            own_keys = head_lanes(high - low, head, lanes)
            none = jnp.zeros_like(query)
            scores = nt(key, jnp.where(own, query, none))
            scores = jnp.where(mask, scores, -1e30)
            attend = jnp.exp(scores - lse_ref[0, head : head + 1, start:high])
            attend_grad = nt(value, jnp.where(own, grad, none))
            inner = jnp.sum(attend * attend_grad, axis=0, keepdims=True)
            score_grad = (attend * (attend_grad - inner)).astype(BF)
            query_grad = jnp.where(own, tn(score_grad, key), query_grad)
            key_grad = jnp.where(
                own_keys, jnp.dot(score_grad, query, preferred_element_type=F32), key_grad
            )
            value_grad = jnp.where(
                own_keys,
                jnp.dot(attend.astype(BF), grad, preferred_element_type=F32),
                value_grad,
            )
        back = [ref[start:high, :] for ref in (cos_ref, a_ref, b_ref)]
        query_grad = turn(query_grad * SCALE, back[0], -back[1], -back[2])
        out_ref[start:high, :lanes] = query_grad.astype(BF)
        key_ref[low:high, :] += key_grad
        value_ref[low:high, :] += value_grad
    key_grad = turn(key_ref[...], cos_ref[...], -a_ref[...], -b_ref[...])
    out_ref[:, lanes : 2 * lanes] = key_grad.astype(BF)
    out_ref[:, 2 * lanes :] = value_ref[...].astype(BF)


def attention_specs(length, lanes):
    table = pl.BlockSpec((length, lanes), lambda s: (0, 0))
    return dict(
        table=table,
        wide=pl.BlockSpec((length, 3 * lanes), lambda s: (s, 0)),
        slim=pl.BlockSpec((length, lanes), lambda s: (s, 0)),
        lse=pl.BlockSpec((1, lanes // HEAD_DIM, length), lambda s: (s, 0, 0)),
        row=pl.BlockSpec((1, 1, length), lambda s: (s, 0, 0)),
        col=pl.BlockSpec((length, 1), lambda s: (s, 0)),
    )


def attention(mixed, lanes, tables, segments):
    sequences, length = segments.shape
    spec = attention_specs(length, lanes)
    rows = sequences * length
    return pl.pallas_call(
        attend_kernel,
        grid=(sequences,),
        in_specs=[spec["wide"]] + [spec["table"]] * 3 + [spec["row"], spec["col"]],
        out_specs=[spec["wide"], spec["slim"], spec["lse"]],
        out_shape=[
            jax.ShapeDtypeStruct((rows, 3 * lanes), BF),
            jax.ShapeDtypeStruct((rows, lanes), BF),
            jax.ShapeDtypeStruct((sequences, lanes // HEAD_DIM, length), F32),
        ],
        compiler_params=pltpu.CompilerParams(vmem_limit_bytes=32 << 20),
        name="attend",
    )(mixed, *tables, segments[:, None, :], segments.reshape(-1, 1))


def attention_grad(qkv, grad, lse, tables, segments, into):
    sequences, length = segments.shape
    rows, lanes = grad.shape
    spec = attention_specs(length, lanes)
    return pl.pallas_call(
        attend_grad_kernel,
        grid=(sequences,),
        in_specs=[spec["wide"], spec["slim"], spec["lse"]]
        + [spec["table"]] * 3
        + [spec["row"], spec["col"], pl.BlockSpec(memory_space=pl.ANY)],
        out_specs=spec["wide"],
        out_shape=jax.ShapeDtypeStruct(into.shape, BF),
        input_output_aliases={8: 0},
        scratch_shapes=[pltpu.VMEM((length, lanes), F32)] * 2,
        compiler_params=pltpu.CompilerParams(vmem_limit_bytes=32 << 20),
        name="attend_grad",
    )(qkv, grad, lse, *tables, segments[:, None, :], segments.reshape(-1, 1), into)


def gelu_slope(values):
    scale = math.sqrt(2.0 / math.pi)
    square = values * values
    bent = jnp.tanh(scale * (values + 0.044715 * values * square))
    return 0.5 * (1.0 + bent) + 0.5 * values * (1.0 - bent * bent) * scale * (
        1.0 + 3.0 * 0.044715 * square
    )


def branch_kernel(acts_ref, dense_ref, down_ref, out_ref):
    local, width = dense_ref.shape
    for low in range(0, width, CHUNK):
        cols = slice(low, low + CHUNK)
        total = jnp.dot(
            acts_ref[:, :local], dense_ref[:, cols], preferred_element_type=F32
        ) + jnp.dot(acts_ref[:, local:], down_ref[:, cols], preferred_element_type=F32)
        out_ref[:, cols] = total.astype(BF)


def back_kernel(grad_ref, dense_ref, down_ref, mixed_ref, context_ref, into_ref):
    units = down_ref.shape[0]
    first = mixed_ref.shape[1] - units
    grad = grad_ref[...]
    context_ref[...] = nt(grad, dense_ref[...]).astype(BF)
    activated_grad = nt(grad, down_ref[...])
    slope = gelu_slope(mixed_ref[:, first:])
    into_ref[:, :first] = jnp.zeros((into_ref.shape[0], first), BF)
    into_ref[:, first:] = (activated_grad * slope).astype(BF)


def norm_grad(group, groups, mine, got, hidden_in, out_grad, ln_gain):
    rows, width = hidden_in.shape
    span = width // groups

    def kernel(group_ref, mine_ref, got_ref, hidden_ref, cot_ref, gain_ref, out_ref, sum_ref):
        for j in range(groups):
            cols = pl.ds(pl.multiple_of((group_ref[0] ^ j) * span, span), span)
            sum_ref[:, j * span : (j + 1) * span] = mine_ref[:, cols].astype(F32) + got_ref[
                :, cols
            ].astype(F32)
        hidden = hidden_ref[...].astype(F32)
        centred = hidden - jnp.mean(hidden, axis=-1, keepdims=True)
        variance = jnp.mean(centred * centred, axis=-1, keepdims=True)
        scale = lax.rsqrt(variance + EPS)
        unit = centred * scale
        slope = sum_ref[...] * gain_ref[...]
        first = jnp.mean(slope, axis=-1, keepdims=True)
        second = jnp.mean(slope * unit, axis=-1, keepdims=True)
        out_ref[...] = scale * (slope - first - unit * second) + cot_ref[...].astype(F32)

    whole = pl.BlockSpec(memory_space=pltpu.VMEM)
    return pl.pallas_call(
        kernel,
        in_specs=[pl.BlockSpec(memory_space=pltpu.SMEM)] + [whole] * 5,
        out_specs=whole,
        out_shape=jax.ShapeDtypeStruct((rows, width), F32),
        scratch_shapes=[pltpu.VMEM((rows, width), F32)],
        compiler_params=pltpu.CompilerParams(vmem_limit_bytes=24 << 20),
        name="norm_grad",
    )(group[None], mine, got, hidden_in, out_grad, ln_gain[None, :])


def settle(order, pieces, local):
    rows, cols = pieces[0].shape
    units = cols - 3 * local

    def kernel(order_ref, *refs):
        ins, qkv_ref, up_ref = refs[:4], refs[4], refs[5]
        for m, ref in enumerate(ins):
            to = pl.multiple_of(order_ref[m] * units, units)
            up_ref[:, pl.ds(to, units)] = ref[:, 3 * local :].astype(F32)
            to = pl.multiple_of(order_ref[m] * local, local)
            for j in range(3):
                qkv_ref[j, :, pl.ds(to, local)] = ref[:, j * local : (j + 1) * local].astype(F32)

    whole = pl.BlockSpec(memory_space=pltpu.VMEM)
    qkv, up = pl.pallas_call(
        kernel,
        in_specs=[pl.BlockSpec(memory_space=pltpu.SMEM)] + [whole] * 4,
        out_specs=[whole] * 2,
        out_shape=[
            jax.ShapeDtypeStruct((3, rows, 4 * local), F32),
            jax.ShapeDtypeStruct((rows, 4 * units), F32),
        ],
        compiler_params=pltpu.CompilerParams(vmem_limit_bytes=24 << 20),
        name="settle",
    )(order, *pieces)
    return jnp.transpose(qkv, (1, 0, 2)), up


def by_tokens(kernel, name, rows, flops, blocked, whole, outs):
    def cut(cols):
        return pl.BlockSpec((ROWS, cols), lambda i: (i, 0))

    def kept(array):
        return pl.BlockSpec(array.shape, lambda i: (0, 0))

    specs = [cut(a.shape[1]) if a.shape[0] == rows and cutting else kept(a)
             for a, cutting in [(a, True) for a in blocked] + [(a, False) for a in whole]]
    size = sum(a.size * a.dtype.itemsize for a in list(blocked) + list(whole))
    return pl.pallas_call(
        kernel,
        grid=(rows // ROWS,),
        in_specs=specs,
        out_specs=[cut(cols) for cols in outs],
        out_shape=[jax.ShapeDtypeStruct((rows, cols), BF) for cols in outs],
        compiler_params=pltpu.CompilerParams(vmem_limit_bytes=48 << 20),
        cost_estimate=pl.CostEstimate(
            flops=flops, bytes_accessed=size + 2 * rows * sum(outs), transcendentals=0
        ),
        name=name,
    )(*blocked, *whole)


def place(order, sources, count, axis, shape):
    arrays = []
    for array, _, _, _ in sources:
        if not any(array is seen for seen in arrays):
            arrays.append(array)
    where = [[array is seen for seen in arrays].index(True) for array, _, _, _ in sources]
    size = shape[axis] // count

    def kernel(order_ref, *refs):
        ins, out = refs[: len(arrays)], refs[-1]
        for i, (_, (rows, cols), slot, entry) in enumerate(sources):
            to = pl.multiple_of((slot * 4 + order_ref[entry]) * size, size)
            if axis == 0:
                out[pl.ds(to, size), :] = ins[where[i]][rows : rows + size, cols : cols + shape[1]]
            else:
                out[:, pl.ds(to, size)] = ins[where[i]][rows : rows + shape[0], cols : cols + size]

    if axis == 1 and size % 128:
        result = jnp.zeros(shape, arrays[0].dtype)
        for array, (rows, cols), slot, entry in sources:
            piece = lax.slice(array, (rows, cols), (rows + shape[0], cols + size))
            to = (slot * 4 + order[entry]) * size
            result = lax.dynamic_update_slice_in_dim(result, piece, to, 1)
        return result

    whole = pl.BlockSpec(memory_space=pltpu.VMEM)
    return pl.pallas_call(
        kernel,
        in_specs=[pl.BlockSpec(memory_space=pltpu.SMEM)] + [whole] * len(arrays),
        out_specs=whole,
        out_shape=jax.ShapeDtypeStruct(shape, arrays[0].dtype),
        compiler_params=pltpu.CompilerParams(vmem_limit_bytes=24 << 20),
        name="place",
    )(order, *arrays)


def swap_with(values, axis, mask, size):
    return lax.ppermute(values, axis, [(i, i ^ mask) for i in range(size)])


def dot(left, right, dims):
    return lax.dot_general(left, right, (dims, ((), ())), preferred_element_type=F32)


def after(values, *earlier):
    return lax.optimization_barrier((values,) + earlier)[0]


def step(*values):
    return lax.optimization_barrier(values)


TEAM = ("l", "x", "y", "core")


def make_body(groups):
    def body(
        hidden_in, ln_gain, ln_bias, w_qkv, b_qkv, w_dense, b_dense,
        w_fc1, b_fc1, w_fc2, b_fc2, segment_ids, out_grad,
    ):
        group, lb, xb = lax.axis_index("h"), lax.axis_index("l"), lax.axis_index("x")
        quad = 2 * lb + xb
        tile, width = hidden_in.shape
        span = width // groups

        def part(values, which, count, axis):
            size = values.shape[axis] // count
            return lax.dynamic_slice_in_dim(values, which * size, size, axis)

        def fixed(values, which, count, axis):
            size = values.shape[axis] // count
            return lax.slice_in_dim(values, which * size, (which + 1) * size, axis=axis)

        def own_order(values, axis):
            bit = 1
            while bit < groups:
                blocks = [fixed(values, j ^ bit, groups, axis) for j in range(groups)]
                flipped = jnp.concatenate(blocks, axis=axis)
                values = jnp.where((group // bit) % 2 == 1, flipped, values)
                bit *= 2
            return values

        def trade(give, own):
            return [own] + [swap_with(give(quad ^ m), ("l", "x"), m, 4) for m in (1, 2, 3)]

        def in_order(parts, axis):
            blocks = [
                jnp.where(
                    lb == 1,
                    jnp.where(xb == 1, parts[j ^ 3], parts[j ^ 2]),
                    jnp.where(xb == 1, parts[j ^ 1], parts[j]),
                )
                for j in range(4)
            ]
            return jnp.concatenate(blocks, axis=axis)

        def swap_h(values):
            return [swap_with(values, "h", k, groups) for k in range(1, groups)]

        def fold_start(rows, axis, name):
            sent = lax.dynamic_index_in_dim(rows, 1 - lax.axis_index(name), axis, keepdims=False)
            return swap_with(sent, name, 1, 2)

        def fold_end(rows, got, axis, name):
            mine = lax.dynamic_index_in_dim(rows, lax.axis_index(name), axis, keepdims=False)
            return mine.astype(F32) + got.astype(F32)

        def halves(rows):
            return rows[..., : width // 2], rows[..., width // 2 :]

        def swap_c(values):
            return swap_with(values, "core", 1, 2)

        def quad_swap(values, m):
            return swap_with(values, ("l", "x"), m, 4)

        seg_len = segment_ids.shape[1]
        in_cols = 3 * w_qkv.shape[2] // 4 + w_fc1.shape[1] // 4
        labels = jnp.pad(segment_ids.astype(BF), ((0, 15), (0, in_cols - seg_len)))

        def take_in(which):
            piece = part(w_qkv, which, 4, 2)
            rows = jnp.concatenate(
                [piece[:, j] for j in range(3)] + [part(w_fc1, which, 4, 1)], axis=1
            )
            return jnp.concatenate([rows, labels], axis=0)

        def take_out(which):
            return jnp.concatenate([part(w_dense, which, 4, 0), part(w_fc2, which, 4, 0)], axis=0)

        def stacked(parts, axis):
            return jnp.concatenate(parts, axis=axis)

        def unstack(values, count, axis):
            return [fixed(values, m, count, axis) for m in range(count)]

        local = w_dense.shape[0] // 4
        qkv_cols = 3 * local

        order = jnp.stack([quad, quad ^ 1, quad ^ 2, quad ^ 3])
        rows_in, cols_out = w_fc1.shape[0], w_fc2.shape[1]

        def gather_tokens(mine, other):
            rows = lax.all_gather(
                jnp.stack([mine, other]), ("x", "y", "core"), axis=1, tiled=True
            )
            return rows.reshape(-1, width)

        hidden = hidden_in.astype(F32)
        mine_n = own_order(layer_norm(hidden, ln_gain, ln_bias).astype(BF), 1)
        mine_g = own_order(out_grad, 1)
        next_n = swap_with(mine_n, "l", 1, 2)
        in_own = take_in(quad)
        in_send = [take_in(quad ^ m) for m in (1, 2, 3)]
        mine_n, next_n, in_own, in_send, mine_g = step(mine_n, next_n, in_own, in_send, mine_g)
        normed_all = gather_tokens(mine_n, next_n)
        in_first = swap_h(in_own[:rows_in])
        in_parts = [in_own] + [quad_swap(piece, m) for m, piece in zip((1, 2, 3), in_send)]
        out_own = take_out(quad)
        out_first = swap_h(out_own)
        out_send = [take_out(quad ^ m) for m in (1, 2, 3)]
        in_parts, in_first, mine_g, out_own, out_first, out_send = step(
            in_parts, in_first, mine_g, out_own, out_first, out_send
        )

        in_low = swap_h(in_parts[1][:rows_in])
        next_g = swap_with(mine_g, "l", 1, 2)
        out_1 = quad_swap(out_send[0], 1)
        in_high = stacked([p[:rows_in] for p in in_parts[2:]], 0)
        in_low, next_g, out_1, in_high, out_send, mine_g = step(
            in_low, next_g, out_1, in_high, out_send, mine_g
        )
        in_rest = swap_h(in_high)
        out_parts = [out_own, out_1] + [quad_swap(out_send[m - 1], m) for m in (2, 3)]
        grad_all = gather_tokens(mine_g, next_g)
        out_stack = stacked(out_parts[1:], 1)
        in_rest, out_parts, out_stack = step(in_rest, out_parts, out_stack)

        out_rest = swap_h(out_stack)
        in_first, in_parts, in_low, in_rest = step(in_first, in_parts, in_low, in_rest)
        sources = [(p, (0, 0), 0, m) for m, p in enumerate(in_parts)]
        for k in range(1, groups):
            sources.append((in_first[k - 1], (0, 0), k, 0))
            sources.append((in_low[k - 1], (0, 0), k, 1))
            sources += [(in_rest[k - 1], ((m - 2) * rows_in, 0), k, m) for m in (2, 3)]
        in_w = place(order, sources, 4 * groups, 0, (width, in_cols))
        labels_all = [p[rows_in, :seg_len].astype(jnp.int32)[None] for p in in_parts]
        ordered = in_order(labels_all, 0)
        segments = jnp.where(lb == 1, jnp.roll(ordered, 2, axis=0), ordered)
        in_b = stacked([part(b_qkv, quad, 4, 1).reshape(-1), part(b_fc1, quad, 4, 0)], 0)
        mixed = dot(normed_all, in_w, ((1,), (0,))) + in_b
        tables = rotary_tables(segments.shape[1], local)
        qkv, context, lse = attention(mixed, local, tables, segments)
        before = mixed[:, qkv_cols:]
        acts = stacked([context, gelu_tanh(before).astype(BF)], 1)
        qkv, acts, lse, mixed = step(qkv, acts, lse, mixed)

        def slot(values, k, axis):
            return fixed(values, k, groups, axis)

        out_rows = acts.shape[1]
        out_part = dot(acts, grad_all, ((0,), (0,))).astype(BF)
        cuts = [out_rows * i // 40 for i in (0, 6, 27, 40)]
        out_send = [
            [slot(out_part, k, 1)[cuts[i] : cuts[i + 1]] for i in range(3)] for k in range(groups)
        ]
        out_send, out_rest = step(out_send, out_rest)
        out_ws = []
        for low, high in ((0, local), (local, out_rows)):
            sources = [(p, (low, 0), 0, m) for m, p in enumerate(out_parts)]
            for k in range(1, groups):
                sources.append((out_first[k - 1], (low, 0), k, 0))
                sources += [(out_rest[k - 1], (low, (m - 1) * cols_out), k, m) for m in (1, 2, 3)]
            out_ws.append(place(order, sources, 4 * groups, 1, (high - low, width)))

        def send_out(i):
            return [swap_with(out_send[k][i], "h", k, groups) for k in range(1, groups)]

        def team_sum(values):
            return lax.psum_scatter(
                values.reshape(2, -1, width), ("x", "y", "core"), scatter_dimension=1, tiled=True
            )

        out_0 = send_out(0)
        acts, out_ws = step(acts, out_ws)
        tokens = acts.shape[0]
        (branch,) = by_tokens(
            branch_kernel, "branch", tokens, 2 * tokens * out_rows * width, [acts], out_ws, [width]
        )
        branch, out_ws, out_0, out_send = step(branch, out_ws, out_0, out_send)
        branch_sum = team_sum(branch)
        out_1 = send_out(1)
        out_ws, qkv, lse, mixed = step(out_ws, qkv, lse, mixed)

        def back(grad_ref, mixed_ref, dense_ref, down_ref, context_ref, into_ref):
            back_kernel(grad_ref, dense_ref, down_ref, mixed_ref, context_ref, into_ref)

        context_grad, into = by_tokens(
            back, "back", tokens, 2 * tokens * out_rows * width, [grad_all, mixed], out_ws,
            [local, in_cols],
        )
        into = attention_grad(qkv, context_grad, lse, tables, segments, into)
        into, out_1, out_send = step(into, out_1, out_send)

        def add_up(mine, others):
            mine = mine.astype(F32)
            for piece in others:
                mine = mine + piece.astype(F32)
            return mine

        def out_total(pieces, got):
            total = stacked([add_up(out_send[0][i], g) for i, g in zip(pieces, got)], 0)
            sent = total.astype(BF)
            return part(total, quad, 4, 1), [part(sent, quad ^ m, 4, 1) for m in (1, 2, 3)]

        out_2 = send_out(2)
        low_kept, low_send = out_total((0, 1), (out_0, out_1))
        low_kept, low_send = step(low_kept, low_send)
        low_back = [quad_swap(piece, m) for m, piece in zip((2, 3), low_send[1:])]
        into, normed_all = step(into, normed_all)
        in_part = dot(normed_all, into, ((0,), (0,))).astype(BF)
        in_part, into, out_2, low_back, low_kept, low_send = step(
            in_part, into, out_2, low_back, low_kept, low_send
        )

        def block(k, m):
            start = k * span + (quad ^ m) * (span // 4)
            return lax.dynamic_slice_in_dim(in_part, start, span // 4, 0)

        def swap_block(m):
            return [swap_with(in_send[m][k], "h", k, groups) for k in range(1, groups)]

        high_kept, high_send = out_total((2,), (out_2,))
        in_send = [[block(k, m) for k in range(groups)] for m in range(4)]
        in_send, high_send, high_kept, low_send = step(in_send, high_send, high_kept, low_send)

        in_3 = swap_block(3)
        high_back = [quad_swap(piece, m) for m, piece in zip((1, 2, 3), high_send)]
        low_1 = quad_swap(low_send[0], 1)
        into, in_w, normed_all = step(into, in_w, normed_all)
        terms = dot(into, in_w, ((1,), (1,)))
        unit = (normed_all.astype(F32) - own_order(ln_bias, 0)) / own_order(ln_gain, 0)
        gain_sum, shift_sum = jnp.sum(terms * unit, axis=0), jnp.sum(terms, axis=0)
        terms = terms.astype(BF)
        terms, gain_sum, shift_sum, in_3, in_send, high_back, low_1 = step(
            terms, gain_sum, shift_sum, in_3, in_send, high_back, low_1
        )
        low_back = [low_1] + low_back
        terms_sum = team_sum(terms)
        branch_own, branch_next = branch_sum[0], branch_sum[1]

        in_2, in_1 = swap_block(2), swap_block(1)
        in_send[3], in_3 = step(in_send[3], in_3)
        back_3 = quad_swap(add_up(in_send[3][0], in_3).astype(BF), 3)
        got_m = swap_with(branch_next, "l", 1, 2)
        small = [
            own_order(gain_sum, 0),
            own_order(shift_sum, 0),
            jnp.sum(out_grad.astype(F32), axis=0),
        ]
        bias = jnp.sum(into, axis=0, dtype=F32)
        size = in_cols
        team = 4 * (2 * lax.axis_index("y") + lax.axis_index("core"))
        bias = lax.dynamic_update_slice(jnp.zeros((16 * size,), F32), bias, ((team + quad) * size,))
        total = stacked(small + [bias], 0)
        total = total + swap_c(total)
        total = total + swap_with(total, "y", 1, 2)
        in_2, in_1, back_3, got_m, total, in_send = step(
            in_2, in_1, back_3, got_m, total, in_send
        )

        in_0 = swap_block(0)
        in_1, in_2 = step(in_1, in_2)
        back_1 = quad_swap(add_up(in_send[1][0], in_1).astype(BF), 1)
        back_2 = quad_swap(add_up(in_send[2][0], in_2).astype(BF), 2)
        total = total + swap_with(total, "x", 1, 2)
        total = total + swap_with(total, "l", 1, 2)
        out_pieces = [stacked([low_kept, high_kept], 0)] + [
            stacked([low, high], 0).astype(F32) for low, high in zip(low_back, high_back)
        ]
        dense_grad = in_order([p[:local] for p in out_pieces], 0)
        down_grad = in_order([p[local:] for p in out_pieces], 0)
        branch = own_order(branch_own.astype(F32) + got_m.astype(F32), 1)
        hidden_out = (hidden + branch + b_dense + b_fc2).astype(BF)
        own_in = add_up(in_send[0][0], in_0)
        own_in, back_1, back_2, total, dense_grad, down_grad, hidden_out = step(
            own_in, back_1, back_2, total, dense_grad, down_grad, hidden_out
        )

        bit = 1
        while bit < groups:
            total = total + swap_with(total, "h", bit, groups)
            bit *= 2
        got_n = swap_with(terms_sum[1], "l", 1, 2)
        input_grad = norm_grad(group, groups, terms_sum[0], got_n, hidden_in, out_grad, ln_gain)
        qkv_grad, up_grad = settle(order, [own_in, back_1, back_2, back_3], local)
        gain_grad, shift_grad, out_bias_grad = (
            total[:width], total[width : 2 * width], total[2 * width : 3 * width]
        )
        bias = lax.dynamic_slice(total, (3 * width + team * size,), (4 * size,)).reshape(4, size)
        up_bias_grad = bias[:, qkv_cols:].reshape(-1)
        qkv_bias_grad = jnp.stack(
            [bias[:, j * local : (j + 1) * local].reshape(-1) for j in range(3)]
        )
        return (
            hidden_out, input_grad, gain_grad, shift_grad, qkv_grad, qkv_bias_grad,
            dense_grad, out_bias_grad, up_grad, up_bias_grad, down_grad, out_bias_grad,
        )

    return body


def solution(mesh):
    groups = mesh.shape["fsdp"] // 4
    grid = Mesh(mesh.devices.reshape(groups, 2, 2, 2, 2), ("h", "l", "x", "y", "core"))
    rows, cols = ("h", "l", "x"), ("y", "core")
    tokens = rows + cols
    in_specs = (
        P(tokens, None), P(), P(), P(rows, None, cols), P(None, cols), P(cols, rows), P(),
        P(rows, cols), P(cols), P(cols, rows), P(), P(rows, None), P(tokens, None),
    )
    out_specs = (
        P(tokens, None), P(tokens, None), P(), P(), P(rows, None, cols), P(None, cols),
        P(cols, rows), P(), P(rows, cols), P(cols), P(cols, rows), P(),
    )
    return jax.shard_map(
        make_body(groups), mesh=grid, in_specs=in_specs, out_specs=out_specs, check_vma=False
    )
```
